32 devices in a mesh: groups: 2 (over y), rows: 4 (over z), experts: 2 (over x), heads: 2 (over core).
Axes of the slice: x: 2, y: 2, z: 4, core: 2. Of those that a mesh axis runs over, the one named last changes fastest.
Arguments:
- queries: bfloat16 [2, 32, 6144], P(None, ('groups', 'rows', 'experts'), 'heads'), parts along dimension 1, may hold values from -192 to 192
- new_kv: bfloat16 [2, 32, 2, 1024], P(None, ('groups', 'rows', 'experts'), None, 'heads'), parts along dimension 1, may hold values from -24 to 24
- prefix_kv: bfloat16 [8, 128, 2, 1024], P(('groups', 'experts'), 'rows', None, 'heads'), parts along dimension 0, may hold values from -6 to 6
- cont_prompt: int32 [32], P(('groups', 'rows', 'experts')), parts along dimension 0, may hold values from 0 to 3, as said below
- resid: bfloat16 [2, 32, 6144], P(None, ('groups', 'rows', 'experts'), 'heads'), parts along dimension 1, may hold values from -400 to 400
- norm_gain: bfloat16 [6144], replicated, may hold values from 0.099609375 to 1.8984375
- w_gate: bfloat16 [2, 6144, 8192], P('experts', None, ('rows', 'heads')), may hold values from -0.078125 to 0.078125
- w_up: bfloat16 [2, 6144, 8192], P('experts', None, ('rows', 'heads')), may hold values from -0.078125 to 0.078125
- w_down: bfloat16 [2, 8192, 6144], P('experts', 'rows', 'heads'), may hold values from -0.0625 to 0.0625
- routes: int32 [2, 32, 2], P(None, ('groups', 'rows', 'experts')), parts along dimension 1, may hold values from 0 to 1, as said below
- route_gates: float32 [2, 32, 2], P(None, ('groups', 'rows', 'experts')), parts along dimension 1, may hold values from 0.2 to 1
Outputs:
- attn_out: bfloat16 [2, 32, 6144], P(None, ('groups', 'rows', 'experts'), 'heads'), parts along dimension 1
- moe_out: bfloat16 [2, 32, 6144], P(None, ('groups', 'rows', 'experts'), 'heads'), parts along dimension 1
The draws below stay inside these ranges and needn't reach their ends.
There are 2 independent parts, one for each index of `groups`. The reference program is written for one: setup_inputs(seed, part) draws one part's arguments, and reference() takes and returns one part's arrays. A program takes and returns all parts, laid end to end along the dimension named above; an argument that names none is the same for every part. Nothing has to cross between parts.
Inputs may be any that keep to these rules, and one draw needn't show every extreme that they name: `cont_prompt`: continuation c belongs to one of the 2 prompts numbered from o * 2, where o = (c // 2) % 2. `routes`: each token names 2 different experts; no expert is named by more than 32 tokens, and one expert is named by exactly 32.
All inputs are finite; a program needn't handle non-finite values.
Results may differ from the reference program's by a relative error of at most 0.025.
Values may be sent and summed in bfloat16 or wider, within the bound.
No kernel may reach another device: no remote copies, remote signals or barrier semaphores. Data moves between devices by JAX's collectives and lax.ppermute only.
A program may use at most 64 MiB of HBM per device.

```python
import jax
import jax.numpy as jnp
from jax import lax

D = 6144
HEADS = 48
KV_HEADS = 8
HEAD_DIM = 128
FF_WIN = 8192
EXPERTS = 2
TOP = 2
PROMPT_DEV = 2
PROMPTS = 4
CONT_DEV = 2
CONTS = 16
PREFIX = 128
STEPS = 2
SUM_BLOCKS = 4


def prompt_map(key):
    owners = PROMPTS // PROMPT_DEV
    conts = jnp.arange(CONTS)
    owner = conts // CONT_DEV % owners
    row_index = conts // (CONT_DEV * owners)
    picked = jax.random.randint(jax.random.fold_in(key, 23), (CONTS,), 0, PROMPT_DEV)
    picked = jnp.where(row_index == 0, PROMPT_DEV - 1, jnp.where(row_index == 1, 0, picked))
    return (owner * PROMPT_DEV + picked).astype(jnp.int32)


def prefix_base(key):
    shape = (PROMPTS, PREFIX, 2, KV_HEADS * HEAD_DIM)
    cache = jnp.clip(jax.random.normal(jax.random.fold_in(key, 11), shape, jnp.float32), -6.0, 6.0)
    return cache


def query_base(key):
    shape = (STEPS, CONTS, D)
    return jnp.clip(jax.random.normal(jax.random.fold_in(key, 31), shape, jnp.float32), -6.0, 6.0)


def draw_prefix_kv(key, part):
    return prefix_base(key).astype(jnp.bfloat16)


def draw_cont_prompt(key, part):
    return prompt_map(key)


def draw_queries(key, part):
    base = query_base(key)
    return base.astype(jnp.bfloat16)


def draw_new_kv(key, part):
    group_size = HEADS // KV_HEADS
    base = query_base(key).reshape(STEPS, CONTS, KV_HEADS, group_size, HEAD_DIM)
    noise = jnp.clip(jax.random.normal(jax.random.fold_in(key, 51), (STEPS, CONTS, KV_HEADS, HEAD_DIM), jnp.float32), -6.0, 6.0)
    fresh_keys = (0.55 * jnp.sum(base, axis=3) + 0.5 * noise).reshape(STEPS, CONTS, KV_HEADS * HEAD_DIM)
    fresh_values = jnp.clip(jax.random.normal(jax.random.fold_in(key, 53), (STEPS, CONTS, KV_HEADS * HEAD_DIM), jnp.float32), -6.0, 6.0)
    return jnp.stack([fresh_keys, fresh_values], axis=2).astype(jnp.bfloat16)


def draw_resid(key, part):
    shape = (STEPS, CONTS, D)
    return jnp.clip(jax.random.normal(jax.random.fold_in(key, 45), shape, jnp.float32), -6.0, 6.0).astype(jnp.bfloat16)


def draw_routes(key, part):
    total = STEPS * CONTS
    order = jax.random.permutation(jax.random.fold_in(key, 61), total)
    hot = jax.random.randint(jax.random.fold_in(key, 62), (), 0, EXPERTS)
    other = jax.random.randint(jax.random.fold_in(key, 63), (total,), 0, EXPERTS - 1)
    lower = order < total // 2
    first = jnp.where(lower, hot, (hot + 1 + other) % EXPERTS)
    if EXPERTS >= 3:
        extra = jax.random.randint(jax.random.fold_in(key, 64), (total,), 0, EXPERTS - 2)
        third = (hot + 1 + (other + 1 + extra) % (EXPERTS - 1)) % EXPERTS
        upper_second = jnp.where(order < total // 2 + total // 4, hot, third)
    else:
        upper_second = jnp.zeros((total,), jnp.int32) + hot
    second = jnp.where(lower, (hot + 1 + other) % EXPERTS, upper_second)
    return jnp.stack([first, second], axis=-1).astype(jnp.int32).reshape(STEPS, CONTS, TOP)


def level_of(key, dims, shards, smallest, high):
    factor_of = 1.0
    for dim, blocks in shards:
        steps = jax.random.uniform(jax.random.fold_in(jax.random.fold_in(key, 6), dim), (blocks,), jnp.float32, smallest / len(shards), high / len(shards))
        factor_of = factor_of * jnp.repeat(jnp.exp(steps), dims[dim] // blocks).reshape((-1,) + (1,) * (len(dims) - 1 - dim))
    return factor_of


def scatter_about(own_key, shape, scale, bound, shards=(), kind=jnp.bfloat16):
    values = scale * jax.random.normal(own_key, shape, jnp.float32)
    if shards:
        values = values * level_of(own_key, shape, shards, -0.22, 0.18)
    return jnp.clip(values, -bound, bound).astype(kind)


def setup_inputs(seed: int = 0, part: int = 0) -> dict:
    arg_keys = jax.random.split(jax.random.key(seed), 12)
    own_keys = jax.random.split(jax.random.fold_in(arg_keys[11], part), 12)
    queries = draw_queries(jax.random.fold_in(jax.random.fold_in(arg_keys[11], part), 71), part)
    new_kv = draw_new_kv(jax.random.fold_in(jax.random.fold_in(arg_keys[11], part), 71), part)
    prefix_kv = draw_prefix_kv(jax.random.fold_in(jax.random.fold_in(arg_keys[11], part), 71), part)
    cont_prompt = draw_cont_prompt(jax.random.fold_in(jax.random.fold_in(arg_keys[11], part), 71), part)
    resid = draw_resid(jax.random.fold_in(jax.random.fold_in(arg_keys[11], part), 71), part)
    norm_gain = jnp.clip(1.0 + 0.18 * jax.random.normal(arg_keys[5], (D,), jnp.float32), 0.099609375, 1.8984375).astype(jnp.bfloat16)
    w_gate = scatter_about(arg_keys[6], (EXPERTS, D, FF_WIN), D ** -0.5, 0.078125, ((0, 2), (2, 8)))
    w_up = scatter_about(arg_keys[7], (EXPERTS, D, FF_WIN), D ** -0.5, 0.078125, ((0, 2), (2, 8)))
    w_down = scatter_about(arg_keys[8], (EXPERTS, FF_WIN, D), FF_WIN ** -0.5, 0.0625, ((0, 2), (1, 4), (2, 2)))
    routes = draw_routes(jax.random.fold_in(jax.random.fold_in(arg_keys[11], part), 71), part)
    route_gates = jnp.clip(0.2 + 0.8 * jax.random.uniform(own_keys[10], (STEPS, CONTS, TOP), jnp.float32) ** level_of(own_keys[10], (STEPS, CONTS, TOP), ((1, 8),), -0.2, 0.2), 0.2, 1.0)
    return {"queries": queries, "new_kv": new_kv, "prefix_kv": prefix_kv, "cont_prompt": cont_prompt, "resid": resid, "norm_gain": norm_gain, "w_gate": w_gate, "w_up": w_up, "w_down": w_down, "routes": routes, "route_gates": route_gates}


def reference(queries, new_kv, prefix_kv, cont_prompt, resid, norm_gain, w_gate, w_up, w_down, routes, route_gates):
    group_size = HEADS // KV_HEADS
    score_scale = HEAD_DIM ** (-0.5)
    live = jnp.arange(PREFIX + STEPS)[None, :] < (PREFIX + 1 + jnp.arange(STEPS))[:, None]

    def attend(packed):
        query, fresh, prompt = packed
        cache = lax.dynamic_index_in_dim(prefix_kv, prompt.astype(jnp.int32), 0, keepdims=False)
        entries = jnp.concatenate([cache, fresh], axis=0).astype(jnp.float32)
        cache_keys = entries[:, 0].reshape(PREFIX + STEPS, KV_HEADS, HEAD_DIM)
        cache_values = entries[:, 1].reshape(PREFIX + STEPS, KV_HEADS, HEAD_DIM)
        grouped = query.astype(jnp.float32).reshape(STEPS, KV_HEADS, group_size, HEAD_DIM)
        scores = jnp.einsum('sgnd,kgd->sgnk', grouped, cache_keys) * score_scale
        scores = jnp.where(live[:, None, None, :], scores, -jnp.inf)
        highest = lax.optimization_barrier(jnp.max(scores, axis=-1, keepdims=True))
        expo = jnp.exp(scores - highest)
        totals = lax.optimization_barrier(jnp.sum(expo, axis=-1, keepdims=True))
        weights = lax.optimization_barrier(expo.astype(jnp.bfloat16)).astype(jnp.float32)
        weighted = jnp.einsum('sgnk,kgd->sgnd', weights, cache_values) / totals
        return weighted.reshape(STEPS, D).astype(jnp.bfloat16)
    attended = lax.map(attend, (jnp.transpose(queries, (1, 0, 2)), jnp.transpose(new_kv, (1, 0, 2, 3)), cont_prompt))
    attn_out = jnp.transpose(attended, (1, 0, 2))
    combined = resid.astype(jnp.float32) + attn_out.astype(jnp.float32)
    square_mean = lax.optimization_barrier(jnp.mean(combined * combined, axis=-1, keepdims=True))
    normed = (combined * lax.rsqrt(square_mean + 1e-05) * norm_gain.astype(jnp.float32)).astype(jnp.bfloat16)
    token_count = STEPS * CONTS
    flat_tokens = normed.reshape(token_count, D).astype(jnp.float32)
    block_len = FF_WIN // SUM_BLOCKS

    def expert(packed):
        gate_weights, up_weights, down_weights = packed
        gate = jnp.dot(flat_tokens, gate_weights.astype(jnp.float32))
        up_part = jnp.dot(flat_tokens, up_weights.astype(jnp.float32))
        hidden = lax.optimization_barrier((jax.nn.silu(gate) * up_part).astype(jnp.bfloat16)).astype(jnp.float32)
        down_float = down_weights.astype(jnp.float32)

        def add_block(carry, index):
            segment = lax.dynamic_slice_in_dim(hidden, index * block_len, block_len, 1)
            down_rows = lax.dynamic_slice_in_dim(down_float, index * block_len, block_len, 0)
            block_out = lax.optimization_barrier(jnp.dot(segment, down_rows).astype(jnp.bfloat16))
            return (carry + block_out.astype(jnp.float32), None)
        summed, _ = lax.scan(add_block, jnp.zeros((token_count, D), jnp.float32), jnp.arange(SUM_BLOCKS, dtype=jnp.int32))
        return summed.astype(jnp.bfloat16)
    expert_out = lax.map(expert, (w_gate, w_up, w_down))
    matches = routes.reshape(token_count, TOP)[:, :, None] == jnp.arange(EXPERTS, dtype=jnp.int32)[None, None, :]
    mixing = lax.optimization_barrier(jnp.sum(jnp.where(matches, route_gates.reshape(token_count, TOP)[:, :, None], jnp.float32(0.0)), axis=1))
    mixture = jnp.einsum('ne,end->nd', mixing, expert_out.astype(jnp.float32))
    moe_out = mixture.astype(jnp.bfloat16).reshape(STEPS, CONTS, D)
    return (attn_out, moe_out)
```

```python
import functools

import jax
import jax.numpy as jnp
from jax import lax
from jax.experimental import pallas as pl
from jax.experimental.pallas import tpu as pltpu
from jax.sharding import PartitionSpec as P

HEADS = 48
KV_HEADS = 8
HEAD_DIM = 128
GROUP = HEADS // KV_HEADS

VMEM = pltpu.VMEM
MIB = 1 << 20


def fresh_terms(queries, new_kv):
    step_count, own_rows = (queries.shape[0], queries.shape[1])
    kv_local = new_kv.shape[-1] // HEAD_DIM
    group_size = HEADS // KV_HEADS
    grouped = queries.reshape(step_count, own_rows, kv_local, group_size, HEAD_DIM)
    fresh_keys = new_kv[:, :, 0].reshape(step_count, own_rows, kv_local, HEAD_DIM)
    fresh_values = new_kv[:, :, 1].reshape(step_count, own_rows, kv_local, HEAD_DIM)
    fresh_scores = jnp.einsum(
        "scgnd,tcgd->scgnt", grouped, fresh_keys, preferred_element_type=jnp.float32
    ) * HEAD_DIM ** (-0.5)
    future = jnp.arange(step_count)[None, :] > jnp.arange(step_count)[:, None]
    fresh_scores = jnp.where(future[:, None, None, None, :], -jnp.inf, fresh_scores)
    return (grouped, fresh_scores, fresh_values)


def attend_gathered(queries, new_kv, prefix_kv, local_prompt):
    grouped, fresh_scores, fresh_values = fresh_terms(queries, new_kv)
    own_rows = queries.shape[1]
    kv_local = new_kv.shape[-1] // HEAD_DIM
    cache = lax.all_gather(prefix_kv, "rows", axis=1, tiled=True)
    length = cache.shape[1]
    picked = jnp.take(cache, local_prompt, axis=0)
    cache_keys = picked[:, :, 0].reshape(own_rows, length, kv_local, HEAD_DIM)
    cache_values = picked[:, :, 1].reshape(own_rows, length, kv_local, HEAD_DIM)
    prefix_scores = jnp.einsum(
        "scgnd,ckgd->scgnk", grouped, cache_keys, preferred_element_type=jnp.float32
    ) * HEAD_DIM ** (-0.5)
    highest = jnp.maximum(jnp.max(prefix_scores, axis=-1), jnp.max(fresh_scores, axis=-1))
    prefix_expo = jnp.exp(prefix_scores - highest[..., None])
    fresh_expo = jnp.exp(fresh_scores - highest[..., None])
    totals = jnp.sum(prefix_expo, axis=-1) + jnp.sum(fresh_expo, axis=-1)
    weighted = jnp.einsum(
        "scgnk,ckgd->scgnd",
        prefix_expo.astype(jnp.bfloat16),
        cache_values,
        preferred_element_type=jnp.float32,
    )
    weighted = weighted + jnp.einsum(
        "scgnt,tcgd->scgnd",
        fresh_expo.astype(jnp.bfloat16),
        fresh_values,
        preferred_element_type=jnp.float32,
    )
    return (weighted, totals)


def per_device_wide(
    queries,
    new_kv,
    prefix_kv,
    cont_prompt,
    resid,
    norm_gain,
    w_gate,
    w_up,
    w_down,
    routes,
    route_gates,
):
    step_count, own_rows, half_width = queries.shape
    prompt_count = prefix_kv.shape[0]
    local_prompt = cont_prompt - lax.axis_index("experts") * prompt_count
    weighted, totals = attend_gathered(queries, new_kv, prefix_kv, local_prompt)
    attn_out = (
        (weighted / totals[..., None])
        .astype(jnp.bfloat16)
        .reshape(step_count, own_rows, half_width)
    )
    halves = (
        lax.all_gather(resid, "heads", axis=2, tiled=True),
        lax.all_gather(attn_out, "heads", axis=2, tiled=True),
    )
    combined = halves[0].astype(jnp.float32) + halves[1].astype(jnp.float32)
    square_mean = jnp.mean(combined * combined, axis=-1, keepdims=True)
    normed = (combined * lax.rsqrt(square_mean + 1e-05) * norm_gain.astype(jnp.float32)).astype(
        jnp.bfloat16
    )
    token_count = step_count * own_rows
    flat_tokens = normed.reshape(token_count, -1)
    flat_routes = routes.reshape(token_count, -1)
    experts = lax.axis_size("experts")
    matches = flat_routes[:, :, None] == jnp.arange(experts)[None, None, :]
    gate_weights = w_gate[0]
    up_weights = w_up[0]
    wanted = jnp.transpose(jnp.any(matches, axis=1))
    outgoing = jnp.where(wanted[:, :, None], flat_tokens[None], jnp.zeros((), jnp.bfloat16))
    arrived = lax.all_to_all(outgoing, "experts", split_axis=0, concat_axis=0, tiled=True)
    segment = lax.all_gather(arrived.reshape(experts * token_count, -1), "rows", axis=0, tiled=True)
    gate = jnp.dot(segment, gate_weights, preferred_element_type=jnp.float32)
    up_part = jnp.dot(segment, up_weights, preferred_element_type=jnp.float32)
    hidden = (jax.nn.silu(gate) * up_part).astype(jnp.bfloat16)
    paired = lax.all_gather(hidden, "heads", axis=1, tiled=True)
    down_rows = w_down[0]
    segment = paired
    summed = lax.psum_scatter(
        jnp.dot(segment, down_rows, preferred_element_type=jnp.float32).astype(jnp.bfloat16),
        "rows",
        scatter_dimension=0,
        tiled=True,
    )
    result = summed.reshape(experts, token_count, -1)
    returned = lax.all_to_all(result, "experts", split_axis=0, concat_axis=0, tiled=True)
    mixing = jnp.sum(
        jnp.where(matches, route_gates.reshape(token_count, -1)[:, :, None], 0.0), axis=1
    )
    mixture = jnp.einsum("ne,end->nd", mixing, returned.astype(jnp.float32))
    moe_out = mixture.astype(jnp.bfloat16).reshape(step_count, own_rows, half_width)
    return (attn_out, moe_out)


def call(body, outs, in_spaces, name, scratch=(), limit=16 * MIB, cost=None):
    spaces = {"v": VMEM, "s": pltpu.SMEM, "a": pl.ANY}
    single = not isinstance(outs, (list, tuple))
    shapes = [outs] if single else list(outs)
    specs = [pl.BlockSpec(memory_space=VMEM) for _ in shapes]
    return pl.pallas_call(
        body,
        out_shape=shapes[0] if single else tuple(shapes),
        in_specs=[pl.BlockSpec(memory_space=spaces[s]) for s in in_spaces],
        out_specs=specs[0] if single else tuple(specs),
        scratch_shapes=list(scratch),
        compiler_params=pltpu.CompilerParams(vmem_limit_bytes=limit),
        cost_estimate=cost,
        name=name,
    )


class Plan:
    def __init__(self, queries, new_kv, prefix_kv):
        self.steps, self.conts, self.half = queries.shape
        self.kv_local = new_kv.shape[-1] // HEAD_DIM
        self.prompts, self.positions = prefix_kv.shape[:2]
        self.tokens = self.steps * self.conts
        self.block = self.prompts * self.positions * 2
        self.fresh = self.block
        self.query = self.fresh + 2 * self.tokens
        self.resid = self.query + GROUP * self.tokens
        self.prompt = self.resid + GROUP * self.tokens
        self.rows = -(-(self.prompt + self.tokens) // 16) * 16


def pack_body(plan, prompt_ref, q_ref, new_ref, prefix_ref, resid_ref, out_ref):
    t, c = plan.tokens, plan.conts
    base = lax.axis_index("experts") * plan.prompts
    row = lax.broadcasted_iota(jnp.int32, (c, HEAD_DIM), 0)
    local = jnp.zeros((c, HEAD_DIM), jnp.float32)
    for i in range(c):
        local = jnp.where(row == i, (prompt_ref[i] - base).astype(jnp.float32), local)
    local = local.astype(jnp.bfloat16)
    for h in range(plan.kv_local):
        lanes = pl.ds(h * HEAD_DIM, HEAD_DIM)
        for p in range(plan.prompts):
            for k in range(plan.positions):
                out_ref[h, pl.ds((p * plan.positions + k) * 2, 2), :] = prefix_ref[p, k, :, lanes]
        for s in range(plan.steps):
            for i in range(c):
                out_ref[h, pl.ds(plan.fresh + (s * c + i) * 2, 2), :] = new_ref[s, i, :, lanes]
            for g in range(GROUP):
                head = pl.ds((h * GROUP + g) * HEAD_DIM, HEAD_DIM)
                out_ref[h, pl.ds(plan.query + g * t + s * c, c), :] = q_ref[s, :, head]
                out_ref[h, pl.ds(plan.resid + g * t + s * c, c), :] = resid_ref[s, :, head]
            out_ref[h, pl.ds(plan.prompt + s * c, c), :] = local


def attend_body(plan, rows, got_ref, gain_ref, x_ref, attn_ref, q_s, r_s, kv_s, p_s):
    t, c = plan.tokens, plan.conts
    total = rows * t
    f32 = jnp.float32
    for src in range(rows):
        kv_s[pl.ds(src * plan.block, plan.block), :] = got_ref[src, pl.ds(0, plan.block), :]
        kv_s[pl.ds(rows * plan.block + src * 2 * t, 2 * t), :] = got_ref[src, pl.ds(plan.fresh, 2 * t), :]
        p_s[pl.ds(src * t, t), :] = got_ref[src, pl.ds(plan.prompt, t), :]
        for g in range(GROUP):
            q_s[pl.ds(g * total + src * t, t), :] = got_ref[src, pl.ds(plan.query + g * t, t), :]
            r_s[pl.ds(g * total + src * t, t), :] = got_ref[src, pl.ds(plan.resid + g * t, t), :]
    used = rows * plan.block + rows * 2 * t
    spare = kv_s.shape[0] - used
    if spare:
        kv_s[pl.ds(used, spare), :] = jnp.zeros((spare, HEAD_DIM), jnp.bfloat16)
    kv = kv_s[...]
    scores = lax.dot_general(
        q_s[...], kv, (((1,), (1,)), ((), ())), preferred_element_type=f32
    ) * HEAD_DIM ** (-0.5)
    shape = scores.shape
    row = lax.broadcasted_iota(jnp.int32, shape, 0) % total
    col = lax.broadcasted_iota(jnp.int32, shape, 1)
    prompt = p_s[...].astype(f32)[:, :1]
    prompt = jnp.concatenate([prompt] * GROUP, axis=0).astype(jnp.int32)
    in_prefix = (col < rows * plan.block) & ((col % plan.block) // (2 * plan.positions) == prompt)
    late = col - rows * plan.block
    same = (late // (2 * t) == row // t) & (((late // 2) % t) % c == row % c)
    seen = ((late // 2) % t) // c <= (row % t) // c
    in_fresh = (late >= 0) & (col < used) & same & seen
    live = (col % 2 == 0) & (in_prefix | in_fresh)
    scores = jnp.where(live, scores, -jnp.inf)
    highest = jnp.max(scores, axis=-1, keepdims=True)
    expo = jnp.exp(scores - highest)
    totals = jnp.sum(expo, axis=-1, keepdims=True)
    weights = pltpu.roll(expo, 1, 1).astype(jnp.bfloat16)
    out = jnp.dot(weights, kv, preferred_element_type=f32) / totals
    attn = out.astype(jnp.bfloat16)
    combined = attn.astype(f32) + r_s[...].astype(f32)
    square = jnp.zeros((total, HEAD_DIM), f32)
    pieces = x_ref.shape[0]
    for g in range(GROUP):
        part = combined[g * total : (g + 1) * total]
        square = square + part * part
        lanes = pl.ds(g * HEAD_DIM, HEAD_DIM)
        gained = (part * gain_ref[:, lanes].astype(f32)).astype(jnp.bfloat16)
        for piece in range(pieces):
            x_ref[piece, :, lanes] = gained
        attn_ref[:, lanes] = attn[g * total : (g + 1) * total]
    square = jnp.sum(square, axis=-1, keepdims=True)
    high = square.astype(jnp.bfloat16)
    low = (square - high.astype(f32)).astype(jnp.bfloat16)
    lane = lax.broadcasted_iota(jnp.int32, (total, HEAD_DIM), 1)
    extra = jnp.where(lane == 0, high.astype(f32), jnp.where(lane == 1, low.astype(f32), 0.0))
    extra = extra.astype(jnp.bfloat16)
    for piece in range(pieces):
        x_ref[piece, :, pl.ds(GROUP * HEAD_DIM, HEAD_DIM)] = extra


def gate_up_half(offset, x_ref, gate_hbm, up_hbm, gate_buf, up_buf, sems, init):
    chunks, _, width = x_ref.shape
    depth = width - HEAD_DIM
    copies = []
    for k in range(chunks):
        rows = pl.ds(offset + k * depth, depth)
        pair = (
            pltpu.make_async_copy(gate_hbm.at[0, rows], gate_buf.at[k], sems.at[0, k]),
            pltpu.make_async_copy(up_hbm.at[0, rows], up_buf.at[k], sems.at[1, k]),
        )
        for copy in pair:
            copy.start()
        copies.append(pair)
    gate, up = init
    for k in range(chunks):
        x = x_ref[k, :, pl.ds(0, depth)]
        copies[k][0].wait()
        part = jnp.dot(x, gate_buf[k], preferred_element_type=jnp.float32)
        gate = part if gate is None else gate + part
        copies[k][1].wait()
        part = jnp.dot(x, up_buf[k], preferred_element_type=jnp.float32)
        up = part if up is None else up + part
    return gate, up


def first_half_body(x_ref, gate_hbm, up_hbm, gate_ref, up_ref, gate_buf, up_buf, sems):
    chunks, _, width = x_ref.shape
    offset = lax.axis_index("heads") * (chunks * (width - HEAD_DIM))
    gate, up = gate_up_half(offset, x_ref, gate_hbm, up_hbm, gate_buf, up_buf, sems, (None, None))
    gate_ref[...] = gate
    up_ref[...] = up


def second_half_body(
    x_ref, own_ref, gate_in, up_in, gate_hbm, up_hbm, hidden_ref, gate_buf, up_buf, sems
):
    chunks, _, width = x_ref.shape
    depth = width - HEAD_DIM
    half = chunks * depth
    offset = (1 - lax.axis_index("heads")) * half
    square = jnp.zeros((x_ref.shape[1], 1), jnp.float32)
    for ref in (own_ref, x_ref):
        for k in range(chunks):
            extra = ref[k, :, pl.ds(depth, HEAD_DIM)].astype(jnp.float32)
            square = square + jnp.sum(extra, axis=-1, keepdims=True)
    scale = lax.rsqrt(square / (2 * half) + 1e-05)
    gate, up = gate_up_half(
        offset, x_ref, gate_hbm, up_hbm, gate_buf, up_buf, sems, (gate_in[...], up_in[...])
    )
    gate = gate * scale
    up = up * scale
    hidden_ref[...] = (gate / (1.0 + jnp.exp(-gate)) * up).astype(jnp.bfloat16)


def down_first_body(hidden_ref, down_hbm, out_ref, buf, sems):
    depth = hidden_ref.shape[1]
    out_ref[...] = down_half(lax.axis_index("heads") * depth, hidden_ref, down_hbm, buf, sems)


def down_half(offset, hidden_ref, down_hbm, buf, sems):
    parts, depth, _ = buf.shape
    copies = []
    for k in range(parts):
        rows = pl.ds(offset + k * depth, depth)
        copy = pltpu.make_async_copy(down_hbm.at[0, rows], buf.at[k], sems.at[k])
        copy.start()
        copies.append(copy)
    total = None
    for k in range(parts):
        copies[k].wait()
        part = jnp.dot(
            hidden_ref[:, pl.ds(k * depth, depth)], buf[k], preferred_element_type=jnp.float32
        )
        total = part if total is None else total + part
    return total


def down_second_body(rows, hidden_ref, own_ref, attn_ref, down_hbm, out_ref, buf, sems):
    depth = hidden_ref.shape[1]
    other = (1 - lax.axis_index("heads")) * depth
    total = own_ref[...] + down_half(other, hidden_ref, down_hbm, buf, sems)
    result = total.astype(jnp.bfloat16)
    pieces, t, width = out_ref.shape
    experts = pieces // rows
    half = result.shape[1]
    for r in range(rows):
        attn = attn_ref[pl.ds(r * t, t), :]
        for e in range(experts):
            first = (e * rows + r) * t
            out_ref[r * experts + e, :, pl.ds(0, half)] = result[first : first + t]
            out_ref[r * experts + e, :, pl.ds(half, width - half)] = attn


def mix_body(rows, routes_ref, gates_ref, got_ref, attn_ref, moe_ref):
    pieces, t, width = got_ref.shape
    experts = pieces // rows
    steps, conts, half = moe_ref.shape
    own = lax.axis_index("experts")
    row = lax.broadcasted_iota(jnp.int32, (t, 1), 0)
    mixture = jnp.zeros((t, half), jnp.float32)
    for e in range(experts):
        summed = jnp.zeros((t, half), jnp.float32)
        for r in range(rows):
            summed = summed + got_ref[r * experts + e, :, pl.ds(0, half)].astype(jnp.float32)
        share = jnp.zeros((t, 1), jnp.float32)
        for s in range(steps):
            for c in range(conts):
                amount = jnp.float32(0.0)
                for k in range(routes_ref.shape[2]):
                    amount = amount + jnp.where(routes_ref[s, c, k] == e, gates_ref[s, c, k], 0.0)
                share = jnp.where(row == s * conts + c, amount, share)
        mixture = mixture + share * summed.astype(jnp.bfloat16).astype(jnp.float32)
    mixture = mixture.astype(jnp.bfloat16)
    piece = width - half
    for s in range(steps):
        moe_ref[s] = mixture[s * conts : (s + 1) * conts]
        for r in range(rows):
            attn_ref[s, :, pl.ds(r * piece, piece)] = got_ref[
                r * experts + own, pl.ds(s * conts, conts), pl.ds(half, piece)
            ]


def per_device(
    queries,
    new_kv,
    prefix_kv,
    cont_prompt,
    resid,
    norm_gain,
    w_gate,
    w_up,
    w_down,
    routes,
    route_gates,
):
    rows, experts = lax.axis_size("rows"), lax.axis_size("experts")
    plan = Plan(queries, new_kv, prefix_kv)
    bf16, f32 = jnp.bfloat16, jnp.float32
    shape = jax.ShapeDtypeStruct
    piece = GROUP * HEAD_DIM
    total = rows * plan.tokens
    tokens = experts * total

    packed = call(
        functools.partial(pack_body, plan),
        shape((rows, plan.rows, HEAD_DIM), bf16),
        "svvvv",
        "pack",
    )(cont_prompt, queries, new_kv, prefix_kv, resid)
    got = lax.all_to_all(packed, "rows", split_axis=0, concat_axis=0, tiled=True)

    start = lax.axis_index("heads") * plan.half + lax.axis_index("rows") * piece
    gain = lax.dynamic_slice_in_dim(norm_gain, start, piece).reshape(1, piece)
    keys = -(-(rows * (plan.block + 2 * plan.tokens)) // 128) * 128
    x, attn = call(
        functools.partial(attend_body, plan, rows),
        (shape((rows * experts, total, piece + HEAD_DIM), bf16), shape((total, piece), bf16)),
        "vv",
        "attend",
        scratch=(
            VMEM((GROUP * total, HEAD_DIM), bf16),
            VMEM((GROUP * total, HEAD_DIM), bf16),
            VMEM((keys, HEAD_DIM), bf16),
            VMEM((total, HEAD_DIM), bf16),
        ),
    )(got, gain)
    x = lax.all_to_all(x, ("rows", "experts"), split_axis=0, concat_axis=0, tiled=True)
    own = x.reshape(rows, tokens, piece + HEAD_DIM)
    swap = [(0, 1), (1, 0)]
    other = lax.ppermute(own, "heads", swap)

    hbm = functools.partial(pltpu.with_memory_space_constraint, memory_space=pltpu.HBM)
    w_gate, w_up, w_down = hbm(w_gate), hbm(w_up), hbm(w_down)
    units = w_gate.shape[2]
    buffers = (
        VMEM((rows, piece, units), bf16),
        VMEM((rows, piece, units), bf16),
        pltpu.SemaphoreType.DMA((2, rows)),
    )
    cost = pl.CostEstimate(
        flops=4 * tokens * plan.half * units,
        bytes_accessed=4 * plan.half * units,
        transcendentals=0,
    )
    gate, up = call(
        first_half_body,
        (shape((tokens, units), f32), shape((tokens, units), f32)),
        "vaa",
        "first_half",
        scratch=buffers,
        limit=32 * MIB,
        cost=cost,
    )(own, w_gate, w_up)
    hidden = call(
        second_half_body,
        shape((tokens, units), bf16),
        "vvvvaa",
        "second_half",
        scratch=buffers,
        limit=32 * MIB,
        cost=cost,
    )(other, own, gate, up, w_gate, w_up)
    other_hidden = lax.ppermute(hidden, "heads", swap)
    parts = 4
    buffers = (
        VMEM((parts, units // parts, plan.half), bf16),
        pltpu.SemaphoreType.DMA((parts,)),
    )
    cost = pl.CostEstimate(
        flops=2 * tokens * plan.half * units,
        bytes_accessed=2 * plan.half * units,
        transcendentals=0,
    )
    partial = call(
        down_first_body,
        shape((tokens, plan.half), f32),
        "va",
        "down_first",
        scratch=buffers,
        limit=32 * MIB,
        cost=cost,
    )(hidden, w_down)
    blocks = call(
        functools.partial(down_second_body, rows),
        shape((rows * experts, plan.tokens, plan.half + piece), bf16),
        "vvva",
        "down_second",
        scratch=buffers,
        limit=32 * MIB,
        cost=cost,
    )(other_hidden, partial, attn, w_down)
    blocks = lax.all_to_all(blocks, ("rows", "experts"), split_axis=0, concat_axis=0, tiled=True)
    out = shape(queries.shape, bf16)
    attn_out, moe_out = call(functools.partial(mix_body, rows), (out, out), "ssv", "mix")(
        routes, route_gates, blocks
    )
    return (attn_out, moe_out)


def solution(mesh):
    placed = (
        P(None, ("groups", "rows", "experts"), "heads"),
        P(None, ("groups", "rows", "experts"), None, "heads"),
        P(("groups", "experts"), "rows", None, "heads"),
        P(("groups", "rows", "experts")),
        P(None, ("groups", "rows", "experts"), "heads"),
        P(),
        P("experts", None, ("rows", "heads")),
        P("experts", None, ("rows", "heads")),
        P("experts", "rows", "heads"),
        P(None, ("groups", "rows", "experts"), None),
        P(None, ("groups", "rows", "experts"), None),
    )
    sizes = mesh.shape
    by_head = sizes["heads"] == 2 and sizes["rows"] * sizes["heads"] == KV_HEADS
    return jax.shard_map(
        per_device if by_head else per_device_wide,
        mesh=mesh,
        in_specs=placed,
        out_specs=(
            P(None, ("groups", "rows", "experts"), "heads"),
            P(None, ("groups", "rows", "experts"), "heads"),
        ),
        check_vma=False,
    )
```

```python
import functools

import jax
import jax.numpy as jnp
from jax import lax
from jax.experimental import pallas as pl
from jax.experimental.pallas import tpu as pltpu
from jax.sharding import PartitionSpec as P

HEADS = 48
KV_HEADS = 8
HEAD_DIM = 128
GROUP = HEADS // KV_HEADS

VMEM = pltpu.VMEM
MIB = 1 << 20


def fresh_terms(queries, new_kv):
    step_count, own_rows = (queries.shape[0], queries.shape[1])
    kv_local = new_kv.shape[-1] // HEAD_DIM
    group_size = HEADS // KV_HEADS
    grouped = queries.reshape(step_count, own_rows, kv_local, group_size, HEAD_DIM)
    fresh_keys = new_kv[:, :, 0].reshape(step_count, own_rows, kv_local, HEAD_DIM)
    fresh_values = new_kv[:, :, 1].reshape(step_count, own_rows, kv_local, HEAD_DIM)
    fresh_scores = jnp.einsum(
        "scgnd,tcgd->scgnt", grouped, fresh_keys, preferred_element_type=jnp.float32
    ) * HEAD_DIM ** (-0.5)
    future = jnp.arange(step_count)[None, :] > jnp.arange(step_count)[:, None]
    fresh_scores = jnp.where(future[:, None, None, None, :], -jnp.inf, fresh_scores)
    return (grouped, fresh_scores, fresh_values)


def attend_gathered(queries, new_kv, prefix_kv, local_prompt):
    grouped, fresh_scores, fresh_values = fresh_terms(queries, new_kv)
    own_rows = queries.shape[1]
    kv_local = new_kv.shape[-1] // HEAD_DIM
    cache = lax.all_gather(prefix_kv, "rows", axis=1, tiled=True)
    length = cache.shape[1]
    picked = jnp.take(cache, local_prompt, axis=0)
    cache_keys = picked[:, :, 0].reshape(own_rows, length, kv_local, HEAD_DIM)
    cache_values = picked[:, :, 1].reshape(own_rows, length, kv_local, HEAD_DIM)
    prefix_scores = jnp.einsum(
        "scgnd,ckgd->scgnk", grouped, cache_keys, preferred_element_type=jnp.float32
    ) * HEAD_DIM ** (-0.5)
    highest = jnp.maximum(jnp.max(prefix_scores, axis=-1), jnp.max(fresh_scores, axis=-1))
    prefix_expo = jnp.exp(prefix_scores - highest[..., None])
    fresh_expo = jnp.exp(fresh_scores - highest[..., None])
    totals = jnp.sum(prefix_expo, axis=-1) + jnp.sum(fresh_expo, axis=-1)
    weighted = jnp.einsum(
        "scgnk,ckgd->scgnd",
        prefix_expo.astype(jnp.bfloat16),
        cache_values,
        preferred_element_type=jnp.float32,
    )
    weighted = weighted + jnp.einsum(
        "scgnt,tcgd->scgnd",
        fresh_expo.astype(jnp.bfloat16),
        fresh_values,
        preferred_element_type=jnp.float32,
    )
    return (weighted, totals)


def per_device_wide(
    queries,
    new_kv,
    prefix_kv,
    cont_prompt,
    resid,
    norm_gain,
    w_gate,
    w_up,
    w_down,
    routes,
    route_gates,
):
    step_count, own_rows, half_width = queries.shape
    prompt_count = prefix_kv.shape[0]
    local_prompt = cont_prompt - lax.axis_index("experts") * prompt_count
    weighted, totals = attend_gathered(queries, new_kv, prefix_kv, local_prompt)
    attn_out = (
        (weighted / totals[..., None])
        .astype(jnp.bfloat16)
        .reshape(step_count, own_rows, half_width)
    )
    halves = (
        lax.all_gather(resid, "heads", axis=2, tiled=True),
        lax.all_gather(attn_out, "heads", axis=2, tiled=True),
    )
    combined = halves[0].astype(jnp.float32) + halves[1].astype(jnp.float32)
    square_mean = jnp.mean(combined * combined, axis=-1, keepdims=True)
    normed = (combined * lax.rsqrt(square_mean + 1e-05) * norm_gain.astype(jnp.float32)).astype(
        jnp.bfloat16
    )
    token_count = step_count * own_rows
    flat_tokens = normed.reshape(token_count, -1)
    flat_routes = routes.reshape(token_count, -1)
    experts = lax.axis_size("experts")
    matches = flat_routes[:, :, None] == jnp.arange(experts)[None, None, :]
    gate_weights = w_gate[0]
    up_weights = w_up[0]
    wanted = jnp.transpose(jnp.any(matches, axis=1))
    outgoing = jnp.where(wanted[:, :, None], flat_tokens[None], jnp.zeros((), jnp.bfloat16))
    arrived = lax.all_to_all(outgoing, "experts", split_axis=0, concat_axis=0, tiled=True)
    segment = lax.all_gather(arrived.reshape(experts * token_count, -1), "rows", axis=0, tiled=True)
    gate = jnp.dot(segment, gate_weights, preferred_element_type=jnp.float32)
    up_part = jnp.dot(segment, up_weights, preferred_element_type=jnp.float32)
    hidden = (jax.nn.silu(gate) * up_part).astype(jnp.bfloat16)
    paired = lax.all_gather(hidden, "heads", axis=1, tiled=True)
    down_rows = w_down[0]
    segment = paired
    summed = lax.psum_scatter(
        jnp.dot(segment, down_rows, preferred_element_type=jnp.float32).astype(jnp.bfloat16),
        "rows",
        scatter_dimension=0,
        tiled=True,
    )
    result = summed.reshape(experts, token_count, -1)
    returned = lax.all_to_all(result, "experts", split_axis=0, concat_axis=0, tiled=True)
    mixing = jnp.sum(
        jnp.where(matches, route_gates.reshape(token_count, -1)[:, :, None], 0.0), axis=1
    )
    mixture = jnp.einsum("ne,end->nd", mixing, returned.astype(jnp.float32))
    moe_out = mixture.astype(jnp.bfloat16).reshape(step_count, own_rows, half_width)
    return (attn_out, moe_out)


def call(body, outs, in_spaces, name, scratch=(), limit=4 * MIB, cost=None):
    spaces = {"v": VMEM, "s": pltpu.SMEM, "a": pl.ANY}
    single = not isinstance(outs, (list, tuple))
    shapes = [outs] if single else list(outs)
    specs = [pl.BlockSpec(memory_space=VMEM) for _ in shapes]
    return pl.pallas_call(
        body,
        out_shape=shapes[0] if single else tuple(shapes),
        in_specs=[pl.BlockSpec(memory_space=spaces[s]) for s in in_spaces],
        out_specs=specs[0] if single else tuple(specs),
        scratch_shapes=list(scratch),
        compiler_params=pltpu.CompilerParams(vmem_limit_bytes=limit),
        cost_estimate=cost,
        name=name,
    )


class Plan:
    def __init__(self, queries, new_kv, prefix_kv):
        self.steps, self.conts, self.half = queries.shape
        self.kv_local = new_kv.shape[-1] // HEAD_DIM
        self.prompts, self.positions = prefix_kv.shape[:2]
        self.tokens = self.steps * self.conts
        self.block = self.prompts * self.positions * 2
        self.fresh = self.block
        self.query = self.fresh + 2 * self.tokens
        self.resid = self.query + GROUP * self.tokens
        self.prompt = self.resid + GROUP * self.tokens
        self.rows = -(-(self.prompt + self.tokens) // 16) * 16


def pack_body(plan, prompt_hbm, q_hbm, new_hbm, prefix_hbm, resid_hbm, *rest):
    outs, buffers, sems = rest[: plan.kv_local], rest[plan.kv_local : -1], rest[-1]
    sources = (prompt_hbm, q_hbm, new_hbm, prefix_hbm, resid_hbm)
    copies = []
    for i, (source, buffer) in enumerate(zip(sources, buffers)):
        copy = pltpu.make_async_copy(source, buffer, sems.at[i])
        copy.start()
        copies.append(copy)
    for copy in copies:
        copy.wait()
    prompt_ref, q_ref, new_ref, prefix_ref, resid_ref = buffers
    t, c = plan.tokens, plan.conts
    base = lax.axis_index("experts") * plan.prompts
    row = lax.broadcasted_iota(jnp.int32, (c, HEAD_DIM), 0)
    local = jnp.zeros((c, HEAD_DIM), jnp.float32)
    for i in range(c):
        local = jnp.where(row == i, (prompt_ref[i] - base).astype(jnp.float32), local)
    local = local.astype(jnp.bfloat16)
    own = lax.axis_index("rows")
    for k, out_ref in enumerate(outs):
        h = own ^ k
        lanes = pl.ds(pl.multiple_of(h * HEAD_DIM, HEAD_DIM), HEAD_DIM)
        for p in range(plan.prompts):
            for i in range(plan.positions):
                out_ref[pl.ds((p * plan.positions + i) * 2, 2), :] = prefix_ref[p, i, :, lanes]
        for s in range(plan.steps):
            for i in range(c):
                out_ref[pl.ds(plan.fresh + (s * c + i) * 2, 2), :] = new_ref[s, i, :, lanes]
            for g in range(GROUP):
                head = pl.ds(pl.multiple_of((h * GROUP + g) * HEAD_DIM, HEAD_DIM), HEAD_DIM)
                out_ref[pl.ds(plan.query + g * t + s * c, c), :] = q_ref[s, :, head]
                out_ref[pl.ds(plan.resid + g * t + s * c, c), :] = resid_ref[s, :, head]
            out_ref[pl.ds(plan.prompt + s * c, c), :] = local


def attend_body(plan, rows, *refs):
    pieces, (gain_ref, _, x_ref, attn_ref, q_s, r_s, kv_s, p_s) = refs[:rows], refs[rows:]
    t, c = plan.tokens, plan.conts
    total = rows * t
    f32 = jnp.float32

    def place(own):
        for k, got_ref in enumerate(pieces):
            src = own ^ k
            kv_s[pl.ds(src * plan.block, plan.block), :] = got_ref[pl.ds(0, plan.block), :]
            late = pl.ds(rows * plan.block + src * 2 * t, 2 * t)
            kv_s[late, :] = got_ref[pl.ds(plan.fresh, 2 * t), :]
            p_s[pl.ds(src * t, t), :] = got_ref[pl.ds(plan.prompt, t), :]
            for g in range(GROUP):
                q_s[pl.ds(g * total + src * t, t), :] = got_ref[pl.ds(plan.query + g * t, t), :]
                r_s[pl.ds(g * total + src * t, t), :] = got_ref[pl.ds(plan.resid + g * t, t), :]

    for own in range(rows):
        pl.when(lax.axis_index("rows") == own)(functools.partial(place, own))
    used = rows * plan.block + rows * 2 * t
    spare = kv_s.shape[0] - used
    if spare:
        kv_s[pl.ds(used, spare), :] = jnp.zeros((spare, HEAD_DIM), jnp.bfloat16)
    kv = kv_s[...]
    scores = lax.dot_general(
        q_s[...], kv, (((1,), (1,)), ((), ())), preferred_element_type=f32
    ) * HEAD_DIM ** (-0.5)
    shape = scores.shape
    row = lax.broadcasted_iota(jnp.int32, shape, 0) % total
    col = lax.broadcasted_iota(jnp.int32, shape, 1)
    prompt = p_s[...].astype(f32)[:, :1]
    prompt = jnp.concatenate([prompt] * GROUP, axis=0).astype(jnp.int32)
    in_prefix = (col < rows * plan.block) & ((col % plan.block) // (2 * plan.positions) == prompt)
    late = col - rows * plan.block
    same = (late // (2 * t) == row // t) & (((late // 2) % t) % c == row % c)
    seen = ((late // 2) % t) // c <= (row % t) // c
    in_fresh = (late >= 0) & (col < used) & same & seen
    live = (col % 2 == 0) & (in_prefix | in_fresh)
    scores = jnp.where(live, scores, -jnp.inf)
    highest = jnp.max(scores, axis=-1, keepdims=True)
    expo = jnp.exp(scores - highest)
    totals = jnp.sum(expo, axis=-1, keepdims=True)
    weights = pltpu.roll(expo, 1, 1).astype(jnp.bfloat16)
    out = jnp.dot(weights, kv, preferred_element_type=f32) / totals
    attn = out.astype(jnp.bfloat16)
    combined = attn.astype(f32) + r_s[...].astype(f32)
    square = jnp.zeros((total, HEAD_DIM), f32)
    pieces = x_ref.shape[0]
    for g in range(GROUP):
        part = combined[g * total : (g + 1) * total]
        square = square + part * part
        lanes = pl.ds(g * HEAD_DIM, HEAD_DIM)
        gained = (part * gain_ref[:, lanes].astype(f32)).astype(jnp.bfloat16)
        for piece in range(pieces):
            x_ref[piece, :, lanes] = gained
        attn_ref[:, lanes] = attn[g * total : (g + 1) * total]
    square = jnp.sum(square, axis=-1, keepdims=True)
    high = square.astype(jnp.bfloat16)
    low = (square - high.astype(f32)).astype(jnp.bfloat16)
    lane = lax.broadcasted_iota(jnp.int32, (total, HEAD_DIM), 1)
    extra = jnp.where(lane == 0, high.astype(f32), jnp.where(lane == 1, low.astype(f32), 0.0))
    extra = extra.astype(jnp.bfloat16)
    for piece in range(pieces):
        x_ref[piece, :, pl.ds(GROUP * HEAD_DIM, HEAD_DIM)] = extra


def stream(source, target, sems):
    core = lax.axis_index("heads")
    half = source.shape[1] // 2
    parts = sems.shape[1]
    step = half // parts
    copies = []
    for side in range(2):
        first = (core if side == 0 else 1 - core) * half
        copies.append(
            [
                pltpu.make_async_copy(
                    source.at[0, pl.ds(first + k * step, step)],
                    target.at[side, pl.ds(k * step, step)],
                    sems.at[side, k],
                )
                for k in range(parts)
            ]
        )
    for copy in copies[0] + copies[1]:
        copy.start()
    return copies


def load_body(_, source, target, sems):
    copies = stream(source, target, sems)
    for copy in copies[0] + copies[1]:
        copy.wait()


def half_products(side, x_ref, weight, total, ready=None):
    chunks, _, width = x_ref.shape
    depth = width - HEAD_DIM
    for k in range(chunks):
        if ready is not None:
            ready[k].wait()
        part = jnp.dot(
            x_ref[k, :, pl.ds(0, depth)],
            weight[side, pl.ds(k * depth, depth)],
            preferred_element_type=jnp.float32,
        )
        total = part if total is None else total + part
    return total


def first_half_body(x_ref, gate_w, up_hbm, gate_ref, up_ref, up_w, sems):
    copies = stream(up_hbm, up_w, sems)
    gate_ref[...] = half_products(0, x_ref, gate_w, None)
    up_ref[...] = half_products(0, x_ref, up_w, None, copies[0])
    for copy in copies[1]:
        copy.wait()


def second_half_body(
    x_ref, own_ref, gate_in, up_in, gate_w, up_w, down_hbm, hidden_ref, down_w, sems
):
    copies = stream(down_hbm, down_w, sems)
    chunks, _, width = x_ref.shape
    depth = width - HEAD_DIM
    square = jnp.zeros((x_ref.shape[1], 1), jnp.float32)
    for ref in (own_ref, x_ref):
        for k in range(chunks):
            extra = ref[k, :, pl.ds(depth, HEAD_DIM)].astype(jnp.float32)
            square = square + jnp.sum(extra, axis=-1, keepdims=True)
    scale = lax.rsqrt(square / (2 * chunks * depth) + 1e-05)
    gate = half_products(1, x_ref, gate_w, gate_in[...]) * scale
    up = half_products(1, x_ref, up_w, up_in[...]) * scale
    hidden_ref[...] = (gate / (1.0 + jnp.exp(-gate)) * up).astype(jnp.bfloat16)
    for copy in copies[0] + copies[1]:
        copy.wait()


def down_first_body(hidden_ref, down_w, out_ref):
    out_ref[...] = jnp.dot(hidden_ref[...], down_w[0], preferred_element_type=jnp.float32)


def down_second_body(rows, hidden_ref, own_ref, attn_ref, down_w, out_ref):
    total = own_ref[...] + jnp.dot(
        hidden_ref[...], down_w[1], preferred_element_type=jnp.float32
    )
    result = total.astype(jnp.bfloat16)
    pieces, t, width = out_ref.shape
    experts = pieces // rows
    half = result.shape[1]
    for r in range(rows):
        attn = attn_ref[pl.ds(r * t, t), :]
        for e in range(experts):
            first = (e * rows + r) * t
            out_ref[r * experts + e, :, pl.ds(0, half)] = result[first : first + t]
            out_ref[r * experts + e, :, pl.ds(half, width - half)] = attn


def mix_body(rows, routes_ref, gates_ref, got_ref, attn_ref, moe_ref):
    pieces, t, width = got_ref.shape
    experts = pieces // rows
    steps, conts, half = moe_ref.shape
    own = lax.axis_index("experts")
    row = lax.broadcasted_iota(jnp.int32, (t, 1), 0)
    mixture = jnp.zeros((t, half), jnp.float32)
    for e in range(experts):
        summed = jnp.zeros((t, half), jnp.float32)
        for r in range(rows):
            summed = summed + got_ref[r * experts + e, :, pl.ds(0, half)].astype(jnp.float32)
        share = jnp.zeros((t, 1), jnp.float32)
        for s in range(steps):
            for c in range(conts):
                amount = jnp.float32(0.0)
                for k in range(routes_ref.shape[2]):
                    amount = amount + jnp.where(routes_ref[s, c, k] == e, gates_ref[s, c, k], 0.0)
                share = jnp.where(row == s * conts + c, amount, share)
        mixture = mixture + share * summed.astype(jnp.bfloat16).astype(jnp.float32)
    mixture = mixture.astype(jnp.bfloat16)
    piece = width - half
    for s in range(steps):
        moe_ref[s] = mixture[s * conts : (s + 1) * conts]
        for r in range(rows):
            attn_ref[s, :, pl.ds(r * piece, piece)] = got_ref[
                r * experts + own, pl.ds(s * conts, conts), pl.ds(half, piece)
            ]


def per_device(
    queries,
    new_kv,
    prefix_kv,
    cont_prompt,
    resid,
    norm_gain,
    w_gate,
    w_up,
    w_down,
    routes,
    route_gates,
):
    rows, experts = lax.axis_size("rows"), lax.axis_size("experts")
    plan = Plan(queries, new_kv, prefix_kv)
    bf16, f32 = jnp.bfloat16, jnp.float32
    shape = jax.ShapeDtypeStruct
    piece = GROUP * HEAD_DIM
    total = rows * plan.tokens
    tokens = experts * total

    hbm = functools.partial(pltpu.with_memory_space_constraint, memory_space=pltpu.HBM)
    vmem = functools.partial(pltpu.with_memory_space_constraint, memory_space=VMEM)
    sources = (cont_prompt, queries, new_kv, prefix_kv, resid)
    packed = call(
        functools.partial(pack_body, plan),
        (shape((plan.rows, HEAD_DIM), bf16),) * rows,
        "aaaaa",
        "pack",
        scratch=(pltpu.SMEM(cont_prompt.shape, jnp.int32),)
        + tuple(VMEM(source.shape, bf16) for source in sources[1:])
        + (pltpu.SemaphoreType.DMA((len(sources),)),),
    )(*map(hbm, sources))
    got = [
        lax.ppermute(packed[k], "rows", [(i, i ^ k) for i in range(rows)]) if k else packed[0]
        for k in range(rows)
    ]

    def resident(weight):
        return VMEM((2, weight.shape[1] // 2, weight.shape[2]), bf16)

    def reading(weight):
        return pl.CostEstimate(flops=0, bytes_accessed=2 * weight.size, transcendentals=0)

    sems = pltpu.SemaphoreType.DMA((2, rows))
    gate_w = call(
        load_body, resident(w_gate), "va", "load_gate", (sems,), MIB, reading(w_gate)
    )(packed[0], hbm(w_gate))

    start = lax.axis_index("heads") * plan.half + lax.axis_index("rows") * piece
    gain = lax.dynamic_slice_in_dim(norm_gain, start, piece).reshape(1, piece)
    keys = -(-(rows * (plan.block + 2 * plan.tokens)) // 128) * 128
    x, attn = call(
        functools.partial(attend_body, plan, rows),
        (shape((rows * experts, total, piece + HEAD_DIM), bf16), shape((total, piece), bf16)),
        "v" * (rows + 2),
        "attend",
        scratch=(
            VMEM((GROUP * total, HEAD_DIM), bf16),
            VMEM((GROUP * total, HEAD_DIM), bf16),
            VMEM((keys, HEAD_DIM), bf16),
            VMEM((total, HEAD_DIM), bf16),
        ),
    )(*got, gain, vmem(gate_w))
    x = lax.all_to_all(x, ("rows", "experts"), split_axis=0, concat_axis=0, tiled=True)
    own = x.reshape(rows, tokens, piece + HEAD_DIM)
    swap = [(0, 1), (1, 0)]
    other = lax.ppermute(own, "heads", swap)

    units = w_gate.shape[2]
    gate, up, up_w = call(
        first_half_body,
        (shape((tokens, units), f32), shape((tokens, units), f32), resident(w_up)),
        "vva",
        "first_half",
        (sems,),
        cost=reading(w_up),
    )(own, vmem(gate_w), hbm(w_up))
    hidden, down_w = call(
        second_half_body,
        (shape((tokens, units), bf16), resident(w_down)),
        "vvvvvva",
        "second_half",
        (sems,),
        cost=reading(w_down),
    )(other, own, gate, up, vmem(gate_w), vmem(up_w), hbm(w_down))
    other_hidden = lax.ppermute(hidden, "heads", swap)
    partial = call(
        down_first_body,
        shape((tokens, plan.half), f32),
        "vv",
        "down_first",
        cost=reading(w_down),
    )(hidden, vmem(down_w))
    blocks = call(
        functools.partial(down_second_body, rows),
        shape((rows * experts, plan.tokens, plan.half + piece), bf16),
        "vvvv",
        "down_second",
        cost=reading(w_down),
    )(other_hidden, partial, attn, vmem(down_w))
    blocks = lax.all_to_all(blocks, ("rows", "experts"), split_axis=0, concat_axis=0, tiled=True)
    out = shape(queries.shape, bf16)
    attn_out, moe_out = call(functools.partial(mix_body, rows), (out, out), "ssv", "mix")(
        routes, route_gates, blocks
    )
    return (attn_out, moe_out)


def solution(mesh):
    placed = (
        P(None, ("groups", "rows", "experts"), "heads"),
        P(None, ("groups", "rows", "experts"), None, "heads"),
        P(("groups", "experts"), "rows", None, "heads"),
        P(("groups", "rows", "experts")),
        P(None, ("groups", "rows", "experts"), "heads"),
        P(),
        P("experts", None, ("rows", "heads")),
        P("experts", None, ("rows", "heads")),
        P("experts", "rows", "heads"),
        P(None, ("groups", "rows", "experts"), None),
        P(None, ("groups", "rows", "experts"), None),
    )
    sizes = mesh.shape
    by_head = sizes["heads"] == 2 and sizes["rows"] * sizes["heads"] == KV_HEADS
    return jax.shard_map(
        per_device if by_head else per_device_wide,
        mesh=mesh,
        in_specs=placed,
        out_specs=(
            P(None, ("groups", "rows", "experts"), "heads"),
            P(None, ("groups", "rows", "experts"), "heads"),
        ),
        check_vma=False,
    )
```

```python
import functools

import jax
import jax.numpy as jnp
from jax import lax
from jax.experimental import pallas as pl
from jax.experimental.pallas import tpu as pltpu
from jax.sharding import PartitionSpec as P

HEADS = 48
KV_HEADS = 8
HEAD_DIM = 128
GROUP = HEADS // KV_HEADS

VMEM = pltpu.VMEM
MIB = 1 << 20


def fresh_terms(queries, new_kv):
    step_count, own_rows = (queries.shape[0], queries.shape[1])
    kv_local = new_kv.shape[-1] // HEAD_DIM
    group_size = HEADS // KV_HEADS
    grouped = queries.reshape(step_count, own_rows, kv_local, group_size, HEAD_DIM)
    fresh_keys = new_kv[:, :, 0].reshape(step_count, own_rows, kv_local, HEAD_DIM)
    fresh_values = new_kv[:, :, 1].reshape(step_count, own_rows, kv_local, HEAD_DIM)
    fresh_scores = jnp.einsum(
        "scgnd,tcgd->scgnt", grouped, fresh_keys, preferred_element_type=jnp.float32
    ) * HEAD_DIM ** (-0.5)
    future = jnp.arange(step_count)[None, :] > jnp.arange(step_count)[:, None]
    fresh_scores = jnp.where(future[:, None, None, None, :], -jnp.inf, fresh_scores)
    return (grouped, fresh_scores, fresh_values)


def attend_gathered(queries, new_kv, prefix_kv, local_prompt):
    grouped, fresh_scores, fresh_values = fresh_terms(queries, new_kv)
    own_rows = queries.shape[1]
    kv_local = new_kv.shape[-1] // HEAD_DIM
    cache = lax.all_gather(prefix_kv, "rows", axis=1, tiled=True)
    length = cache.shape[1]
    picked = jnp.take(cache, local_prompt, axis=0)
    cache_keys = picked[:, :, 0].reshape(own_rows, length, kv_local, HEAD_DIM)
    cache_values = picked[:, :, 1].reshape(own_rows, length, kv_local, HEAD_DIM)
    prefix_scores = jnp.einsum(
        "scgnd,ckgd->scgnk", grouped, cache_keys, preferred_element_type=jnp.float32
    ) * HEAD_DIM ** (-0.5)
    highest = jnp.maximum(jnp.max(prefix_scores, axis=-1), jnp.max(fresh_scores, axis=-1))
    prefix_expo = jnp.exp(prefix_scores - highest[..., None])
    fresh_expo = jnp.exp(fresh_scores - highest[..., None])
    totals = jnp.sum(prefix_expo, axis=-1) + jnp.sum(fresh_expo, axis=-1)
    weighted = jnp.einsum(
        "scgnk,ckgd->scgnd",
        prefix_expo.astype(jnp.bfloat16),
        cache_values,
        preferred_element_type=jnp.float32,
    )
    weighted = weighted + jnp.einsum(
        "scgnt,tcgd->scgnd",
        fresh_expo.astype(jnp.bfloat16),
        fresh_values,
        preferred_element_type=jnp.float32,
    )
    return (weighted, totals)


def per_device_wide(
    queries,
    new_kv,
    prefix_kv,
    cont_prompt,
    resid,
    norm_gain,
    w_gate,
    w_up,
    w_down,
    routes,
    route_gates,
):
    step_count, own_rows, half_width = queries.shape
    prompt_count = prefix_kv.shape[0]
    local_prompt = cont_prompt - lax.axis_index("experts") * prompt_count
    weighted, totals = attend_gathered(queries, new_kv, prefix_kv, local_prompt)
    attn_out = (
        (weighted / totals[..., None])
        .astype(jnp.bfloat16)
        .reshape(step_count, own_rows, half_width)
    )
    halves = (
        lax.all_gather(resid, "heads", axis=2, tiled=True),
        lax.all_gather(attn_out, "heads", axis=2, tiled=True),
    )
    combined = halves[0].astype(jnp.float32) + halves[1].astype(jnp.float32)
    square_mean = jnp.mean(combined * combined, axis=-1, keepdims=True)
    normed = (combined * lax.rsqrt(square_mean + 1e-05) * norm_gain.astype(jnp.float32)).astype(
        jnp.bfloat16
    )
    token_count = step_count * own_rows
    flat_tokens = normed.reshape(token_count, -1)
    flat_routes = routes.reshape(token_count, -1)
    experts = lax.axis_size("experts")
    matches = flat_routes[:, :, None] == jnp.arange(experts)[None, None, :]
    gate_weights = w_gate[0]
    up_weights = w_up[0]
    wanted = jnp.transpose(jnp.any(matches, axis=1))
    outgoing = jnp.where(wanted[:, :, None], flat_tokens[None], jnp.zeros((), jnp.bfloat16))
    arrived = lax.all_to_all(outgoing, "experts", split_axis=0, concat_axis=0, tiled=True)
    segment = lax.all_gather(arrived.reshape(experts * token_count, -1), "rows", axis=0, tiled=True)
    gate = jnp.dot(segment, gate_weights, preferred_element_type=jnp.float32)
    up_part = jnp.dot(segment, up_weights, preferred_element_type=jnp.float32)
    hidden = (jax.nn.silu(gate) * up_part).astype(jnp.bfloat16)
    paired = lax.all_gather(hidden, "heads", axis=1, tiled=True)
    down_rows = w_down[0]
    segment = paired
    summed = lax.psum_scatter(
        jnp.dot(segment, down_rows, preferred_element_type=jnp.float32).astype(jnp.bfloat16),
        "rows",
        scatter_dimension=0,
        tiled=True,
    )
    result = summed.reshape(experts, token_count, -1)
    returned = lax.all_to_all(result, "experts", split_axis=0, concat_axis=0, tiled=True)
    mixing = jnp.sum(
        jnp.where(matches, route_gates.reshape(token_count, -1)[:, :, None], 0.0), axis=1
    )
    mixture = jnp.einsum("ne,end->nd", mixing, returned.astype(jnp.float32))
    moe_out = mixture.astype(jnp.bfloat16).reshape(step_count, own_rows, half_width)
    return (attn_out, moe_out)


def call(body, outs, in_spaces, name, scratch=(), limit=4 * MIB, cost=None):
    spaces = {"v": VMEM, "s": pltpu.SMEM, "a": pl.ANY}
    single = not isinstance(outs, (list, tuple))
    shapes = [outs] if single else list(outs)
    specs = [pl.BlockSpec(memory_space=VMEM) for _ in shapes]
    return pl.pallas_call(
        body,
        out_shape=shapes[0] if single else tuple(shapes),
        in_specs=[pl.BlockSpec(memory_space=spaces[s]) for s in in_spaces],
        out_specs=specs[0] if single else tuple(specs),
        scratch_shapes=list(scratch),
        compiler_params=pltpu.CompilerParams(vmem_limit_bytes=limit),
        cost_estimate=cost,
        name=name,
    )


class Plan:
    def __init__(self, queries, new_kv, prefix_kv):
        self.steps, self.conts, self.half = queries.shape
        self.kv_local = new_kv.shape[-1] // HEAD_DIM
        self.prompts, self.positions = prefix_kv.shape[:2]
        self.tokens = self.steps * self.conts
        self.block = self.prompts * self.positions * 2
        self.fresh = self.block
        self.query = self.fresh + 2 * self.tokens
        self.resid = self.query + GROUP * self.tokens
        self.prompt = self.resid + GROUP * self.tokens
        self.rows = -(-(self.prompt + self.tokens) // 16) * 16


def pack_body(plan, prompt_hbm, q_hbm, new_hbm, prefix_hbm, resid_hbm, *rest):
    outs, buffers, sems = rest[: plan.kv_local], rest[plan.kv_local : -1], rest[-1]
    sources = (prompt_hbm, q_hbm, new_hbm, prefix_hbm, resid_hbm)
    copies = []
    for i, (source, buffer) in enumerate(zip(sources, buffers)):
        copy = pltpu.make_async_copy(source, buffer, sems.at[i])
        copy.start()
        copies.append(copy)
    for copy in copies:
        copy.wait()
    prompt_ref, q_ref, new_ref, prefix_ref, resid_ref = buffers
    t, c = plan.tokens, plan.conts
    base = lax.axis_index("experts") * plan.prompts
    row = lax.broadcasted_iota(jnp.int32, (c, HEAD_DIM), 0)
    local = jnp.zeros((c, HEAD_DIM), jnp.float32)
    for i in range(c):
        local = jnp.where(row == i, (prompt_ref[i] - base).astype(jnp.float32), local)
    local = local.astype(jnp.bfloat16)
    own = lax.axis_index("rows")
    for k, out_ref in enumerate(outs):
        h = own ^ k
        lanes = pl.ds(pl.multiple_of(h * HEAD_DIM, HEAD_DIM), HEAD_DIM)
        for p in range(plan.prompts):
            for i in range(plan.positions):
                out_ref[pl.ds((p * plan.positions + i) * 2, 2), :] = prefix_ref[p, i, :, lanes]
        for s in range(plan.steps):
            for i in range(c):
                out_ref[pl.ds(plan.fresh + (s * c + i) * 2, 2), :] = new_ref[s, i, :, lanes]
            for g in range(GROUP):
                head = pl.ds(pl.multiple_of((h * GROUP + g) * HEAD_DIM, HEAD_DIM), HEAD_DIM)
                out_ref[pl.ds(plan.query + g * t + s * c, c), :] = q_ref[s, :, head]
                out_ref[pl.ds(plan.resid + g * t + s * c, c), :] = resid_ref[s, :, head]
            out_ref[pl.ds(plan.prompt + s * c, c), :] = local


def attend_body(plan, rows, *refs):
    pieces, (gain_ref, _, x_ref, attn_ref, q_s, r_s, kv_s, p_s) = refs[:rows], refs[rows:]
    t, c = plan.tokens, plan.conts
    total = rows * t
    f32 = jnp.float32

    def place(own):
        for k, got_ref in enumerate(pieces):
            src = own ^ k
            kv_s[pl.ds(src * plan.block, plan.block), :] = got_ref[pl.ds(0, plan.block), :]
            late = pl.ds(rows * plan.block + src * 2 * t, 2 * t)
            kv_s[late, :] = got_ref[pl.ds(plan.fresh, 2 * t), :]
            p_s[pl.ds(src * t, t), :] = got_ref[pl.ds(plan.prompt, t), :]
            for g in range(GROUP):
                q_s[pl.ds(g * total + src * t, t), :] = got_ref[pl.ds(plan.query + g * t, t), :]
                r_s[pl.ds(g * total + src * t, t), :] = got_ref[pl.ds(plan.resid + g * t, t), :]

    for own in range(rows):
        pl.when(lax.axis_index("rows") == own)(functools.partial(place, own))
    used = rows * plan.block + rows * 2 * t
    spare = kv_s.shape[0] - used
    if spare:
        kv_s[pl.ds(used, spare), :] = jnp.zeros((spare, HEAD_DIM), jnp.bfloat16)
    kv = kv_s[...]
    scores = lax.dot_general(
        q_s[...], kv, (((1,), (1,)), ((), ())), preferred_element_type=f32
    ) * HEAD_DIM ** (-0.5)
    shape = scores.shape
    row = lax.broadcasted_iota(jnp.int32, shape, 0) % total
    col = lax.broadcasted_iota(jnp.int32, shape, 1)
    prompt = p_s[...].astype(f32)[:, :1]
    prompt = jnp.concatenate([prompt] * GROUP, axis=0).astype(jnp.int32)
    in_prefix = (col < rows * plan.block) & ((col % plan.block) // (2 * plan.positions) == prompt)
    late = col - rows * plan.block
    same = (late // (2 * t) == row // t) & (((late // 2) % t) % c == row % c)
    seen = ((late // 2) % t) // c <= (row % t) // c
    in_fresh = (late >= 0) & (col < used) & same & seen
    live = (col % 2 == 0) & (in_prefix | in_fresh)
    scores = jnp.where(live, scores, -jnp.inf)
    highest = jnp.max(scores, axis=-1, keepdims=True)
    expo = jnp.exp(scores - highest)
    totals = jnp.sum(expo, axis=-1, keepdims=True)
    weights = pltpu.roll(expo, 1, 1).astype(jnp.bfloat16)
    out = jnp.dot(weights, kv, preferred_element_type=f32) / totals
    attn = out.astype(jnp.bfloat16)
    combined = attn.astype(f32) + r_s[...].astype(f32)
    square = jnp.zeros((total, HEAD_DIM), f32)
    for g in range(GROUP):
        part = combined[g * total : (g + 1) * total]
        square = square + part * part
        lanes = pl.ds(g * HEAD_DIM, HEAD_DIM)
        x_ref[:, lanes] = (part * gain_ref[:, lanes].astype(f32)).astype(jnp.bfloat16)
        attn_ref[:, lanes] = attn[g * total : (g + 1) * total]
    square = jnp.sum(square, axis=-1, keepdims=True)
    high = square.astype(jnp.bfloat16)
    low = (square - high.astype(f32)).astype(jnp.bfloat16)
    lane = lax.broadcasted_iota(jnp.int32, (total, HEAD_DIM), 1)
    extra = jnp.where(lane == 0, high.astype(f32), jnp.where(lane == 1, low.astype(f32), 0.0))
    x_ref[:, pl.ds(GROUP * HEAD_DIM, HEAD_DIM)] = extra.astype(jnp.bfloat16)


def other_half(side):
    core = lax.axis_index("heads")
    return 1 - core if side else core


def stream(source, side, target, sems):
    parts = sems.shape[0]
    step = source.shape[1] // 2 // parts
    first = other_half(side) * (step * parts)
    copies = [
        pltpu.make_async_copy(
            source.at[0, pl.ds(first + k * step, step)], target.at[pl.ds(k * step, step)], sems.at[k]
        )
        for k in range(parts)
    ]
    for copy in copies:
        copy.start()
    return copies


def finish(copies):
    for copy in copies:
        copy.wait()


def load_body(sides, _, source, *rest):
    targets, sems = rest[:-1], rest[-1]
    copies = [stream(source, side, target, sems.at[side]) for side, target in zip(sides, targets)]
    for each in copies:
        finish(each)


def merge_body(own_ref, peer_ref, _, out_ref):
    total = own_ref.shape[0]
    out_ref[pl.ds(0, total), :] = own_ref[...]
    out_ref[pl.ds(total, total), :] = peer_ref[...]


def stack_body(*refs):
    *pieces, _, out_ref = refs
    for k, ref in enumerate(pieces):
        out_ref[k] = ref[...]


def products(x, weight, src, total):
    depth = x.shape[1]
    part = jnp.dot(
        x,
        weight[pl.ds(pl.multiple_of(src * depth, depth), depth)],
        preferred_element_type=jnp.float32,
    )
    return part if total is None else total + part


def own_chunk_body(x_ref, gate_w, up_w, up_hbm, gate_ref, up_ref, up_other, sems):
    copies = stream(up_hbm, 1, up_other, sems.at[0])
    depth = x_ref.shape[1] - HEAD_DIM
    x = x_ref[:, pl.ds(0, depth)]
    own = lax.axis_index("rows")
    gate_ref[...] = products(x, gate_w, own, None)
    up_ref[...] = products(x, up_w, own, None)
    finish(copies)


def first_half_body(x_ref, gate_in, up_in, gate_w, up_w, down_hbm, gate_ref, up_ref, down_w, sems):
    copies = stream(down_hbm, 0, down_w, sems.at[0])
    chunks, _, width = x_ref.shape
    own = lax.axis_index("rows")
    gate, up = gate_in[...], up_in[...]
    for k in range(1, chunks):
        x = x_ref[k, :, pl.ds(0, width - HEAD_DIM)]
        gate = products(x, gate_w, own ^ k, gate)
        up = products(x, up_w, own ^ k, up)
    gate_ref[...] = gate
    up_ref[...] = up
    finish(copies)


def second_half_body(
    x_ref, own_ref, gate_in, up_in, gate_w, up_w, down_hbm, hidden_ref, down_w, sems
):
    copies = stream(down_hbm, 1, down_w, sems.at[0])
    chunks, _, width = x_ref.shape
    depth = width - HEAD_DIM
    square = jnp.zeros((x_ref.shape[1], 1), jnp.float32)
    for ref in (own_ref, x_ref):
        for k in range(chunks):
            extra = ref[k, :, pl.ds(depth, HEAD_DIM)].astype(jnp.float32)
            square = square + jnp.sum(extra, axis=-1, keepdims=True)
    scale = lax.rsqrt(square / (2 * chunks * depth) + 1e-05)
    own = lax.axis_index("rows")
    gate, up = gate_in[...], up_in[...]
    for k in range(chunks):
        x = x_ref[k, :, pl.ds(0, depth)]
        gate = products(x, gate_w, own ^ k, gate)
        up = products(x, up_w, own ^ k, up)
    gate = gate * scale
    up = up * scale
    hidden_ref[...] = (gate / (1.0 + jnp.exp(-gate)) * up).astype(jnp.bfloat16)
    finish(copies)


def down_first_body(hidden_ref, down_w, out_ref):
    out_ref[...] = jnp.dot(hidden_ref[...], down_w[...], preferred_element_type=jnp.float32)


def down_second_body(rows, hidden_ref, own_ref, attn_ref, down_w, out_ref):
    total = own_ref[...] + jnp.dot(
        hidden_ref[...], down_w[...], preferred_element_type=jnp.float32
    )
    result = total.astype(jnp.bfloat16)
    pieces, t, width = out_ref.shape
    experts = pieces // rows
    half = result.shape[1]
    own = lax.axis_index("experts")
    for r in range(rows):
        attn = attn_ref[pl.ds(r * t, t), :]
        for e in range(experts):
            first = (e * rows + r) * t
            out_ref[r * experts + (own ^ e), :, pl.ds(0, half)] = result[first : first + t]
            out_ref[r * experts + (own ^ e), :, pl.ds(half, width - half)] = attn


def mix_body(rows, routes_ref, gates_ref, got_ref, attn_ref, moe_ref):
    pieces, t, width = got_ref.shape
    experts = pieces // rows
    steps, conts, half = moe_ref.shape
    own = lax.axis_index("experts")
    row = lax.broadcasted_iota(jnp.int32, (t, 1), 0)
    mixture = jnp.zeros((t, half), jnp.float32)
    for e in range(experts):
        summed = jnp.zeros((t, half), jnp.float32)
        for r in range(rows):
            summed = summed + got_ref[r * experts + e, :, pl.ds(0, half)].astype(jnp.float32)
        share = jnp.zeros((t, 1), jnp.float32)
        for s in range(steps):
            for c in range(conts):
                amount = jnp.float32(0.0)
                for k in range(routes_ref.shape[2]):
                    amount = amount + jnp.where(routes_ref[s, c, k] == e, gates_ref[s, c, k], 0.0)
                share = jnp.where(row == s * conts + c, amount, share)
        mixture = mixture + share * summed.astype(jnp.bfloat16).astype(jnp.float32)
    mixture = mixture.astype(jnp.bfloat16)
    piece = width - half
    for s in range(steps):
        moe_ref[s] = mixture[s * conts : (s + 1) * conts]
        for r in range(rows):
            attn_ref[s, :, pl.ds(r * piece, piece)] = got_ref[
                r * experts + own, pl.ds(s * conts, conts), pl.ds(half, piece)
            ]


def per_device(
    queries,
    new_kv,
    prefix_kv,
    cont_prompt,
    resid,
    norm_gain,
    w_gate,
    w_up,
    w_down,
    routes,
    route_gates,
):
    rows, experts = lax.axis_size("rows"), lax.axis_size("experts")
    plan = Plan(queries, new_kv, prefix_kv)
    bf16, f32 = jnp.bfloat16, jnp.float32
    shape = jax.ShapeDtypeStruct
    piece = GROUP * HEAD_DIM
    total = rows * plan.tokens
    tokens = experts * total

    hbm = functools.partial(pltpu.with_memory_space_constraint, memory_space=pltpu.HBM)
    vmem = functools.partial(pltpu.with_memory_space_constraint, memory_space=VMEM)
    sources = (cont_prompt, queries, new_kv, prefix_kv, resid)
    packed = call(
        functools.partial(pack_body, plan),
        (shape((plan.rows, HEAD_DIM), bf16),) * rows,
        "aaaaa",
        "pack",
        scratch=(pltpu.SMEM(cont_prompt.shape, jnp.int32),)
        + tuple(VMEM(source.shape, bf16) for source in sources[1:])
        + (pltpu.SemaphoreType.DMA((len(sources),)),),
    )(*map(hbm, sources))
    got = [
        lax.ppermute(packed[k], "rows", [(i, i ^ k) for i in range(rows)]) if k else packed[0]
        for k in range(rows)
    ]

    def half_of(weight):
        return VMEM((weight.shape[1] // 2, weight.shape[2]), bf16)

    def reading(weight, halves=1):
        return pl.CostEstimate(
            flops=tokens * weight.size * halves,
            bytes_accessed=weight.size * halves,
            transcendentals=0,
        )

    sems = pltpu.SemaphoreType.DMA((2, rows))
    gate_own, gate_other = map(
        vmem,
        call(
            functools.partial(load_body, (0, 1)),
            (half_of(w_gate), half_of(w_gate)),
            "va",
            "load_gate",
            (sems,),
            MIB,
            reading(w_gate, 2),
        )(packed[0], hbm(w_gate)),
    )

    start = lax.axis_index("heads") * plan.half + lax.axis_index("rows") * piece
    gain = lax.dynamic_slice_in_dim(norm_gain, start, piece).reshape(1, piece)
    keys = -(-(rows * (plan.block + 2 * plan.tokens)) // 128) * 128
    x, attn = call(
        functools.partial(attend_body, plan, rows),
        (shape((total, piece + HEAD_DIM), bf16), shape((total, piece), bf16)),
        "v" * (rows + 2),
        "attend",
        scratch=(
            VMEM((GROUP * total, HEAD_DIM), bf16),
            VMEM((GROUP * total, HEAD_DIM), bf16),
            VMEM((keys, HEAD_DIM), bf16),
            VMEM((total, HEAD_DIM), bf16),
        ),
    )(*got, gain, gate_own)
    swap = [(0, 1), (1, 0)]
    peer = lax.ppermute(x, "experts", swap)
    up_own = vmem(
        call(
            functools.partial(load_body, (0,)),
            half_of(w_up),
            "va",
            "load_up",
            (sems,),
            MIB,
            reading(w_up),
        )(x, hbm(w_up))
    )
    merged = call(merge_body, shape((tokens, piece + HEAD_DIM), bf16), "vvv", "merge")(
        x, peer, up_own
    )
    chunks = [
        lax.ppermute(merged, "rows", [(i, i ^ k) for i in range(rows)]) if k else merged
        for k in range(rows)
    ]
    units = w_gate.shape[2]
    products_of = shape((tokens, units), f32)
    gate, up, up_other = call(
        own_chunk_body,
        (products_of, products_of, half_of(w_up)),
        "vvva",
        "own_chunk",
        (sems,),
        cost=reading(w_up),
    )(merged, gate_own, up_own, hbm(w_up))
    own = call(
        stack_body,
        shape((rows, tokens, piece + HEAD_DIM), bf16),
        "v" * (rows + 1),
        "stack",
    )(*chunks, vmem(up_other))
    other = lax.ppermute(own, "heads", swap)
    gate, up, down_own = call(
        first_half_body,
        (products_of, products_of, half_of(w_down)),
        "vvvvva",
        "first_half",
        (sems,),
        cost=reading(w_down),
    )(own, gate, up, gate_own, up_own, hbm(w_down))
    hidden, down_other = call(
        second_half_body,
        (shape((tokens, units), bf16), half_of(w_down)),
        "vvvvvva",
        "second_half",
        (sems,),
        cost=reading(w_down),
    )(other, own, gate, up, gate_other, vmem(up_other), hbm(w_down))
    other_hidden = lax.ppermute(hidden, "heads", swap)
    partial = call(
        down_first_body,
        shape((tokens, plan.half), f32),
        "vv",
        "down_first",
        cost=reading(w_down),
    )(hidden, vmem(down_own))
    blocks = call(
        functools.partial(down_second_body, rows),
        shape((rows * experts, plan.tokens, plan.half + piece), bf16),
        "vvvv",
        "down_second",
        cost=reading(w_down),
    )(other_hidden, partial, attn, vmem(down_other))
    blocks = lax.all_to_all(blocks, ("rows", "experts"), split_axis=0, concat_axis=0, tiled=True)
    out = shape(queries.shape, bf16)
    attn_out, moe_out = call(functools.partial(mix_body, rows), (out, out), "ssv", "mix")(
        routes, route_gates, blocks
    )
    return (attn_out, moe_out)


def solution(mesh):
    placed = (
        P(None, ("groups", "rows", "experts"), "heads"),
        P(None, ("groups", "rows", "experts"), None, "heads"),
        P(("groups", "experts"), "rows", None, "heads"),
        P(("groups", "rows", "experts")),
        P(None, ("groups", "rows", "experts"), "heads"),
        P(),
        P("experts", None, ("rows", "heads")),
        P("experts", None, ("rows", "heads")),
        P("experts", "rows", "heads"),
        P(None, ("groups", "rows", "experts"), None),
        P(None, ("groups", "rows", "experts"), None),
    )
    sizes = mesh.shape
    by_head = (
        sizes["heads"] == 2
        and sizes["experts"] == 2
        and sizes["rows"] == 4
        and sizes["rows"] * sizes["heads"] == KV_HEADS
    )
    return jax.shard_map(
        per_device if by_head else per_device_wide,
        mesh=mesh,
        in_specs=placed,
        out_specs=(
            P(None, ("groups", "rows", "experts"), "heads"),
            P(None, ("groups", "rows", "experts"), "heads"),
        ),
        check_vma=False,
    )
```

```python
import functools

import jax
import jax.numpy as jnp
from jax import lax
from jax.experimental import pallas as pl
from jax.experimental.pallas import tpu as pltpu
from jax.sharding import PartitionSpec as P

HEADS = 48
KV_HEADS = 8
HEAD_DIM = 128
GROUP = HEADS // KV_HEADS

VMEM = pltpu.VMEM
MIB = 1 << 20
PACK_COVER = 40 * MIB
FLOPS = 1000
OWN_COVER = 40 * MIB
FIRST_COVER = 8 * MIB
SECOND_COVER = 8 * MIB
FIRST_LIMIT = 4 * MIB
SECOND_LIMIT = 24 * MIB
DOWN_LIMIT = 40 * MIB
ATTEND_COVER = MIB
MERGE_COVER = MIB


def fresh_terms(queries, new_kv):
    step_count, own_rows = (queries.shape[0], queries.shape[1])
    kv_local = new_kv.shape[-1] // HEAD_DIM
    group_size = HEADS // KV_HEADS
    grouped = queries.reshape(step_count, own_rows, kv_local, group_size, HEAD_DIM)
    fresh_keys = new_kv[:, :, 0].reshape(step_count, own_rows, kv_local, HEAD_DIM)
    fresh_values = new_kv[:, :, 1].reshape(step_count, own_rows, kv_local, HEAD_DIM)
    fresh_scores = jnp.einsum(
        "scgnd,tcgd->scgnt", grouped, fresh_keys, preferred_element_type=jnp.float32
    ) * HEAD_DIM ** (-0.5)
    future = jnp.arange(step_count)[None, :] > jnp.arange(step_count)[:, None]
    fresh_scores = jnp.where(future[:, None, None, None, :], -jnp.inf, fresh_scores)
    return (grouped, fresh_scores, fresh_values)


def attend_gathered(queries, new_kv, prefix_kv, local_prompt):
    grouped, fresh_scores, fresh_values = fresh_terms(queries, new_kv)
    own_rows = queries.shape[1]
    kv_local = new_kv.shape[-1] // HEAD_DIM
    cache = lax.all_gather(prefix_kv, "rows", axis=1, tiled=True)
    length = cache.shape[1]
    picked = jnp.take(cache, local_prompt, axis=0)
    cache_keys = picked[:, :, 0].reshape(own_rows, length, kv_local, HEAD_DIM)
    cache_values = picked[:, :, 1].reshape(own_rows, length, kv_local, HEAD_DIM)
    prefix_scores = jnp.einsum(
        "scgnd,ckgd->scgnk", grouped, cache_keys, preferred_element_type=jnp.float32
    ) * HEAD_DIM ** (-0.5)
    highest = jnp.maximum(jnp.max(prefix_scores, axis=-1), jnp.max(fresh_scores, axis=-1))
    prefix_expo = jnp.exp(prefix_scores - highest[..., None])
    fresh_expo = jnp.exp(fresh_scores - highest[..., None])
    totals = jnp.sum(prefix_expo, axis=-1) + jnp.sum(fresh_expo, axis=-1)
    weighted = jnp.einsum(
        "scgnk,ckgd->scgnd",
        prefix_expo.astype(jnp.bfloat16),
        cache_values,
        preferred_element_type=jnp.float32,
    )
    weighted = weighted + jnp.einsum(
        "scgnt,tcgd->scgnd",
        fresh_expo.astype(jnp.bfloat16),
        fresh_values,
        preferred_element_type=jnp.float32,
    )
    return (weighted, totals)


def per_device_wide(
    queries,
    new_kv,
    prefix_kv,
    cont_prompt,
    resid,
    norm_gain,
    w_gate,
    w_up,
    w_down,
    routes,
    route_gates,
):
    step_count, own_rows, half_width = queries.shape
    prompt_count = prefix_kv.shape[0]
    local_prompt = cont_prompt - lax.axis_index("experts") * prompt_count
    weighted, totals = attend_gathered(queries, new_kv, prefix_kv, local_prompt)
    attn_out = (
        (weighted / totals[..., None])
        .astype(jnp.bfloat16)
        .reshape(step_count, own_rows, half_width)
    )
    halves = (
        lax.all_gather(resid, "heads", axis=2, tiled=True),
        lax.all_gather(attn_out, "heads", axis=2, tiled=True),
    )
    combined = halves[0].astype(jnp.float32) + halves[1].astype(jnp.float32)
    square_mean = jnp.mean(combined * combined, axis=-1, keepdims=True)
    normed = (combined * lax.rsqrt(square_mean + 1e-05) * norm_gain.astype(jnp.float32)).astype(
        jnp.bfloat16
    )
    token_count = step_count * own_rows
    flat_tokens = normed.reshape(token_count, -1)
    flat_routes = routes.reshape(token_count, -1)
    experts = lax.axis_size("experts")
    matches = flat_routes[:, :, None] == jnp.arange(experts)[None, None, :]
    gate_weights = w_gate[0]
    up_weights = w_up[0]
    wanted = jnp.transpose(jnp.any(matches, axis=1))
    outgoing = jnp.where(wanted[:, :, None], flat_tokens[None], jnp.zeros((), jnp.bfloat16))
    arrived = lax.all_to_all(outgoing, "experts", split_axis=0, concat_axis=0, tiled=True)
    segment = lax.all_gather(arrived.reshape(experts * token_count, -1), "rows", axis=0, tiled=True)
    gate = jnp.dot(segment, gate_weights, preferred_element_type=jnp.float32)
    up_part = jnp.dot(segment, up_weights, preferred_element_type=jnp.float32)
    hidden = (jax.nn.silu(gate) * up_part).astype(jnp.bfloat16)
    paired = lax.all_gather(hidden, "heads", axis=1, tiled=True)
    down_rows = w_down[0]
    segment = paired
    summed = lax.psum_scatter(
        jnp.dot(segment, down_rows, preferred_element_type=jnp.float32).astype(jnp.bfloat16),
        "rows",
        scatter_dimension=0,
        tiled=True,
    )
    result = summed.reshape(experts, token_count, -1)
    returned = lax.all_to_all(result, "experts", split_axis=0, concat_axis=0, tiled=True)
    mixing = jnp.sum(
        jnp.where(matches, route_gates.reshape(token_count, -1)[:, :, None], 0.0), axis=1
    )
    mixture = jnp.einsum("ne,end->nd", mixing, returned.astype(jnp.float32))
    moe_out = mixture.astype(jnp.bfloat16).reshape(step_count, own_rows, half_width)
    return (attn_out, moe_out)


def call(body, outs, in_spaces, name, scratch=(), limit=4 * MIB, cost=None):
    spaces = {"v": VMEM, "s": pltpu.SMEM, "a": pl.ANY}
    single = not isinstance(outs, (list, tuple))
    shapes = [outs] if single else list(outs)
    specs = [pl.BlockSpec(memory_space=VMEM) for _ in shapes]
    return pl.pallas_call(
        body,
        out_shape=shapes[0] if single else tuple(shapes),
        in_specs=[pl.BlockSpec(memory_space=spaces[s]) for s in in_spaces],
        out_specs=specs[0] if single else tuple(specs),
        scratch_shapes=list(scratch),
        compiler_params=pltpu.CompilerParams(vmem_limit_bytes=limit),
        cost_estimate=cost,
        name=name,
    )


class Plan:
    def __init__(self, queries, new_kv, prefix_kv):
        self.steps, self.conts, self.half = queries.shape
        self.kv_local = new_kv.shape[-1] // HEAD_DIM
        self.prompts, self.positions = prefix_kv.shape[:2]
        self.tokens = self.steps * self.conts
        self.block = self.prompts * self.positions * 2
        self.fresh = self.block
        self.query = self.fresh + 2 * self.tokens
        self.resid = self.query + GROUP * self.tokens
        self.prompt = self.resid + GROUP * self.tokens
        self.rows = -(-(self.prompt + self.tokens) // 16) * 16


def fetch_body(plan, *refs):
    count = (len(refs) - 2) // 2
    sources, targets, (prompts, sems) = refs[:count], refs[count : 2 * count], refs[2 * count :]
    copies = [
        pltpu.make_async_copy(source, target, sems.at[i])
        for i, (source, target) in enumerate(zip(sources, (prompts,) + targets[1:]))
    ]
    for copy in copies:
        copy.start()
    for copy in copies:
        copy.wait()
    c = plan.conts
    base = lax.axis_index("experts") * plan.prompts
    row = lax.broadcasted_iota(jnp.int32, (c, HEAD_DIM), 0)
    local = jnp.zeros((c, HEAD_DIM), jnp.float32)
    for i in range(c):
        local = jnp.where(row == i, (prompts[i] - base).astype(jnp.float32), local)
    targets[0][...] = local.astype(jnp.bfloat16)


def pack_body(plan, local_ref, q_ref, new_ref, prefix_ref, resid_ref, *outs):
    t, c = plan.tokens, plan.conts
    own = lax.axis_index("rows")
    for k, out_ref in enumerate(outs):
        h = own ^ k
        lanes = pl.ds(pl.multiple_of(h * HEAD_DIM, HEAD_DIM), HEAD_DIM)
        for p in range(plan.prompts):
            for i in range(plan.positions):
                out_ref[pl.ds((p * plan.positions + i) * 2, 2), :] = prefix_ref[p, i, :, lanes]
        for s in range(plan.steps):
            for i in range(c):
                out_ref[pl.ds(plan.fresh + (s * c + i) * 2, 2), :] = new_ref[s, i, :, lanes]
            for g in range(GROUP):
                head = pl.ds(pl.multiple_of((h * GROUP + g) * HEAD_DIM, HEAD_DIM), HEAD_DIM)
                out_ref[pl.ds(plan.query + g * t + s * c, c), :] = q_ref[s, :, head]
                out_ref[pl.ds(plan.resid + g * t + s * c, c), :] = resid_ref[s, :, head]
            out_ref[pl.ds(plan.prompt + s * c, c), :] = local_ref[...]


def attend_body(plan, rows, *refs):
    pieces, (gain_ref, x_ref, attn_ref, q_s, r_s, kv_s, p_s, gain_s) = refs[:rows], refs[rows:]
    t, c = plan.tokens, plan.conts
    total = rows * t
    f32 = jnp.float32

    def place(own):
        for k, got_ref in enumerate(pieces):
            src = own ^ k
            kv_s[pl.ds(src * plan.block, plan.block), :] = got_ref[pl.ds(0, plan.block), :]
            late = pl.ds(rows * plan.block + src * 2 * t, 2 * t)
            kv_s[late, :] = got_ref[pl.ds(plan.fresh, 2 * t), :]
            p_s[pl.ds(src * t, t), :] = got_ref[pl.ds(plan.prompt, t), :]
            for g in range(GROUP):
                q_s[pl.ds(g * total + src * t, t), :] = got_ref[pl.ds(plan.query + g * t, t), :]
                r_s[pl.ds(g * total + src * t, t), :] = got_ref[pl.ds(plan.resid + g * t, t), :]

    for own in range(rows):
        pl.when(lax.axis_index("rows") == own)(functools.partial(place, own))
    used = rows * plan.block + rows * 2 * t
    spare = kv_s.shape[0] - used
    if spare:
        kv_s[pl.ds(used, spare), :] = jnp.zeros((spare, HEAD_DIM), jnp.bfloat16)
    kv = kv_s[...]
    scores = lax.dot_general(
        q_s[...], kv, (((1,), (1,)), ((), ())), preferred_element_type=f32
    ) * HEAD_DIM ** (-0.5)
    shape = scores.shape
    row = lax.broadcasted_iota(jnp.int32, shape, 0) % total
    col = lax.broadcasted_iota(jnp.int32, shape, 1)
    prompt = p_s[...].astype(f32)[:, :1]
    prompt = jnp.concatenate([prompt] * GROUP, axis=0).astype(jnp.int32)
    in_prefix = (col < rows * plan.block) & ((col % plan.block) // (2 * plan.positions) == prompt)
    late = col - rows * plan.block
    same = (late // (2 * t) == row // t) & (((late // 2) % t) % c == row % c)
    seen = ((late // 2) % t) // c <= (row % t) // c
    in_fresh = (late >= 0) & (col < used) & same & seen
    live = (col % 2 == 0) & (in_prefix | in_fresh)
    scores = jnp.where(live, scores, -jnp.inf)
    highest = jnp.max(scores, axis=-1, keepdims=True)
    expo = jnp.exp(scores - highest)
    totals = jnp.sum(expo, axis=-1, keepdims=True)
    weights = pltpu.roll(expo, 1, 1).astype(jnp.bfloat16)
    out = jnp.dot(weights, kv, preferred_element_type=f32) / totals
    attn = out.astype(jnp.bfloat16)
    attn_ref[...] = attn
    gain_s[...] = gain_ref[...].astype(f32)
    first = (lax.axis_index("heads") * rows + lax.axis_index("rows")) * GROUP
    combined = attn.astype(f32) + r_s[...].astype(f32)
    square = jnp.zeros((total, HEAD_DIM), f32)
    for g in range(GROUP):
        part = combined[g * total : (g + 1) * total]
        square = square + part * part
        gained = part * gain_s[pl.ds(first + g, 1), :]
        x_ref[:, pl.ds(g * HEAD_DIM, HEAD_DIM)] = gained.astype(jnp.bfloat16)
    square = jnp.sum(square, axis=-1, keepdims=True)
    high = square.astype(jnp.bfloat16)
    low = (square - high.astype(f32)).astype(jnp.bfloat16)
    lane = lax.broadcasted_iota(jnp.int32, (total, HEAD_DIM), 1)
    extra = jnp.where(lane == 0, high.astype(f32), jnp.where(lane == 1, low.astype(f32), 0.0))
    x_ref[:, pl.ds(GROUP * HEAD_DIM, HEAD_DIM)] = extra.astype(jnp.bfloat16)


def to_row(column, first, lanes):
    shape = (column.shape[0], lanes)
    hit = lax.broadcasted_iota(jnp.int32, shape, 1) == lax.broadcasted_iota(jnp.int32, shape, 0) + first
    return jnp.sum(jnp.where(hit, column, 0.0), axis=0, keepdims=True)


def to_column(row, count):
    shape = (count, row.shape[1])
    hit = lax.broadcasted_iota(jnp.int32, shape, 1) == lax.broadcasted_iota(jnp.int32, shape, 0)
    return jnp.sum(jnp.where(hit, row, 0.0), axis=1, keepdims=True)


def merge_body(plan, rows, own_ref, peer_ref, attn_ref, *outs):
    t = plan.tokens
    total, width = own_ref.shape
    depth = width - HEAD_DIM
    spare = pl.ds(depth, HEAD_DIM)
    high, low = [], []
    for i, ref in enumerate((own_ref, peer_ref)):
        extra = ref[:, spare].astype(jnp.float32)
        high.append(to_row(extra[:, 0:1], i * total, HEAD_DIM))
        low.append(to_row(extra[:, 1:2], i * total, HEAD_DIM))
    row = lax.broadcasted_iota(jnp.int32, (2 * total - GROUP * t, HEAD_DIM), 0)
    squares = jnp.where(row == 0, high[0] + high[1], jnp.where(row == 1, low[0] + low[1], 0.0))
    squares = squares.astype(jnp.bfloat16)
    for out_ref in outs:
        for i, ref in enumerate((own_ref, peer_ref)):
            out_ref[pl.ds(i * total, total), pl.ds(0, depth)] = ref[:, pl.ds(0, depth)]
        out_ref[pl.ds(GROUP * t, row.shape[0]), spare] = squares

    def place(own):
        for k, out_ref in enumerate(outs):
            for g in range(GROUP):
                part = attn_ref[pl.ds(g * total + (own ^ k) * t, t), :]
                out_ref[pl.ds(g * t, t), spare] = part

    for own in range(rows):
        pl.when(lax.axis_index("rows") == own)(functools.partial(place, own))


def stack_body(*refs):
    *pieces, _, out_ref = refs
    for k, ref in enumerate(pieces):
        out_ref[k] = ref[...]


def products(side, x, weight, k, total):
    depth = x.shape[1]
    core = lax.axis_index("heads")
    core = 1 - core if side else core
    half = weight.shape[1] // 2
    first = pl.multiple_of(core * half + (lax.axis_index("rows") ^ k) * depth, depth)
    part = jnp.dot(x, weight[0, pl.ds(first, depth)], preferred_element_type=jnp.float32)
    return part if total is None else total + part


def own_chunk_body(x_ref, gate_w, up_w, gate_ref, up_ref):
    x = x_ref[:, pl.ds(0, x_ref.shape[1] - HEAD_DIM)]
    gate_ref[...] = products(0, x, gate_w, 0, None)
    up_ref[...] = products(0, x, up_w, 0, None)


def first_half_body(x_ref, gate_in, up_in, gate_w, up_w, gate_ref, up_ref):
    chunks, _, width = x_ref.shape
    gate, up = gate_in[...], up_in[...]
    for k in range(1, chunks):
        x = x_ref[k, :, pl.ds(0, width - HEAD_DIM)]
        gate = products(0, x, gate_w, k, gate)
        up = products(0, x, up_w, k, up)
    gate_ref[...] = gate
    up_ref[...] = up


def second_half_body(plan, x_ref, own_ref, gate_in, up_in, gate_w, up_w, hidden_ref):
    chunks, tokens, width = x_ref.shape
    depth = width - HEAD_DIM
    first = GROUP * plan.tokens
    square = jnp.zeros((tokens - first, HEAD_DIM), jnp.float32)
    for ref in (own_ref, x_ref):
        for k in range(chunks):
            extra = ref[k, pl.ds(first, tokens - first), pl.ds(depth, HEAD_DIM)]
            square = square + extra.astype(jnp.float32)
    square = to_column(square[0:1] + square[1:2], tokens)
    scale = lax.rsqrt(square / (2 * chunks * depth) + 1e-05)
    gate, up = gate_in[...], up_in[...]
    for k in range(chunks):
        x = x_ref[k, :, pl.ds(0, depth)]
        gate = products(1, x, gate_w, k, gate)
        up = products(1, x, up_w, k, up)
    gate = gate * scale
    up = up * scale
    hidden_ref[...] = (gate / (1.0 + jnp.exp(-gate)) * up).astype(jnp.bfloat16)


def down_product(side, hidden_ref, down_w):
    depth = hidden_ref.shape[1]
    core = lax.axis_index("heads")
    first = pl.multiple_of((1 - core if side else core) * depth, depth)
    return jnp.dot(
        hidden_ref[...], down_w[0, pl.ds(first, depth)], preferred_element_type=jnp.float32
    )


def down_first_body(hidden_ref, down_w, out_ref):
    out_ref[...] = down_product(0, hidden_ref, down_w)


def down_second_body(rows, hidden_ref, own_ref, down_w, out_ref):
    result = (own_ref[...] + down_product(1, hidden_ref, down_w)).astype(jnp.bfloat16)
    pieces, t, _ = out_ref.shape
    experts = pieces // rows
    own = lax.axis_index("experts")
    for r in range(rows):
        for e in range(experts):
            first = (e * rows + r) * t
            out_ref[r * experts + (own ^ e)] = result[first : first + t]


def mix_body(rows, routes_ref, gates_ref, got_ref, own_ref, attn_ref, moe_ref):
    pieces, t, half = got_ref.shape
    experts = pieces // rows
    steps, conts, _ = moe_ref.shape
    depth = own_ref.shape[2] - HEAD_DIM
    for k in range(rows):
        head = (lax.axis_index("rows") ^ k) * GROUP
        for g in range(GROUP):
            lanes = pl.ds(pl.multiple_of((head + g) * HEAD_DIM, HEAD_DIM), HEAD_DIM)
            for s in range(steps):
                attn_ref[s, :, lanes] = own_ref[
                    k, pl.ds(g * t + s * conts, conts), pl.ds(depth, HEAD_DIM)
                ]
    row = lax.broadcasted_iota(jnp.int32, (t, 1), 0)
    mixture = jnp.zeros((t, half), jnp.float32)
    for e in range(experts):
        summed = jnp.zeros((t, half), jnp.float32)
        for r in range(rows):
            summed = summed + got_ref[r * experts + e].astype(jnp.float32)
        share = jnp.zeros((t, 1), jnp.float32)
        for s in range(steps):
            for c in range(conts):
                amount = jnp.float32(0.0)
                for k in range(routes_ref.shape[2]):
                    amount = amount + jnp.where(routes_ref[s, c, k] == e, gates_ref[s, c, k], 0.0)
                share = jnp.where(row == s * conts + c, amount, share)
        mixture = mixture + share * summed.astype(jnp.bfloat16).astype(jnp.float32)
    mixture = mixture.astype(jnp.bfloat16)
    for s in range(steps):
        moe_ref[s] = mixture[s * conts : (s + 1) * conts]


def per_device(
    queries,
    new_kv,
    prefix_kv,
    cont_prompt,
    resid,
    norm_gain,
    w_gate,
    w_up,
    w_down,
    routes,
    route_gates,
):
    rows, experts = lax.axis_size("rows"), lax.axis_size("experts")
    plan = Plan(queries, new_kv, prefix_kv)
    bf16, f32 = jnp.bfloat16, jnp.float32
    shape = jax.ShapeDtypeStruct
    piece = GROUP * HEAD_DIM
    total = rows * plan.tokens
    tokens = experts * total

    hbm = functools.partial(pltpu.with_memory_space_constraint, memory_space=pltpu.HBM)
    vmem = functools.partial(pltpu.with_memory_space_constraint, memory_space=VMEM)
    gate_w, up_w, down_w = w_gate, w_up, w_down

    def cover(size):
        return pl.CostEstimate(flops=FLOPS * size, bytes_accessed=size, transcendentals=0)

    sources = (cont_prompt, queries, new_kv, prefix_kv, resid)
    fetched = call(
        functools.partial(fetch_body, plan),
        (VMEM((plan.conts, HEAD_DIM), bf16),)
        + tuple(VMEM(source.shape, bf16) for source in sources[1:]),
        "aaaaa",
        "fetch",
        scratch=(
            pltpu.SMEM(cont_prompt.shape, jnp.int32),
            pltpu.SemaphoreType.DMA((len(sources),)),
        ),
    )(*map(hbm, sources))
    packed = call(
        functools.partial(pack_body, plan),
        (shape((plan.rows, HEAD_DIM), bf16),) * rows,
        "vvvvv",
        "pack",
        cost=cover(PACK_COVER),
    )(*map(vmem, fetched))

    def spread(pieces):
        return [
            lax.ppermute(pieces[k], "rows", [(i, i ^ k) for i in range(rows)]) if k else pieces[0]
            for k in range(rows)
        ]

    keys = -(-(rows * (plan.block + 2 * plan.tokens)) // 128) * 128
    lanes = piece + HEAD_DIM
    x, attn = call(
        functools.partial(attend_body, plan, rows),
        (shape((total, lanes), bf16), shape((GROUP * total, HEAD_DIM), bf16)),
        "v" * (rows + 1),
        "attend",
        scratch=(
            VMEM((GROUP * total, HEAD_DIM), bf16),
            VMEM((GROUP * total, HEAD_DIM), bf16),
            VMEM((keys, HEAD_DIM), bf16),
            VMEM((total, HEAD_DIM), bf16),
            VMEM((norm_gain.size // HEAD_DIM, HEAD_DIM), f32),
        ),
        cost=cover(ATTEND_COVER),
    )(*spread(packed), norm_gain.reshape(-1, HEAD_DIM))
    swap = [(0, 1), (1, 0)]
    peer = lax.ppermute(x, "experts", swap)
    merged = call(
        functools.partial(merge_body, plan, rows),
        (shape((tokens, lanes), bf16),) * rows,
        "vvv",
        "merge",
        cost=cover(MERGE_COVER),
    )(x, peer, attn)
    chunks = spread(merged)
    units = w_gate.shape[2]
    products_of = shape((tokens, units), f32)
    gate, up = call(
        own_chunk_body,
        (products_of, products_of),
        "vvv",
        "own_chunk",
        cost=cover(OWN_COVER),
    )(merged[0], gate_w, up_w)
    own = call(stack_body, shape((rows, tokens, lanes), bf16), "v" * (rows + 1), "stack")(
        *chunks, gate
    )
    other = lax.ppermute(own, "heads", swap)
    gate, up = call(
        first_half_body,
        (products_of, products_of),
        "vvvvv",
        "first_half",
        limit=FIRST_LIMIT,
        cost=cover(FIRST_COVER),
    )(own, gate, up, gate_w, up_w)
    hidden = call(
        functools.partial(second_half_body, plan),
        shape((tokens, units), bf16),
        "vvvvvv",
        "second_half",
        limit=SECOND_LIMIT,
        cost=cover(SECOND_COVER),
    )(other, own, gate, up, gate_w, up_w)
    other_hidden = lax.ppermute(hidden, "heads", swap)
    partial = call(
        down_first_body,
        shape((tokens, plan.half), f32),
        "vv",
        "down_first",
        limit=DOWN_LIMIT,
        cost=cover(2 * plan.half * units),
    )(hidden, down_w)
    blocks = call(
        functools.partial(down_second_body, rows),
        shape((rows * experts, plan.tokens, plan.half), bf16),
        "vvv",
        "down_second",
        cost=cover(2 * plan.half * units),
    )(other_hidden, partial, down_w)
    blocks = lax.all_to_all(blocks, ("rows", "experts"), split_axis=0, concat_axis=0, tiled=True)
    out = shape(queries.shape, bf16)
    attn_out, moe_out = call(functools.partial(mix_body, rows), (out, out), "ssvv", "mix")(
        routes, route_gates, blocks, own
    )
    return (attn_out, moe_out)


def solution(mesh):
    placed = (
        P(None, ("groups", "rows", "experts"), "heads"),
        P(None, ("groups", "rows", "experts"), None, "heads"),
        P(("groups", "experts"), "rows", None, "heads"),
        P(("groups", "rows", "experts")),
        P(None, ("groups", "rows", "experts"), "heads"),
        P(),
        P("experts", None, ("rows", "heads")),
        P("experts", None, ("rows", "heads")),
        P("experts", "rows", "heads"),
        P(None, ("groups", "rows", "experts"), None),
        P(None, ("groups", "rows", "experts"), None),
    )
    sizes = mesh.shape
    by_head = (
        sizes["heads"] == 2
        and sizes["experts"] == 2
        and sizes["rows"] == 4
        and sizes["rows"] * sizes["heads"] == KV_HEADS
    )
    return jax.shard_map(
        per_device if by_head else per_device_wide,
        mesh=mesh,
        in_specs=placed,
        out_specs=(
            P(None, ("groups", "rows", "experts"), "heads"),
            P(None, ("groups", "rows", "experts"), "heads"),
        ),
        check_vma=False,
    )
```

```python
import functools

import jax
import jax.numpy as jnp
from jax import lax
from jax.experimental import pallas as pl
from jax.experimental.pallas import tpu as pltpu
from jax.sharding import PartitionSpec as P

HEADS = 48
KV_HEADS = 8
HEAD_DIM = 128
GROUP = HEADS // KV_HEADS

VMEM = pltpu.VMEM
MIB = 1 << 20
PACK_COVER = 40 * MIB
FLOPS = 1000
OWN_COVER = 40 * MIB
FIRST_COVER = 1 * MIB
SECOND_COVER = 1 * MIB
FIRST_LIMIT = 4 * MIB
SECOND_LIMIT = 4 * MIB
DOWN_LIMIT = 4 * MIB
ATTEND_COVER = MIB
MERGE_COVER = MIB


def fresh_terms(queries, new_kv):
    step_count, own_rows = (queries.shape[0], queries.shape[1])
    kv_local = new_kv.shape[-1] // HEAD_DIM
    group_size = HEADS // KV_HEADS
    grouped = queries.reshape(step_count, own_rows, kv_local, group_size, HEAD_DIM)
    fresh_keys = new_kv[:, :, 0].reshape(step_count, own_rows, kv_local, HEAD_DIM)
    fresh_values = new_kv[:, :, 1].reshape(step_count, own_rows, kv_local, HEAD_DIM)
    fresh_scores = jnp.einsum(
        "scgnd,tcgd->scgnt", grouped, fresh_keys, preferred_element_type=jnp.float32
    ) * HEAD_DIM ** (-0.5)
    future = jnp.arange(step_count)[None, :] > jnp.arange(step_count)[:, None]
    fresh_scores = jnp.where(future[:, None, None, None, :], -jnp.inf, fresh_scores)
    return (grouped, fresh_scores, fresh_values)


def attend_gathered(queries, new_kv, prefix_kv, local_prompt):
    grouped, fresh_scores, fresh_values = fresh_terms(queries, new_kv)
    own_rows = queries.shape[1]
    kv_local = new_kv.shape[-1] // HEAD_DIM
    cache = lax.all_gather(prefix_kv, "rows", axis=1, tiled=True)
    length = cache.shape[1]
    picked = jnp.take(cache, local_prompt, axis=0)
    cache_keys = picked[:, :, 0].reshape(own_rows, length, kv_local, HEAD_DIM)
    cache_values = picked[:, :, 1].reshape(own_rows, length, kv_local, HEAD_DIM)
    prefix_scores = jnp.einsum(
        "scgnd,ckgd->scgnk", grouped, cache_keys, preferred_element_type=jnp.float32
    ) * HEAD_DIM ** (-0.5)
    highest = jnp.maximum(jnp.max(prefix_scores, axis=-1), jnp.max(fresh_scores, axis=-1))
    prefix_expo = jnp.exp(prefix_scores - highest[..., None])
    fresh_expo = jnp.exp(fresh_scores - highest[..., None])
    totals = jnp.sum(prefix_expo, axis=-1) + jnp.sum(fresh_expo, axis=-1)
    weighted = jnp.einsum(
        "scgnk,ckgd->scgnd",
        prefix_expo.astype(jnp.bfloat16),
        cache_values,
        preferred_element_type=jnp.float32,
    )
    weighted = weighted + jnp.einsum(
        "scgnt,tcgd->scgnd",
        fresh_expo.astype(jnp.bfloat16),
        fresh_values,
        preferred_element_type=jnp.float32,
    )
    return (weighted, totals)


def per_device_wide(
    queries,
    new_kv,
    prefix_kv,
    cont_prompt,
    resid,
    norm_gain,
    w_gate,
    w_up,
    w_down,
    routes,
    route_gates,
):
    step_count, own_rows, half_width = queries.shape
    prompt_count = prefix_kv.shape[0]
    local_prompt = cont_prompt - lax.axis_index("experts") * prompt_count
    weighted, totals = attend_gathered(queries, new_kv, prefix_kv, local_prompt)
    attn_out = (
        (weighted / totals[..., None])
        .astype(jnp.bfloat16)
        .reshape(step_count, own_rows, half_width)
    )
    halves = (
        lax.all_gather(resid, "heads", axis=2, tiled=True),
        lax.all_gather(attn_out, "heads", axis=2, tiled=True),
    )
    combined = halves[0].astype(jnp.float32) + halves[1].astype(jnp.float32)
    square_mean = jnp.mean(combined * combined, axis=-1, keepdims=True)
    normed = (combined * lax.rsqrt(square_mean + 1e-05) * norm_gain.astype(jnp.float32)).astype(
        jnp.bfloat16
    )
    token_count = step_count * own_rows
    flat_tokens = normed.reshape(token_count, -1)
    flat_routes = routes.reshape(token_count, -1)
    experts = lax.axis_size("experts")
    matches = flat_routes[:, :, None] == jnp.arange(experts)[None, None, :]
    gate_weights = w_gate[0]
    up_weights = w_up[0]
    wanted = jnp.transpose(jnp.any(matches, axis=1))
    outgoing = jnp.where(wanted[:, :, None], flat_tokens[None], jnp.zeros((), jnp.bfloat16))
    arrived = lax.all_to_all(outgoing, "experts", split_axis=0, concat_axis=0, tiled=True)
    segment = lax.all_gather(arrived.reshape(experts * token_count, -1), "rows", axis=0, tiled=True)
    gate = jnp.dot(segment, gate_weights, preferred_element_type=jnp.float32)
    up_part = jnp.dot(segment, up_weights, preferred_element_type=jnp.float32)
    hidden = (jax.nn.silu(gate) * up_part).astype(jnp.bfloat16)
    paired = lax.all_gather(hidden, "heads", axis=1, tiled=True)
    down_rows = w_down[0]
    segment = paired
    summed = lax.psum_scatter(
        jnp.dot(segment, down_rows, preferred_element_type=jnp.float32).astype(jnp.bfloat16),
        "rows",
        scatter_dimension=0,
        tiled=True,
    )
    result = summed.reshape(experts, token_count, -1)
    returned = lax.all_to_all(result, "experts", split_axis=0, concat_axis=0, tiled=True)
    mixing = jnp.sum(
        jnp.where(matches, route_gates.reshape(token_count, -1)[:, :, None], 0.0), axis=1
    )
    mixture = jnp.einsum("ne,end->nd", mixing, returned.astype(jnp.float32))
    moe_out = mixture.astype(jnp.bfloat16).reshape(step_count, own_rows, half_width)
    return (attn_out, moe_out)


def call(body, outs, in_spaces, name, scratch=(), limit=4 * MIB, cost=None):
    spaces = {"v": VMEM, "s": pltpu.SMEM, "a": pl.ANY}
    single = not isinstance(outs, (list, tuple))
    shapes = [outs] if single else list(outs)
    specs = [pl.BlockSpec(memory_space=VMEM) for _ in shapes]
    return pl.pallas_call(
        body,
        out_shape=shapes[0] if single else tuple(shapes),
        in_specs=[pl.BlockSpec(memory_space=spaces[s]) for s in in_spaces],
        out_specs=specs[0] if single else tuple(specs),
        scratch_shapes=list(scratch),
        compiler_params=pltpu.CompilerParams(vmem_limit_bytes=limit),
        cost_estimate=cost,
        name=name,
    )


class Plan:
    def __init__(self, queries, new_kv, prefix_kv):
        self.steps, self.conts, self.half = queries.shape
        self.kv_local = new_kv.shape[-1] // HEAD_DIM
        self.prompts, self.positions = prefix_kv.shape[:2]
        self.tokens = self.steps * self.conts
        self.block = self.prompts * self.positions * 2
        self.fresh = self.block
        self.query = self.fresh + 2 * self.tokens
        self.resid = self.query + GROUP * self.tokens
        self.prompt = self.resid + GROUP * self.tokens
        self.rows = -(-(self.prompt + self.tokens) // 16) * 16


def fetch_body(plan, *refs):
    count = (len(refs) - 2) // 2
    sources, targets, (prompts, sems) = refs[:count], refs[count : 2 * count], refs[2 * count :]
    copies = [
        pltpu.make_async_copy(source, target, sems.at[i])
        for i, (source, target) in enumerate(zip(sources, (prompts,) + targets[1:]))
    ]
    for copy in copies:
        copy.start()
    for copy in copies:
        copy.wait()
    c = plan.conts
    base = lax.axis_index("experts") * plan.prompts
    row = lax.broadcasted_iota(jnp.int32, (c, HEAD_DIM), 0)
    local = jnp.zeros((c, HEAD_DIM), jnp.float32)
    for i in range(c):
        local = jnp.where(row == i, (prompts[i] - base).astype(jnp.float32), local)
    targets[0][...] = local.astype(jnp.bfloat16)


def pack_body(plan, local_ref, q_ref, new_ref, prefix_ref, resid_ref, *outs):
    t, c = plan.tokens, plan.conts
    own = lax.axis_index("rows")
    for k, out_ref in enumerate(outs):
        h = own ^ k
        lanes = pl.ds(pl.multiple_of(h * HEAD_DIM, HEAD_DIM), HEAD_DIM)
        for p in range(plan.prompts):
            for i in range(plan.positions):
                out_ref[pl.ds((p * plan.positions + i) * 2, 2), :] = prefix_ref[p, i, :, lanes]
        for s in range(plan.steps):
            for i in range(c):
                out_ref[pl.ds(plan.fresh + (s * c + i) * 2, 2), :] = new_ref[s, i, :, lanes]
            for g in range(GROUP):
                head = pl.ds(pl.multiple_of((h * GROUP + g) * HEAD_DIM, HEAD_DIM), HEAD_DIM)
                out_ref[pl.ds(plan.query + g * t + s * c, c), :] = q_ref[s, :, head]
                out_ref[pl.ds(plan.resid + g * t + s * c, c), :] = resid_ref[s, :, head]
            out_ref[pl.ds(plan.prompt + s * c, c), :] = local_ref[...]


def attend_body(plan, rows, *refs):
    pieces, (gain_ref, x_ref, attn_ref, q_s, r_s, kv_s, p_s, gain_s) = refs[:rows], refs[rows:]
    t, c = plan.tokens, plan.conts
    total = rows * t
    f32 = jnp.float32

    def place(own):
        for k, got_ref in enumerate(pieces):
            src = own ^ k
            kv_s[pl.ds(src * plan.block, plan.block), :] = got_ref[pl.ds(0, plan.block), :]
            late = pl.ds(rows * plan.block + src * 2 * t, 2 * t)
            kv_s[late, :] = got_ref[pl.ds(plan.fresh, 2 * t), :]
            p_s[pl.ds(src * t, t), :] = got_ref[pl.ds(plan.prompt, t), :]
            for g in range(GROUP):
                q_s[pl.ds(g * total + src * t, t), :] = got_ref[pl.ds(plan.query + g * t, t), :]
                r_s[pl.ds(g * total + src * t, t), :] = got_ref[pl.ds(plan.resid + g * t, t), :]

    for own in range(rows):
        pl.when(lax.axis_index("rows") == own)(functools.partial(place, own))
    used = rows * plan.block + rows * 2 * t
    spare = kv_s.shape[0] - used
    if spare:
        kv_s[pl.ds(used, spare), :] = jnp.zeros((spare, HEAD_DIM), jnp.bfloat16)
    kv = kv_s[...]
    scores = lax.dot_general(
        q_s[...], kv, (((1,), (1,)), ((), ())), preferred_element_type=f32
    ) * HEAD_DIM ** (-0.5)
    shape = scores.shape
    row = lax.broadcasted_iota(jnp.int32, shape, 0) % total
    col = lax.broadcasted_iota(jnp.int32, shape, 1)
    prompt = p_s[...].astype(f32)[:, :1]
    prompt = jnp.concatenate([prompt] * GROUP, axis=0).astype(jnp.int32)
    in_prefix = (col < rows * plan.block) & ((col % plan.block) // (2 * plan.positions) == prompt)
    late = col - rows * plan.block
    same = (late // (2 * t) == row // t) & (((late // 2) % t) % c == row % c)
    seen = ((late // 2) % t) // c <= (row % t) // c
    in_fresh = (late >= 0) & (col < used) & same & seen
    live = (col % 2 == 0) & (in_prefix | in_fresh)
    scores = jnp.where(live, scores, -jnp.inf)
    highest = jnp.max(scores, axis=-1, keepdims=True)
    expo = jnp.exp(scores - highest)
    totals = jnp.sum(expo, axis=-1, keepdims=True)
    weights = pltpu.roll(expo, 1, 1).astype(jnp.bfloat16)
    out = jnp.dot(weights, kv, preferred_element_type=f32) / totals
    attn = out.astype(jnp.bfloat16)
    attn_ref[...] = attn
    gain_s[...] = gain_ref[...].astype(f32)
    first = (lax.axis_index("heads") * rows + lax.axis_index("rows")) * GROUP
    combined = attn.astype(f32) + r_s[...].astype(f32)
    square = jnp.zeros((total, HEAD_DIM), f32)
    for g in range(GROUP):
        part = combined[g * total : (g + 1) * total]
        square = square + part * part
        gained = part * gain_s[pl.ds(first + g, 1), :]
        x_ref[:, pl.ds(g * HEAD_DIM, HEAD_DIM)] = gained.astype(jnp.bfloat16)
    square = jnp.sum(square, axis=-1, keepdims=True)
    high = square.astype(jnp.bfloat16)
    low = (square - high.astype(f32)).astype(jnp.bfloat16)
    lane = lax.broadcasted_iota(jnp.int32, (total, HEAD_DIM), 1)
    extra = jnp.where(lane == 0, high.astype(f32), jnp.where(lane == 1, low.astype(f32), 0.0))
    x_ref[:, pl.ds(GROUP * HEAD_DIM, HEAD_DIM)] = extra.astype(jnp.bfloat16)


def to_row(column, first, lanes):
    shape = (column.shape[0], lanes)
    hit = lax.broadcasted_iota(jnp.int32, shape, 1) == lax.broadcasted_iota(jnp.int32, shape, 0) + first
    return jnp.sum(jnp.where(hit, column, 0.0), axis=0, keepdims=True)


def to_column(row, count):
    shape = (count, row.shape[1])
    hit = lax.broadcasted_iota(jnp.int32, shape, 1) == lax.broadcasted_iota(jnp.int32, shape, 0)
    return jnp.sum(jnp.where(hit, row, 0.0), axis=1, keepdims=True)


def merge_body(plan, rows, own_ref, peer_ref, attn_ref, *outs):
    t = plan.tokens
    total, width = own_ref.shape
    depth = width - HEAD_DIM
    spare = pl.ds(depth, HEAD_DIM)
    high, low = [], []
    for i, ref in enumerate((own_ref, peer_ref)):
        extra = ref[:, spare].astype(jnp.float32)
        high.append(to_row(extra[:, 0:1], i * total, HEAD_DIM))
        low.append(to_row(extra[:, 1:2], i * total, HEAD_DIM))
    row = lax.broadcasted_iota(jnp.int32, (2 * total - GROUP * t, HEAD_DIM), 0)
    squares = jnp.where(row == 0, high[0] + high[1], jnp.where(row == 1, low[0] + low[1], 0.0))
    squares = squares.astype(jnp.bfloat16)
    for out_ref in outs:
        for i, ref in enumerate((own_ref, peer_ref)):
            out_ref[pl.ds(i * total, total), pl.ds(0, depth)] = ref[:, pl.ds(0, depth)]
        out_ref[pl.ds(GROUP * t, row.shape[0]), spare] = squares

    def place(own):
        for k, out_ref in enumerate(outs):
            for g in range(GROUP):
                part = attn_ref[pl.ds(g * total + (own ^ k) * t, t), :]
                out_ref[pl.ds(g * t, t), spare] = part

    for own in range(rows):
        pl.when(lax.axis_index("rows") == own)(functools.partial(place, own))


def stack_body(*refs):
    *pieces, _, out_ref = refs
    for k, ref in enumerate(pieces):
        out_ref[k] = ref[...]


def products(side, x, weight, k, total):
    depth = x.shape[1]
    core = lax.axis_index("heads")
    core = 1 - core if side else core
    half = weight.shape[1] // 2
    first = pl.multiple_of(core * half + (lax.axis_index("rows") ^ k) * depth, depth)
    part = jnp.dot(x, weight[0, pl.ds(first, depth)], preferred_element_type=jnp.float32)
    return part if total is None else total + part


def own_chunk_body(x_ref, gate_w, up_w, gate_ref, up_ref):
    x = x_ref[:, pl.ds(0, x_ref.shape[1] - HEAD_DIM)]
    gate_ref[...] = products(0, x, gate_w, 0, None)
    up_ref[...] = products(0, x, up_w, 0, None)


def first_half_body(x_ref, gate_in, up_in, gate_w, up_w, gate_ref, up_ref):
    chunks, _, width = x_ref.shape
    gate, up = gate_in[...], up_in[...]
    for k in range(1, chunks):
        x = x_ref[k, :, pl.ds(0, width - HEAD_DIM)]
        gate = products(0, x, gate_w, k, gate)
        up = products(0, x, up_w, k, up)
    gate_ref[...] = gate
    up_ref[...] = up


def second_half_body(plan, x_ref, own_ref, gate_in, up_in, gate_w, up_w, hidden_ref):
    chunks, tokens, width = x_ref.shape
    depth = width - HEAD_DIM
    first = GROUP * plan.tokens
    square = jnp.zeros((tokens - first, HEAD_DIM), jnp.float32)
    for ref in (own_ref, x_ref):
        for k in range(chunks):
            extra = ref[k, pl.ds(first, tokens - first), pl.ds(depth, HEAD_DIM)]
            square = square + extra.astype(jnp.float32)
    square = to_column(square[0:1] + square[1:2], tokens)
    scale = lax.rsqrt(square / (2 * chunks * depth) + 1e-05)
    gate, up = gate_in[...], up_in[...]
    for k in range(chunks):
        x = x_ref[k, :, pl.ds(0, depth)]
        gate = products(1, x, gate_w, k, gate)
        up = products(1, x, up_w, k, up)
    gate = gate * scale
    up = up * scale
    hidden_ref[...] = (gate / (1.0 + jnp.exp(-gate)) * up).astype(jnp.bfloat16)


def down_product(side, hidden_ref, down_w):
    depth = hidden_ref.shape[1]
    core = lax.axis_index("heads")
    first = pl.multiple_of((1 - core if side else core) * depth, depth)
    return jnp.dot(
        hidden_ref[...], down_w[0, pl.ds(first, depth)], preferred_element_type=jnp.float32
    )


def down_first_body(hidden_ref, down_w, out_ref):
    out_ref[...] = down_product(0, hidden_ref, down_w)


def down_second_body(rows, hidden_ref, own_ref, down_w, out_ref):
    result = (own_ref[...] + down_product(1, hidden_ref, down_w)).astype(jnp.bfloat16)
    pieces, t, _ = out_ref.shape
    experts = pieces // rows
    own = lax.axis_index("experts")
    for r in range(rows):
        for e in range(experts):
            first = (e * rows + r) * t
            out_ref[r * experts + (own ^ e)] = result[first : first + t]


def mix_body(rows, routes_ref, gates_ref, got_ref, own_ref, attn_ref, moe_ref):
    pieces, t, half = got_ref.shape
    experts = pieces // rows
    steps, conts, _ = moe_ref.shape
    depth = own_ref.shape[2] - HEAD_DIM
    for k in range(rows):
        head = (lax.axis_index("rows") ^ k) * GROUP
        for g in range(GROUP):
            lanes = pl.ds(pl.multiple_of((head + g) * HEAD_DIM, HEAD_DIM), HEAD_DIM)
            for s in range(steps):
                attn_ref[s, :, lanes] = own_ref[
                    k, pl.ds(g * t + s * conts, conts), pl.ds(depth, HEAD_DIM)
                ]
    row = lax.broadcasted_iota(jnp.int32, (t, 1), 0)
    mixture = jnp.zeros((t, half), jnp.float32)
    for e in range(experts):
        summed = jnp.zeros((t, half), jnp.float32)
        for r in range(rows):
            summed = summed + got_ref[r * experts + e].astype(jnp.float32)
        share = jnp.zeros((t, 1), jnp.float32)
        for s in range(steps):
            for c in range(conts):
                amount = jnp.float32(0.0)
                for k in range(routes_ref.shape[2]):
                    amount = amount + jnp.where(routes_ref[s, c, k] == e, gates_ref[s, c, k], 0.0)
                share = jnp.where(row == s * conts + c, amount, share)
        mixture = mixture + share * summed.astype(jnp.bfloat16).astype(jnp.float32)
    mixture = mixture.astype(jnp.bfloat16)
    for s in range(steps):
        moe_ref[s] = mixture[s * conts : (s + 1) * conts]


def per_device(
    queries,
    new_kv,
    prefix_kv,
    cont_prompt,
    resid,
    norm_gain,
    w_gate,
    w_up,
    w_down,
    routes,
    route_gates,
):
    rows, experts = lax.axis_size("rows"), lax.axis_size("experts")
    plan = Plan(queries, new_kv, prefix_kv)
    bf16, f32 = jnp.bfloat16, jnp.float32
    shape = jax.ShapeDtypeStruct
    piece = GROUP * HEAD_DIM
    total = rows * plan.tokens
    tokens = experts * total

    hbm = functools.partial(pltpu.with_memory_space_constraint, memory_space=pltpu.HBM)
    vmem = functools.partial(pltpu.with_memory_space_constraint, memory_space=VMEM)
    gate_w, up_w, down_w = w_gate, w_up, w_down

    def cover(size):
        return pl.CostEstimate(flops=FLOPS * size, bytes_accessed=size, transcendentals=0)

    sources = (cont_prompt, queries, new_kv, prefix_kv, resid)
    fetched = call(
        functools.partial(fetch_body, plan),
        (VMEM((plan.conts, HEAD_DIM), bf16),)
        + tuple(VMEM(source.shape, bf16) for source in sources[1:]),
        "aaaaa",
        "fetch",
        scratch=(
            pltpu.SMEM(cont_prompt.shape, jnp.int32),
            pltpu.SemaphoreType.DMA((len(sources),)),
        ),
    )(*map(hbm, sources))
    packed = call(
        functools.partial(pack_body, plan),
        (shape((plan.rows, HEAD_DIM), bf16),) * rows,
        "vvvvv",
        "pack",
        cost=cover(PACK_COVER),
    )(*map(vmem, fetched))

    def spread(pieces):
        return [
            lax.ppermute(pieces[k], "rows", [(i, i ^ k) for i in range(rows)]) if k else pieces[0]
            for k in range(rows)
        ]

    keys = -(-(rows * (plan.block + 2 * plan.tokens)) // 128) * 128
    lanes = piece + HEAD_DIM
    x, attn = call(
        functools.partial(attend_body, plan, rows),
        (shape((total, lanes), bf16), shape((GROUP * total, HEAD_DIM), bf16)),
        "v" * (rows + 1),
        "attend",
        scratch=(
            VMEM((GROUP * total, HEAD_DIM), bf16),
            VMEM((GROUP * total, HEAD_DIM), bf16),
            VMEM((keys, HEAD_DIM), bf16),
            VMEM((total, HEAD_DIM), bf16),
            VMEM((norm_gain.size // HEAD_DIM, HEAD_DIM), f32),
        ),
        cost=cover(ATTEND_COVER),
    )(*spread(packed), norm_gain.reshape(-1, HEAD_DIM))
    swap = [(0, 1), (1, 0)]
    peer = lax.ppermute(x, "experts", swap)
    merged = call(
        functools.partial(merge_body, plan, rows),
        (shape((tokens, lanes), bf16),) * rows,
        "vvv",
        "merge",
        cost=cover(MERGE_COVER),
    )(x, peer, attn)
    chunks = spread(merged)
    units = w_gate.shape[2]
    products_of = shape((tokens, units), f32)
    gate, up = call(
        own_chunk_body,
        (products_of, products_of),
        "vvv",
        "own_chunk",
        cost=cover(OWN_COVER),
    )(merged[0], gate_w, up_w)
    own = call(stack_body, shape((rows, tokens, lanes), bf16), "v" * (rows + 1), "stack")(
        *chunks, gate
    )
    other = lax.ppermute(own, "heads", swap)
    gate, up = call(
        first_half_body,
        (products_of, products_of),
        "vvvvv",
        "first_half",
        limit=FIRST_LIMIT,
        cost=cover(FIRST_COVER),
    )(own, gate, up, gate_w, up_w)
    hidden = call(
        functools.partial(second_half_body, plan),
        shape((tokens, units), bf16),
        "vvvvvv",
        "second_half",
        limit=SECOND_LIMIT,
        cost=cover(SECOND_COVER),
    )(other, own, gate, up, gate_w, up_w)
    other_hidden = lax.ppermute(hidden, "heads", swap)
    partial = call(
        down_first_body,
        shape((tokens, plan.half), f32),
        "vv",
        "down_first",
        limit=DOWN_LIMIT,
        cost=cover(2 * plan.half * units),
    )(hidden, down_w)
    blocks = call(
        functools.partial(down_second_body, rows),
        shape((rows * experts, plan.tokens, plan.half), bf16),
        "vvv",
        "down_second",
        cost=cover(2 * plan.half * units),
    )(other_hidden, partial, down_w)
    blocks = lax.all_to_all(blocks, ("rows", "experts"), split_axis=0, concat_axis=0, tiled=True)
    out = shape(queries.shape, bf16)
    attn_out, moe_out = call(functools.partial(mix_body, rows), (out, out), "ssvv", "mix")(
        routes, route_gates, blocks, own
    )
    return (attn_out, moe_out)


def solution(mesh):
    placed = (
        P(None, ("groups", "rows", "experts"), "heads"),
        P(None, ("groups", "rows", "experts"), None, "heads"),
        P(("groups", "experts"), "rows", None, "heads"),
        P(("groups", "rows", "experts")),
        P(None, ("groups", "rows", "experts"), "heads"),
        P(),
        P("experts", None, ("rows", "heads")),
        P("experts", None, ("rows", "heads")),
        P("experts", "rows", "heads"),
        P(None, ("groups", "rows", "experts"), None),
        P(None, ("groups", "rows", "experts"), None),
    )
    sizes = mesh.shape
    by_head = (
        sizes["heads"] == 2
        and sizes["experts"] == 2
        and sizes["rows"] == 4
        and sizes["rows"] * sizes["heads"] == KV_HEADS
    )
    return jax.shard_map(
        per_device if by_head else per_device_wide,
        mesh=mesh,
        in_specs=placed,
        out_specs=(
            P(None, ("groups", "rows", "experts"), "heads"),
            P(None, ("groups", "rows", "experts"), "heads"),
        ),
        check_vma=False,
    )
```

```python
import functools

import jax
import jax.numpy as jnp
from jax import lax
from jax.experimental import pallas as pl
from jax.experimental.pallas import tpu as pltpu
from jax.sharding import PartitionSpec as P

HEADS = 48
KV_HEADS = 8
HEAD_DIM = 128
GROUP = HEADS // KV_HEADS

VMEM = pltpu.VMEM
MIB = 1 << 20
PACK_COVER = 40 * MIB
FLOPS = 1000
OWN_COVER = 40 * MIB
FIRST_COVER = 1 * MIB
SECOND_COVER = 1 * MIB
FIRST_LIMIT = 4 * MIB
SECOND_LIMIT = 4 * MIB
DOWN_LIMIT = 4 * MIB
ATTEND_COVER = MIB
MERGE_COVER = MIB


def fresh_terms(queries, new_kv):
    step_count, own_rows = (queries.shape[0], queries.shape[1])
    kv_local = new_kv.shape[-1] // HEAD_DIM
    group_size = HEADS // KV_HEADS
    grouped = queries.reshape(step_count, own_rows, kv_local, group_size, HEAD_DIM)
    fresh_keys = new_kv[:, :, 0].reshape(step_count, own_rows, kv_local, HEAD_DIM)
    fresh_values = new_kv[:, :, 1].reshape(step_count, own_rows, kv_local, HEAD_DIM)
    fresh_scores = jnp.einsum(
        "scgnd,tcgd->scgnt", grouped, fresh_keys, preferred_element_type=jnp.float32
    ) * HEAD_DIM ** (-0.5)
    future = jnp.arange(step_count)[None, :] > jnp.arange(step_count)[:, None]
    fresh_scores = jnp.where(future[:, None, None, None, :], -jnp.inf, fresh_scores)
    return (grouped, fresh_scores, fresh_values)


def attend_gathered(queries, new_kv, prefix_kv, local_prompt):
    grouped, fresh_scores, fresh_values = fresh_terms(queries, new_kv)
    own_rows = queries.shape[1]
    kv_local = new_kv.shape[-1] // HEAD_DIM
    cache = lax.all_gather(prefix_kv, "rows", axis=1, tiled=True)
    length = cache.shape[1]
    picked = jnp.take(cache, local_prompt, axis=0)
    cache_keys = picked[:, :, 0].reshape(own_rows, length, kv_local, HEAD_DIM)
    cache_values = picked[:, :, 1].reshape(own_rows, length, kv_local, HEAD_DIM)
    prefix_scores = jnp.einsum(
        "scgnd,ckgd->scgnk", grouped, cache_keys, preferred_element_type=jnp.float32
    ) * HEAD_DIM ** (-0.5)
    highest = jnp.maximum(jnp.max(prefix_scores, axis=-1), jnp.max(fresh_scores, axis=-1))
    prefix_expo = jnp.exp(prefix_scores - highest[..., None])
    fresh_expo = jnp.exp(fresh_scores - highest[..., None])
    totals = jnp.sum(prefix_expo, axis=-1) + jnp.sum(fresh_expo, axis=-1)
    weighted = jnp.einsum(
        "scgnk,ckgd->scgnd",
        prefix_expo.astype(jnp.bfloat16),
        cache_values,
        preferred_element_type=jnp.float32,
    )
    weighted = weighted + jnp.einsum(
        "scgnt,tcgd->scgnd",
        fresh_expo.astype(jnp.bfloat16),
        fresh_values,
        preferred_element_type=jnp.float32,
    )
    return (weighted, totals)


def per_device_wide(
    queries,
    new_kv,
    prefix_kv,
    cont_prompt,
    resid,
    norm_gain,
    w_gate,
    w_up,
    w_down,
    routes,
    route_gates,
):
    step_count, own_rows, half_width = queries.shape
    prompt_count = prefix_kv.shape[0]
    local_prompt = cont_prompt - lax.axis_index("experts") * prompt_count
    weighted, totals = attend_gathered(queries, new_kv, prefix_kv, local_prompt)
    attn_out = (
        (weighted / totals[..., None])
        .astype(jnp.bfloat16)
        .reshape(step_count, own_rows, half_width)
    )
    halves = (
        lax.all_gather(resid, "heads", axis=2, tiled=True),
        lax.all_gather(attn_out, "heads", axis=2, tiled=True),
    )
    combined = halves[0].astype(jnp.float32) + halves[1].astype(jnp.float32)
    square_mean = jnp.mean(combined * combined, axis=-1, keepdims=True)
    normed = (combined * lax.rsqrt(square_mean + 1e-05) * norm_gain.astype(jnp.float32)).astype(
        jnp.bfloat16
    )
    token_count = step_count * own_rows
    flat_tokens = normed.reshape(token_count, -1)
    flat_routes = routes.reshape(token_count, -1)
    experts = lax.axis_size("experts")
    matches = flat_routes[:, :, None] == jnp.arange(experts)[None, None, :]
    gate_weights = w_gate[0]
    up_weights = w_up[0]
    wanted = jnp.transpose(jnp.any(matches, axis=1))
    outgoing = jnp.where(wanted[:, :, None], flat_tokens[None], jnp.zeros((), jnp.bfloat16))
    arrived = lax.all_to_all(outgoing, "experts", split_axis=0, concat_axis=0, tiled=True)
    segment = lax.all_gather(arrived.reshape(experts * token_count, -1), "rows", axis=0, tiled=True)
    gate = jnp.dot(segment, gate_weights, preferred_element_type=jnp.float32)
    up_part = jnp.dot(segment, up_weights, preferred_element_type=jnp.float32)
    hidden = (jax.nn.silu(gate) * up_part).astype(jnp.bfloat16)
    paired = lax.all_gather(hidden, "heads", axis=1, tiled=True)
    down_rows = w_down[0]
    segment = paired
    summed = lax.psum_scatter(
        jnp.dot(segment, down_rows, preferred_element_type=jnp.float32).astype(jnp.bfloat16),
        "rows",
        scatter_dimension=0,
        tiled=True,
    )
    result = summed.reshape(experts, token_count, -1)
    returned = lax.all_to_all(result, "experts", split_axis=0, concat_axis=0, tiled=True)
    mixing = jnp.sum(
        jnp.where(matches, route_gates.reshape(token_count, -1)[:, :, None], 0.0), axis=1
    )
    mixture = jnp.einsum("ne,end->nd", mixing, returned.astype(jnp.float32))
    moe_out = mixture.astype(jnp.bfloat16).reshape(step_count, own_rows, half_width)
    return (attn_out, moe_out)


def call(body, outs, in_spaces, name, scratch=(), limit=4 * MIB, cost=None):
    spaces = {"v": VMEM, "s": pltpu.SMEM, "a": pl.ANY}
    single = not isinstance(outs, (list, tuple))
    shapes = [outs] if single else list(outs)
    specs = [pl.BlockSpec(memory_space=VMEM) for _ in shapes]
    return pl.pallas_call(
        body,
        out_shape=shapes[0] if single else tuple(shapes),
        in_specs=[pl.BlockSpec(memory_space=spaces[s]) for s in in_spaces],
        out_specs=specs[0] if single else tuple(specs),
        scratch_shapes=list(scratch),
        compiler_params=pltpu.CompilerParams(vmem_limit_bytes=limit),
        cost_estimate=cost,
        name=name,
    )


class Plan:
    def __init__(self, queries, new_kv, prefix_kv):
        self.steps, self.conts, self.half = queries.shape
        self.kv_local = new_kv.shape[-1] // HEAD_DIM
        self.prompts, self.positions = prefix_kv.shape[:2]
        self.tokens = self.steps * self.conts
        self.block = self.prompts * self.positions * 2
        self.fresh = self.block
        self.query = self.fresh + 2 * self.tokens
        self.resid = self.query + GROUP * self.tokens
        self.prompt = self.resid + GROUP * self.tokens
        self.rows = -(-(self.prompt + self.tokens) // 16) * 16


def fetch_body(plan, *refs):
    count = (len(refs) - 2) // 2
    sources, targets, (prompts, sems) = refs[:count], refs[count : 2 * count], refs[2 * count :]
    copies = [
        pltpu.make_async_copy(source, target, sems.at[i])
        for i, (source, target) in enumerate(zip(sources, (prompts,) + targets[1:]))
    ]
    for copy in copies:
        copy.start()
    for copy in copies:
        copy.wait()
    c = plan.conts
    base = lax.axis_index("experts") * plan.prompts
    row = lax.broadcasted_iota(jnp.int32, (c, HEAD_DIM), 0)
    local = jnp.zeros((c, HEAD_DIM), jnp.float32)
    for i in range(c):
        local = jnp.where(row == i, (prompts[i] - base).astype(jnp.float32), local)
    targets[0][...] = local.astype(jnp.bfloat16)


def pack_body(plan, local_ref, q_ref, new_ref, prefix_ref, resid_ref, *outs):
    t, c = plan.tokens, plan.conts
    own = lax.axis_index("rows")
    for k, out_ref in enumerate(outs):
        h = own ^ k
        lanes = pl.ds(pl.multiple_of(h * HEAD_DIM, HEAD_DIM), HEAD_DIM)
        for p in range(plan.prompts):
            for i in range(plan.positions):
                out_ref[pl.ds((p * plan.positions + i) * 2, 2), :] = prefix_ref[p, i, :, lanes]
        for s in range(plan.steps):
            for i in range(c):
                out_ref[pl.ds(plan.fresh + (s * c + i) * 2, 2), :] = new_ref[s, i, :, lanes]
            for g in range(GROUP):
                head = pl.ds(pl.multiple_of((h * GROUP + g) * HEAD_DIM, HEAD_DIM), HEAD_DIM)
                out_ref[pl.ds(plan.query + g * t + s * c, c), :] = q_ref[s, :, head]
                out_ref[pl.ds(plan.resid + g * t + s * c, c), :] = resid_ref[s, :, head]
            out_ref[pl.ds(plan.prompt + s * c, c), :] = local_ref[...]


def attend_body(plan, rows, *refs):
    pieces, (gain_ref, x_ref, attn_ref, q_s, r_s, kv_s, p_s, gain_s) = refs[:rows], refs[rows:]
    t, c = plan.tokens, plan.conts
    total = rows * t
    f32 = jnp.float32

    def place(own):
        for k, got_ref in enumerate(pieces):
            src = own ^ k
            kv_s[pl.ds(src * plan.block, plan.block), :] = got_ref[pl.ds(0, plan.block), :]
            late = pl.ds(rows * plan.block + src * 2 * t, 2 * t)
            kv_s[late, :] = got_ref[pl.ds(plan.fresh, 2 * t), :]
            p_s[pl.ds(src * t, t), :] = got_ref[pl.ds(plan.prompt, t), :]
            for g in range(GROUP):
                q_s[pl.ds(g * total + src * t, t), :] = got_ref[pl.ds(plan.query + g * t, t), :]
                r_s[pl.ds(g * total + src * t, t), :] = got_ref[pl.ds(plan.resid + g * t, t), :]

    for own in range(rows):
        pl.when(lax.axis_index("rows") == own)(functools.partial(place, own))
    used = rows * plan.block + rows * 2 * t
    spare = kv_s.shape[0] - used
    if spare:
        kv_s[pl.ds(used, spare), :] = jnp.zeros((spare, HEAD_DIM), jnp.bfloat16)
    kv = kv_s[...]
    scores = lax.dot_general(
        q_s[...], kv, (((1,), (1,)), ((), ())), preferred_element_type=f32
    ) * HEAD_DIM ** (-0.5)
    shape = scores.shape
    row = lax.broadcasted_iota(jnp.int32, shape, 0) % total
    col = lax.broadcasted_iota(jnp.int32, shape, 1)
    prompt = p_s[...].astype(f32)[:, :1]
    prompt = jnp.concatenate([prompt] * GROUP, axis=0).astype(jnp.int32)
    in_prefix = (col < rows * plan.block) & ((col % plan.block) // (2 * plan.positions) == prompt)
    late = col - rows * plan.block
    same = (late // (2 * t) == row // t) & (((late // 2) % t) % c == row % c)
    seen = ((late // 2) % t) // c <= (row % t) // c
    in_fresh = (late >= 0) & (col < used) & same & seen
    live = (col % 2 == 0) & (in_prefix | in_fresh)
    scores = jnp.where(live, scores, -jnp.inf)
    highest = jnp.max(scores, axis=-1, keepdims=True)
    expo = jnp.exp(scores - highest)
    totals = jnp.sum(expo, axis=-1, keepdims=True)
    weights = pltpu.roll(expo, 1, 1).astype(jnp.bfloat16)
    out = jnp.dot(weights, kv, preferred_element_type=f32) / totals
    attn = out.astype(jnp.bfloat16)
    attn_ref[...] = attn
    gain_s[...] = gain_ref[...].astype(f32)
    first = (lax.axis_index("heads") * rows + lax.axis_index("rows")) * GROUP
    combined = attn.astype(f32) + r_s[...].astype(f32)
    square = jnp.zeros((total, HEAD_DIM), f32)
    for g in range(GROUP):
        part = combined[g * total : (g + 1) * total]
        square = square + part * part
        gained = part * gain_s[pl.ds(first + g, 1), :]
        x_ref[:, pl.ds(g * HEAD_DIM, HEAD_DIM)] = gained.astype(jnp.bfloat16)
    square = jnp.sum(square, axis=-1, keepdims=True)
    high = square.astype(jnp.bfloat16)
    low = (square - high.astype(f32)).astype(jnp.bfloat16)
    lane = lax.broadcasted_iota(jnp.int32, (total, HEAD_DIM), 1)
    extra = jnp.where(lane == 0, high.astype(f32), jnp.where(lane == 1, low.astype(f32), 0.0))
    x_ref[:, pl.ds(GROUP * HEAD_DIM, HEAD_DIM)] = extra.astype(jnp.bfloat16)


def to_row(column, first, lanes):
    shape = (column.shape[0], lanes)
    hit = lax.broadcasted_iota(jnp.int32, shape, 1) == lax.broadcasted_iota(jnp.int32, shape, 0) + first
    return jnp.sum(jnp.where(hit, column, 0.0), axis=0, keepdims=True)


def to_column(row, count):
    shape = (count, row.shape[1])
    hit = lax.broadcasted_iota(jnp.int32, shape, 1) == lax.broadcasted_iota(jnp.int32, shape, 0)
    return jnp.sum(jnp.where(hit, row, 0.0), axis=1, keepdims=True)


def merge_body(plan, rows, own_ref, peer_ref, attn_ref, *outs):
    t = plan.tokens
    total, width = own_ref.shape
    depth = width - HEAD_DIM
    spare = pl.ds(depth, HEAD_DIM)
    high, low = [], []
    for i, ref in enumerate((own_ref, peer_ref)):
        extra = ref[:, spare].astype(jnp.float32)
        high.append(to_row(extra[:, 0:1], i * total, HEAD_DIM))
        low.append(to_row(extra[:, 1:2], i * total, HEAD_DIM))
    row = lax.broadcasted_iota(jnp.int32, (2 * total - GROUP * t, HEAD_DIM), 0)
    squares = jnp.where(row == 0, high[0] + high[1], jnp.where(row == 1, low[0] + low[1], 0.0))
    squares = squares.astype(jnp.bfloat16)
    for out_ref in outs:
        for i, ref in enumerate((own_ref, peer_ref)):
            out_ref[pl.ds(i * total, total), pl.ds(0, depth)] = ref[:, pl.ds(0, depth)]
        out_ref[pl.ds(GROUP * t, row.shape[0]), spare] = squares

    def place(own):
        for k, out_ref in enumerate(outs):
            for g in range(GROUP):
                part = attn_ref[pl.ds(g * total + (own ^ k) * t, t), :]
                out_ref[pl.ds(g * t, t), spare] = part

    for own in range(rows):
        pl.when(lax.axis_index("rows") == own)(functools.partial(place, own))


def stack_body(*refs):
    *pieces, _, out_ref = refs
    for k, ref in enumerate(pieces):
        out_ref[k] = ref[...]


def products(side, x, weight, k, total):
    depth = x.shape[1]
    core = lax.axis_index("heads")
    core = 1 - core if side else core
    half = weight.shape[1] // 2
    first = pl.multiple_of(core * half + (lax.axis_index("rows") ^ k) * depth, depth)
    part = jnp.dot(x, weight[0, pl.ds(first, depth)], preferred_element_type=jnp.float32)
    return part if total is None else total + part


def own_chunk_body(x_ref, gate_w, up_w, gate_ref, up_ref):
    x = x_ref[:, pl.ds(0, x_ref.shape[1] - HEAD_DIM)]
    gate_ref[...] = products(0, x, gate_w, 0, None)
    up_ref[...] = products(0, x, up_w, 0, None)


def first_half_body(x_ref, gate_in, up_in, gate_w, up_w, gate_ref, up_ref):
    chunks, _, width = x_ref.shape
    gate, up = gate_in[...], up_in[...]
    for k in range(1, chunks):
        x = x_ref[k, :, pl.ds(0, width - HEAD_DIM)]
        gate = products(0, x, gate_w, k, gate)
        up = products(0, x, up_w, k, up)
    gate_ref[...] = gate
    up_ref[...] = up


def second_half_body(plan, x_ref, own_ref, gate_in, up_in, gate_w, up_w, hidden_ref):
    chunks, tokens, width = x_ref.shape
    depth = width - HEAD_DIM
    first = GROUP * plan.tokens
    square = jnp.zeros((tokens - first, HEAD_DIM), jnp.float32)
    for ref in (own_ref, x_ref):
        for k in range(chunks):
            extra = ref[k, pl.ds(first, tokens - first), pl.ds(depth, HEAD_DIM)]
            square = square + extra.astype(jnp.float32)
    square = to_column(square[0:1] + square[1:2], tokens)
    scale = lax.rsqrt(square / (2 * chunks * depth) + 1e-05)
    gate, up = gate_in[...], up_in[...]
    for k in range(chunks):
        x = x_ref[k, :, pl.ds(0, depth)]
        gate = products(1, x, gate_w, k, gate)
        up = products(1, x, up_w, k, up)
    gate = gate * scale
    up = up * scale
    hidden_ref[...] = (gate / (1.0 + jnp.exp(-gate)) * up).astype(jnp.bfloat16)


def down_product(side, hidden_ref, down_w):
    depth = hidden_ref.shape[1]
    core = lax.axis_index("heads")
    first = pl.multiple_of((1 - core if side else core) * depth, depth)
    return jnp.dot(
        hidden_ref[...], down_w[0, pl.ds(first, depth)], preferred_element_type=jnp.float32
    )


def down_first_body(hidden_ref, down_w, out_ref):
    out_ref[...] = down_product(0, hidden_ref, down_w)


def down_second_body(plan, rows, hidden_ref, own_ref, down_w, *outs):
    result = own_ref[...] + down_product(1, hidden_ref, down_w)
    t = plan.tokens
    total = rows * t

    def place(own):
        for k, out_ref in enumerate(outs):
            first = (own ^ k) * t
            pair = [result[i : i + t] for i in (first, first + total)]
            out_ref[...] = jnp.concatenate(pair, axis=0).astype(jnp.bfloat16)

    for own in range(rows):
        pl.when(lax.axis_index("rows") == own)(functools.partial(place, own))


def sum_body(*refs):
    *pieces, own_ref, peer_ref = refs
    total = pieces[0][...].astype(jnp.float32)
    for ref in pieces[1:]:
        total = total + ref[...].astype(jnp.float32)
    t = own_ref.shape[0]
    own_ref[...] = total[:t].astype(jnp.bfloat16)
    peer_ref[...] = total[t:].astype(jnp.bfloat16)


def attn_body(plan, rows, own_ref, _, attn_ref):
    t = plan.tokens
    depth = own_ref.shape[2] - HEAD_DIM
    for k in range(rows):
        head = (lax.axis_index("rows") ^ k) * GROUP
        for g in range(GROUP):
            lanes = pl.ds(pl.multiple_of((head + g) * HEAD_DIM, HEAD_DIM), HEAD_DIM)
            for s in range(plan.steps):
                attn_ref[s, :, lanes] = own_ref[
                    k, pl.ds(g * t + s * plan.conts, plan.conts), pl.ds(depth, HEAD_DIM)
                ]


def mix_body(plan, routes_ref, gates_ref, own_ref, peer_ref, moe_ref):
    own = lax.axis_index("experts")
    row = lax.broadcasted_iota(jnp.int32, (plan.tokens, 1), 0)
    mixture = None
    for expert, ref in ((own, own_ref), (1 - own, peer_ref)):
        share = jnp.zeros((plan.tokens, 1), jnp.float32)
        for s in range(plan.steps):
            for c in range(plan.conts):
                amount = jnp.float32(0.0)
                for k in range(routes_ref.shape[2]):
                    chosen = routes_ref[s, c, k] == expert
                    amount = amount + jnp.where(chosen, gates_ref[s, c, k], 0.0)
                share = jnp.where(row == s * plan.conts + c, amount, share)
        part = share * ref[...].astype(jnp.float32)
        mixture = part if mixture is None else mixture + part
    mixture = mixture.astype(jnp.bfloat16)
    for s in range(plan.steps):
        moe_ref[s] = mixture[s * plan.conts : (s + 1) * plan.conts]


def per_device(
    queries,
    new_kv,
    prefix_kv,
    cont_prompt,
    resid,
    norm_gain,
    w_gate,
    w_up,
    w_down,
    routes,
    route_gates,
):
    rows, experts = lax.axis_size("rows"), lax.axis_size("experts")
    plan = Plan(queries, new_kv, prefix_kv)
    bf16, f32 = jnp.bfloat16, jnp.float32
    shape = jax.ShapeDtypeStruct
    piece = GROUP * HEAD_DIM
    total = rows * plan.tokens
    tokens = experts * total

    hbm = functools.partial(pltpu.with_memory_space_constraint, memory_space=pltpu.HBM)
    vmem = functools.partial(pltpu.with_memory_space_constraint, memory_space=VMEM)
    gate_w, up_w, down_w = w_gate, w_up, w_down

    def cover(size):
        return pl.CostEstimate(flops=FLOPS * size, bytes_accessed=size, transcendentals=0)

    sources = (cont_prompt, queries, new_kv, prefix_kv, resid)
    fetched = call(
        functools.partial(fetch_body, plan),
        (VMEM((plan.conts, HEAD_DIM), bf16),)
        + tuple(VMEM(source.shape, bf16) for source in sources[1:]),
        "aaaaa",
        "fetch",
        scratch=(
            pltpu.SMEM(cont_prompt.shape, jnp.int32),
            pltpu.SemaphoreType.DMA((len(sources),)),
        ),
    )(*map(hbm, sources))
    packed = call(
        functools.partial(pack_body, plan),
        (shape((plan.rows, HEAD_DIM), bf16),) * rows,
        "vvvvv",
        "pack",
        cost=cover(PACK_COVER),
    )(*map(vmem, fetched))

    def spread(pieces):
        return [
            lax.ppermute(pieces[k], "rows", [(i, i ^ k) for i in range(rows)]) if k else pieces[0]
            for k in range(rows)
        ]

    keys = -(-(rows * (plan.block + 2 * plan.tokens)) // 128) * 128
    lanes = piece + HEAD_DIM
    x, attn = call(
        functools.partial(attend_body, plan, rows),
        (shape((total, lanes), bf16), shape((GROUP * total, HEAD_DIM), bf16)),
        "v" * (rows + 1),
        "attend",
        scratch=(
            VMEM((GROUP * total, HEAD_DIM), bf16),
            VMEM((GROUP * total, HEAD_DIM), bf16),
            VMEM((keys, HEAD_DIM), bf16),
            VMEM((total, HEAD_DIM), bf16),
            VMEM((norm_gain.size // HEAD_DIM, HEAD_DIM), f32),
        ),
        cost=cover(ATTEND_COVER),
    )(*spread(packed), norm_gain.reshape(-1, HEAD_DIM))
    swap = [(0, 1), (1, 0)]
    peer = lax.ppermute(x, "experts", swap)
    merged = call(
        functools.partial(merge_body, plan, rows),
        (shape((tokens, lanes), bf16),) * rows,
        "vvv",
        "merge",
        cost=cover(MERGE_COVER),
    )(x, peer, attn)
    chunks = spread(merged)
    units = w_gate.shape[2]
    products_of = shape((tokens, units), f32)
    gate, up = call(
        own_chunk_body,
        (products_of, products_of),
        "vvv",
        "own_chunk",
        cost=cover(OWN_COVER),
    )(merged[0], gate_w, up_w)
    own = call(stack_body, shape((rows, tokens, lanes), bf16), "v" * (rows + 1), "stack")(
        *chunks, gate
    )
    other = lax.ppermute(own, "heads", swap)
    gate, up = call(
        first_half_body,
        (products_of, products_of),
        "vvvvv",
        "first_half",
        limit=FIRST_LIMIT,
        cost=cover(FIRST_COVER),
    )(own, gate, up, gate_w, up_w)
    hidden = call(
        functools.partial(second_half_body, plan),
        shape((tokens, units), bf16),
        "vvvvvv",
        "second_half",
        limit=SECOND_LIMIT,
        cost=cover(SECOND_COVER),
    )(other, own, gate, up, gate_w, up_w)
    other_hidden = lax.ppermute(hidden, "heads", swap)
    partial = call(
        down_first_body,
        shape((tokens, plan.half), f32),
        "vv",
        "down_first",
        limit=DOWN_LIMIT,
        cost=cover(2 * plan.half * units),
    )(hidden, down_w)
    blocks = call(
        functools.partial(down_second_body, plan, rows),
        (shape((experts * plan.tokens, plan.half), bf16),) * rows,
        "vvv",
        "down_second",
        cost=cover(2 * plan.half * units),
    )(other_hidden, partial, down_w)
    output = shape((plan.tokens, plan.half), bf16)
    mine, theirs = call(sum_body, (output, output), "v" * rows, "sum")(*spread(blocks))
    returned = lax.ppermute(theirs, "experts", swap)
    out = shape(queries.shape, bf16)
    attn_out = call(functools.partial(attn_body, plan, rows), out, "vv", "attn")(own, theirs)
    moe_out = call(functools.partial(mix_body, plan), out, "ssvv", "mix")(
        routes, route_gates, mine, returned
    )
    return (attn_out, moe_out)


def solution(mesh):
    placed = (
        P(None, ("groups", "rows", "experts"), "heads"),
        P(None, ("groups", "rows", "experts"), None, "heads"),
        P(("groups", "experts"), "rows", None, "heads"),
        P(("groups", "rows", "experts")),
        P(None, ("groups", "rows", "experts"), "heads"),
        P(),
        P("experts", None, ("rows", "heads")),
        P("experts", None, ("rows", "heads")),
        P("experts", "rows", "heads"),
        P(None, ("groups", "rows", "experts"), None),
        P(None, ("groups", "rows", "experts"), None),
    )
    sizes = mesh.shape
    by_head = (
        sizes["heads"] == 2
        and sizes["experts"] == 2
        and sizes["rows"] == 4
        and sizes["rows"] * sizes["heads"] == KV_HEADS
    )
    return jax.shard_map(
        per_device if by_head else per_device_wide,
        mesh=mesh,
        in_specs=placed,
        out_specs=(
            P(None, ("groups", "rows", "experts"), "heads"),
            P(None, ("groups", "rows", "experts"), "heads"),
        ),
        check_vma=False,
    )
```

```python
import functools

import jax
import jax.numpy as jnp
from jax import lax
from jax.experimental import pallas as pl
from jax.experimental.pallas import tpu as pltpu
from jax.sharding import PartitionSpec as P


HEADS = 48
KV_HEADS = 8
HEAD_DIM = 128
GROUP = HEADS // KV_HEADS

VMEM = pltpu.VMEM
MIB = 1 << 20
PACK_COVER = 40 * MIB
FLOPS = 1000
OWN_COVER = 40 * MIB
FIRST_COVER = 1 * MIB
SECOND_COVER = 1 * MIB
FIRST_LIMIT = 4 * MIB
SECOND_LIMIT = 4 * MIB
DOWN_LIMIT = 4 * MIB
DOWN_COVER = MIB // 8
ATTEND_COVER = MIB
MERGE_COVER = MIB


def fresh_terms(queries, new_kv):
    step_count, own_rows = (queries.shape[0], queries.shape[1])
    kv_local = new_kv.shape[-1] // HEAD_DIM
    group_size = HEADS // KV_HEADS
    grouped = queries.reshape(step_count, own_rows, kv_local, group_size, HEAD_DIM)
    fresh_keys = new_kv[:, :, 0].reshape(step_count, own_rows, kv_local, HEAD_DIM)
    fresh_values = new_kv[:, :, 1].reshape(step_count, own_rows, kv_local, HEAD_DIM)
    fresh_scores = jnp.einsum(
        "scgnd,tcgd->scgnt", grouped, fresh_keys, preferred_element_type=jnp.float32
    ) * HEAD_DIM ** (-0.5)
    future = jnp.arange(step_count)[None, :] > jnp.arange(step_count)[:, None]
    fresh_scores = jnp.where(future[:, None, None, None, :], -jnp.inf, fresh_scores)
    return (grouped, fresh_scores, fresh_values)


def attend_gathered(queries, new_kv, prefix_kv, local_prompt):
    grouped, fresh_scores, fresh_values = fresh_terms(queries, new_kv)
    own_rows = queries.shape[1]
    kv_local = new_kv.shape[-1] // HEAD_DIM
    cache = lax.all_gather(prefix_kv, "rows", axis=1, tiled=True)
    length = cache.shape[1]
    picked = jnp.take(cache, local_prompt, axis=0)
    cache_keys = picked[:, :, 0].reshape(own_rows, length, kv_local, HEAD_DIM)
    cache_values = picked[:, :, 1].reshape(own_rows, length, kv_local, HEAD_DIM)
    prefix_scores = jnp.einsum(
        "scgnd,ckgd->scgnk", grouped, cache_keys, preferred_element_type=jnp.float32
    ) * HEAD_DIM ** (-0.5)
    highest = jnp.maximum(jnp.max(prefix_scores, axis=-1), jnp.max(fresh_scores, axis=-1))
    prefix_expo = jnp.exp(prefix_scores - highest[..., None])
    fresh_expo = jnp.exp(fresh_scores - highest[..., None])
    totals = jnp.sum(prefix_expo, axis=-1) + jnp.sum(fresh_expo, axis=-1)
    weighted = jnp.einsum(
        "scgnk,ckgd->scgnd",
        prefix_expo.astype(jnp.bfloat16),
        cache_values,
        preferred_element_type=jnp.float32,
    )
    weighted = weighted + jnp.einsum(
        "scgnt,tcgd->scgnd",
        fresh_expo.astype(jnp.bfloat16),
        fresh_values,
        preferred_element_type=jnp.float32,
    )
    return (weighted, totals)


def per_device_wide(
    queries,
    new_kv,
    prefix_kv,
    cont_prompt,
    resid,
    norm_gain,
    w_gate,
    w_up,
    w_down,
    routes,
    route_gates,
):
    step_count, own_rows, half_width = queries.shape
    prompt_count = prefix_kv.shape[0]
    local_prompt = cont_prompt - lax.axis_index("experts") * prompt_count
    weighted, totals = attend_gathered(queries, new_kv, prefix_kv, local_prompt)
    attn_out = (
        (weighted / totals[..., None])
        .astype(jnp.bfloat16)
        .reshape(step_count, own_rows, half_width)
    )
    halves = (
        lax.all_gather(resid, "heads", axis=2, tiled=True),
        lax.all_gather(attn_out, "heads", axis=2, tiled=True),
    )
    combined = halves[0].astype(jnp.float32) + halves[1].astype(jnp.float32)
    square_mean = jnp.mean(combined * combined, axis=-1, keepdims=True)
    normed = (combined * lax.rsqrt(square_mean + 1e-05) * norm_gain.astype(jnp.float32)).astype(
        jnp.bfloat16
    )
    token_count = step_count * own_rows
    flat_tokens = normed.reshape(token_count, -1)
    flat_routes = routes.reshape(token_count, -1)
    experts = lax.axis_size("experts")
    matches = flat_routes[:, :, None] == jnp.arange(experts)[None, None, :]
    gate_weights = w_gate[0]
    up_weights = w_up[0]
    wanted = jnp.transpose(jnp.any(matches, axis=1))
    outgoing = jnp.where(wanted[:, :, None], flat_tokens[None], jnp.zeros((), jnp.bfloat16))
    arrived = lax.all_to_all(outgoing, "experts", split_axis=0, concat_axis=0, tiled=True)
    segment = lax.all_gather(arrived.reshape(experts * token_count, -1), "rows", axis=0, tiled=True)
    gate = jnp.dot(segment, gate_weights, preferred_element_type=jnp.float32)
    up_part = jnp.dot(segment, up_weights, preferred_element_type=jnp.float32)
    hidden = (jax.nn.silu(gate) * up_part).astype(jnp.bfloat16)
    paired = lax.all_gather(hidden, "heads", axis=1, tiled=True)
    down_rows = w_down[0]
    segment = paired
    summed = lax.psum_scatter(
        jnp.dot(segment, down_rows, preferred_element_type=jnp.float32).astype(jnp.bfloat16),
        "rows",
        scatter_dimension=0,
        tiled=True,
    )
    result = summed.reshape(experts, token_count, -1)
    returned = lax.all_to_all(result, "experts", split_axis=0, concat_axis=0, tiled=True)
    mixing = jnp.sum(
        jnp.where(matches, route_gates.reshape(token_count, -1)[:, :, None], 0.0), axis=1
    )
    mixture = jnp.einsum("ne,end->nd", mixing, returned.astype(jnp.float32))
    moe_out = mixture.astype(jnp.bfloat16).reshape(step_count, own_rows, half_width)
    return (attn_out, moe_out)


def call(body, outs, in_spaces, scratch=(), limit=4 * MIB, cost=None):
    spaces = {"v": VMEM, "s": pltpu.SMEM, "a": pl.ANY}
    single = not isinstance(outs, (list, tuple))
    shapes = [outs] if single else list(outs)
    specs = [pl.BlockSpec(memory_space=VMEM) for _ in shapes]
    return pl.pallas_call(
        body,
        out_shape=shapes[0] if single else tuple(shapes),
        in_specs=[pl.BlockSpec(memory_space=spaces[s]) for s in in_spaces],
        out_specs=specs[0] if single else tuple(specs),
        scratch_shapes=list(scratch),
        compiler_params=pltpu.CompilerParams(vmem_limit_bytes=limit),
        cost_estimate=cost,
    )


class Plan:
    def __init__(self, queries, prefix_kv):
        self.steps, self.conts, self.half = queries.shape
        self.prompts, self.positions = prefix_kv.shape[:2]
        self.tokens = self.steps * self.conts
        self.block = self.prompts * self.positions * 2
        self.fresh = self.block
        self.query = self.fresh + 2 * self.tokens
        self.resid = self.query + GROUP * self.tokens
        self.prompt = self.resid + GROUP * self.tokens
        self.rows = -(-(self.prompt + self.tokens) // 16) * 16


def fetch_body(plan, experts, *refs):
    f32, bf16 = jnp.float32, jnp.bfloat16
    sources, targets, scalars, sems = refs[:7], refs[7:12], refs[12:15], refs[15]
    copies = [
        pltpu.make_async_copy(source, target, sems.at[i])
        for i, (source, target) in enumerate(zip(sources, scalars + targets[1:]))
    ]
    for copy in copies:
        copy.start()
    for copy in copies:
        copy.wait()
    prompts, routes, gates = scalars
    base = lax.axis_index("experts") * plan.prompts
    shape = (plan.tokens, HEAD_DIM)
    row = lax.broadcasted_iota(jnp.int32, shape, 0)
    lane = lax.broadcasted_iota(jnp.int32, shape, 1)
    value = jnp.zeros(shape, f32)
    for s in range(plan.steps):
        for c in range(plan.conts):
            here = row == s * plan.conts + c
            value = jnp.where(here & (lane == 0), (prompts[c] - base).astype(f32), value)
            for e in range(experts):
                amount = f32(0.0)
                for k in range(routes.shape[2]):
                    amount = amount + jnp.where(routes[s, c, k] == e, gates[s, c, k], 0.0)
                value = jnp.where(here & ((lane + 2) // 3 == e + 1), amount, value)
    high = value.astype(bf16).astype(f32)
    middle = (value - high).astype(bf16).astype(f32)
    low = value - high - middle
    which = (lane + 2) % 3
    parts = jnp.where(lane == 0, high, jnp.where(which == 0, high, jnp.where(which == 1, middle, low)))
    targets[0][...] = parts.astype(bf16)


def pack_body(plan, local_ref, q_ref, new_ref, prefix_ref, resid_ref, *outs):
    t, c = plan.tokens, plan.conts
    own = lax.axis_index("rows")
    for k, out_ref in enumerate(outs):
        h = own ^ k
        lanes = pl.ds(pl.multiple_of(h * HEAD_DIM, HEAD_DIM), HEAD_DIM)
        for p in range(plan.prompts):
            for i in range(plan.positions):
                out_ref[pl.ds((p * plan.positions + i) * 2, 2), :] = prefix_ref[p, i, :, lanes]
        for s in range(plan.steps):
            for i in range(c):
                out_ref[pl.ds(plan.fresh + (s * c + i) * 2, 2), :] = new_ref[s, i, :, lanes]
            for g in range(GROUP):
                head = pl.ds(pl.multiple_of((h * GROUP + g) * HEAD_DIM, HEAD_DIM), HEAD_DIM)
                out_ref[pl.ds(plan.query + g * t + s * c, c), :] = q_ref[s, :, head]
                out_ref[pl.ds(plan.resid + g * t + s * c, c), :] = resid_ref[s, :, head]
        out_ref[pl.ds(plan.prompt, t), :] = local_ref[...]


def attend_body(plan, rows, *refs):
    pieces = refs[:rows]
    gain_ref, x_ref, attn_ref, share_ref, q_s, r_s, kv_s, p_s, gain_s = refs[rows:]
    t, c = plan.tokens, plan.conts
    total = rows * t
    f32 = jnp.float32

    def place(own):
        for k, got_ref in enumerate(pieces):
            src = own ^ k
            kv_s[pl.ds(src * plan.block, plan.block), :] = got_ref[pl.ds(0, plan.block), :]
            late = pl.ds(rows * plan.block + src * 2 * t, 2 * t)
            kv_s[late, :] = got_ref[pl.ds(plan.fresh, 2 * t), :]
            p_s[pl.ds(src * t, t), :] = got_ref[pl.ds(plan.prompt, t), :]
            for g in range(GROUP):
                q_s[pl.ds(g * total + src * t, t), :] = got_ref[pl.ds(plan.query + g * t, t), :]
                r_s[pl.ds(g * total + src * t, t), :] = got_ref[pl.ds(plan.resid + g * t, t), :]

    for own in range(rows):
        pl.when(lax.axis_index("rows") == own)(functools.partial(place, own))
    used = rows * plan.block + rows * 2 * t
    spare = kv_s.shape[0] - used
    if spare:
        kv_s[pl.ds(used, spare), :] = jnp.zeros((spare, HEAD_DIM), jnp.bfloat16)
    kv = kv_s[...]
    scores = lax.dot_general(
        q_s[...], kv, (((1,), (1,)), ((), ())), preferred_element_type=f32
    ) * HEAD_DIM ** (-0.5)
    shape = scores.shape
    row = lax.broadcasted_iota(jnp.int32, shape, 0) % total
    col = lax.broadcasted_iota(jnp.int32, shape, 1)
    local = p_s[...].astype(f32)
    lane = lax.broadcasted_iota(jnp.int32, local.shape, 1)
    expert = lax.axis_index("experts")
    for i in range(share_ref.shape[0]):
        part = jnp.where((lane > 0) & ((lane + 2) // 3 == (expert ^ i) + 1), local, 0.0)
        share_ref[i] = jnp.broadcast_to(jnp.sum(part, axis=1, keepdims=True), local.shape)
    prompt = local[:, :1]
    prompt = jnp.concatenate([prompt] * GROUP, axis=0).astype(jnp.int32)
    in_prefix = (col < rows * plan.block) & ((col % plan.block) // (2 * plan.positions) == prompt)
    late = col - rows * plan.block
    same = (late // (2 * t) == row // t) & (((late // 2) % t) % c == row % c)
    seen = ((late // 2) % t) // c <= (row % t) // c
    in_fresh = (late >= 0) & (col < used) & same & seen
    live = (col % 2 == 0) & (in_prefix | in_fresh)
    scores = jnp.where(live, scores, -jnp.inf)
    highest = jnp.max(scores, axis=-1, keepdims=True)
    expo = jnp.exp(scores - highest)
    totals = jnp.sum(expo, axis=-1, keepdims=True)
    weights = pltpu.roll(expo, 1, 1).astype(jnp.bfloat16)
    out = jnp.dot(weights, kv, preferred_element_type=f32) / totals
    attn = out.astype(jnp.bfloat16)
    attn_ref[...] = attn
    gain_s[...] = gain_ref[...].astype(f32)
    first = (lax.axis_index("heads") * rows + lax.axis_index("rows")) * GROUP
    combined = attn.astype(f32) + r_s[...].astype(f32)
    square = jnp.zeros((total, HEAD_DIM), f32)
    for g in range(GROUP):
        part = combined[g * total : (g + 1) * total]
        square = square + part * part
        gained = part * gain_s[pl.ds(first + g, 1), :]
        x_ref[:, pl.ds(g * HEAD_DIM, HEAD_DIM)] = gained.astype(jnp.bfloat16)
    square = jnp.sum(square, axis=-1, keepdims=True)
    high = square.astype(jnp.bfloat16)
    low = (square - high.astype(f32)).astype(jnp.bfloat16)
    lane = lax.broadcasted_iota(jnp.int32, (total, HEAD_DIM), 1)
    extra = jnp.where(lane == 0, high.astype(f32), jnp.where(lane == 1, low.astype(f32), 0.0))
    x_ref[:, pl.ds(GROUP * HEAD_DIM, HEAD_DIM)] = extra.astype(jnp.bfloat16)


def to_row(column, first, lanes):
    shape = (column.shape[0], lanes)
    hit = lax.broadcasted_iota(jnp.int32, shape, 1) == lax.broadcasted_iota(jnp.int32, shape, 0) + first
    return jnp.sum(jnp.where(hit, column, 0.0), axis=0, keepdims=True)


def to_column(row, count):
    shape = (count, row.shape[1])
    hit = lax.broadcasted_iota(jnp.int32, shape, 1) == lax.broadcasted_iota(jnp.int32, shape, 0)
    return jnp.sum(jnp.where(hit, row, 0.0), axis=1, keepdims=True)


def merge_body(plan, rows, own_ref, peer_ref, attn_ref, *outs):
    t = plan.tokens
    total, width = own_ref.shape
    depth = width - HEAD_DIM
    spare = pl.ds(depth, HEAD_DIM)
    high, low = [], []
    for i, ref in enumerate((own_ref, peer_ref)):
        extra = ref[:, spare].astype(jnp.float32)
        high.append(to_row(extra[:, 0:1], i * total, HEAD_DIM))
        low.append(to_row(extra[:, 1:2], i * total, HEAD_DIM))
    row = lax.broadcasted_iota(jnp.int32, (2 * total - GROUP * t, HEAD_DIM), 0)
    squares = jnp.where(row == 0, high[0] + high[1], jnp.where(row == 1, low[0] + low[1], 0.0))
    squares = squares.astype(jnp.bfloat16)
    for out_ref in outs:
        for i, ref in enumerate((own_ref, peer_ref)):
            out_ref[pl.ds(i * total, total), pl.ds(0, depth)] = ref[:, pl.ds(0, depth)]
        out_ref[pl.ds(GROUP * t, row.shape[0]), spare] = squares

    def place(own):
        for k, out_ref in enumerate(outs):
            for g in range(GROUP):
                part = attn_ref[pl.ds(g * total + (own ^ k) * t, t), :]
                out_ref[pl.ds(g * t, t), spare] = part

    for own in range(rows):
        pl.when(lax.axis_index("rows") == own)(functools.partial(place, own))


def stack_body(*refs):
    *pieces, _, out_ref = refs
    for k, ref in enumerate(pieces):
        out_ref[k] = ref[...]


def products(side, x, weight, k, total):
    depth = x.shape[1]
    core = lax.axis_index("heads")
    core = 1 - core if side else core
    half = weight.shape[1] // 2
    first = pl.multiple_of(core * half + (lax.axis_index("rows") ^ k) * depth, depth)
    part = jnp.dot(x, weight[0, pl.ds(first, depth)], preferred_element_type=jnp.float32)
    return part if total is None else total + part


def own_chunk_body(x_ref, gate_w, up_w, gate_ref, up_ref):
    x = x_ref[:, pl.ds(0, x_ref.shape[1] - HEAD_DIM)]
    gate_ref[...] = products(0, x, gate_w, 0, None)
    up_ref[...] = products(0, x, up_w, 0, None)


def first_half_body(x_ref, gate_in, up_in, gate_w, up_w, gate_ref, up_ref):
    chunks, _, width = x_ref.shape
    gate, up = gate_in[...], up_in[...]
    for k in range(1, chunks):
        x = x_ref[k, :, pl.ds(0, width - HEAD_DIM)]
        gate = products(0, x, gate_w, k, gate)
        up = products(0, x, up_w, k, up)
    gate_ref[...] = gate
    up_ref[...] = up


def second_half_body(plan, x_ref, own_ref, gate_in, up_in, gate_w, up_w, hidden_ref):
    chunks, tokens, width = x_ref.shape
    depth = width - HEAD_DIM
    first = GROUP * plan.tokens
    square = jnp.zeros((tokens - first, HEAD_DIM), jnp.float32)
    for ref in (own_ref, x_ref):
        for k in range(chunks):
            extra = ref[k, pl.ds(first, tokens - first), pl.ds(depth, HEAD_DIM)]
            square = square + extra.astype(jnp.float32)
    square = to_column(square[0:1] + square[1:2], tokens)
    scale = lax.rsqrt(square / (2 * chunks * depth) + 1e-05)
    gate, up = gate_in[...], up_in[...]
    for k in range(chunks):
        x = x_ref[k, :, pl.ds(0, depth)]
        gate = products(1, x, gate_w, k, gate)
        up = products(1, x, up_w, k, up)
    gate = gate * scale
    up = up * scale
    hidden_ref[...] = (gate / (1.0 + jnp.exp(-gate)) * up).astype(jnp.bfloat16)


def down_product(side, hidden_ref, down_w, lanes):
    depth = hidden_ref.shape[1]
    core = lax.axis_index("heads")
    first = pl.multiple_of((1 - core if side else core) * depth, depth)
    return jnp.dot(
        hidden_ref[...], down_w[0, pl.ds(first, depth), lanes], preferred_element_type=jnp.float32
    )


def down_first_body(hidden_ref, down_w, out_ref):
    out_ref[...] = down_product(0, hidden_ref, down_w, slice(None))


def down_second_body(part, hidden_ref, first_ref, down_w, _, own_ref, peer_ref):
    total, width = own_ref.shape
    lanes = pl.ds(part * width, width)
    result = first_ref[:, lanes] + down_product(1, hidden_ref, down_w, lanes)
    own_ref[...] = result[:total]
    peer_ref[...] = result[total:].astype(jnp.bfloat16)


def blend_body(plan, rows, share_ref, *refs):
    parts = (len(refs) - rows) // 2
    owns, peers, outs = refs[:parts], refs[parts : 2 * parts], refs[2 * parts :]
    t = plan.tokens
    own_share, peer_share = share_ref[0][:, :1], share_ref[1][:, :1]
    mixed = [
        own_share * own_ref[...] + peer_share * peer_ref[...].astype(jnp.float32)
        for own_ref, peer_ref in zip(owns, peers)
    ]
    width = mixed[0].shape[1]

    def place(own):
        for k, out_ref in enumerate(outs):
            first = (own ^ k) * t
            for i, part in enumerate(mixed):
                out_ref[:, pl.ds(i * width, width)] = part[first : first + t].astype(jnp.bfloat16)

    for own in range(rows):
        pl.when(lax.axis_index("rows") == own)(functools.partial(place, own))


def total_body(plan, *refs):
    *pieces, moe_ref = refs
    total = pieces[0][...].astype(jnp.float32)
    for ref in pieces[1:]:
        total = total + ref[...].astype(jnp.float32)
    total = total.astype(jnp.bfloat16)
    for s in range(plan.steps):
        moe_ref[s] = total[s * plan.conts : (s + 1) * plan.conts]


def attn_body(plan, rows, own_ref, _, attn_ref):
    t = plan.tokens
    depth = own_ref.shape[2] - HEAD_DIM
    for k in range(rows):
        head = (lax.axis_index("rows") ^ k) * GROUP
        for g in range(GROUP):
            lanes = pl.ds(pl.multiple_of((head + g) * HEAD_DIM, HEAD_DIM), HEAD_DIM)
            for s in range(plan.steps):
                attn_ref[s, :, lanes] = own_ref[
                    k, pl.ds(g * t + s * plan.conts, plan.conts), pl.ds(depth, HEAD_DIM)
                ]


def per_device(
    queries,
    new_kv,
    prefix_kv,
    cont_prompt,
    resid,
    norm_gain,
    w_gate,
    w_up,
    w_down,
    routes,
    route_gates,
):
    rows, experts = lax.axis_size("rows"), lax.axis_size("experts")
    plan = Plan(queries, prefix_kv)
    bf16, f32 = jnp.bfloat16, jnp.float32
    shape = jax.ShapeDtypeStruct
    piece = GROUP * HEAD_DIM
    total = rows * plan.tokens
    tokens = experts * total

    hbm = functools.partial(pltpu.with_memory_space_constraint, memory_space=pltpu.HBM)
    vmem = functools.partial(pltpu.with_memory_space_constraint, memory_space=VMEM)
    gate_w, up_w, down_w = w_gate, w_up, w_down

    def cover(size):
        return pl.CostEstimate(flops=FLOPS * size, bytes_accessed=size, transcendentals=0)

    scalars = (cont_prompt, routes, route_gates)
    arrays = (queries, new_kv, prefix_kv, resid)
    fetched = call(
        functools.partial(fetch_body, plan, experts),
        (VMEM((plan.tokens, HEAD_DIM), bf16),) + tuple(VMEM(a.shape, bf16) for a in arrays),
        "a" * (len(scalars) + len(arrays)),
        scratch=tuple(pltpu.SMEM(a.shape, a.dtype) for a in scalars)
        + (pltpu.SemaphoreType.DMA((len(scalars) + len(arrays),)),),
    )(*map(hbm, scalars + arrays))
    packed = call(
        functools.partial(pack_body, plan),
        (shape((plan.rows, HEAD_DIM), bf16),) * rows,
        "vvvvv",
        cost=cover(PACK_COVER),
    )(*map(vmem, fetched))

    def spread(pieces):
        return [
            lax.ppermute(pieces[k], "rows", [(i, i ^ k) for i in range(rows)]) if k else pieces[0]
            for k in range(rows)
        ]

    keys = -(-(rows * (plan.block + 2 * plan.tokens)) // 128) * 128
    lanes = piece + HEAD_DIM
    x, attn, share = call(
        functools.partial(attend_body, plan, rows),
        (
            shape((total, lanes), bf16),
            shape((GROUP * total, HEAD_DIM), bf16),
            shape((experts, total, HEAD_DIM), f32),
        ),
        "v" * (rows + 1),
        scratch=(
            VMEM((GROUP * total, HEAD_DIM), bf16),
            VMEM((GROUP * total, HEAD_DIM), bf16),
            VMEM((keys, HEAD_DIM), bf16),
            VMEM((total, HEAD_DIM), bf16),
            VMEM((norm_gain.size // HEAD_DIM, HEAD_DIM), f32),
        ),
        cost=cover(ATTEND_COVER),
    )(*spread(packed), norm_gain.reshape(-1, HEAD_DIM))
    swap = [(0, 1), (1, 0)]
    peer = lax.ppermute(x, "experts", swap)
    merged = call(
        functools.partial(merge_body, plan, rows),
        (shape((tokens, lanes), bf16),) * rows,
        "vvv",
        cost=cover(MERGE_COVER),
    )(x, peer, attn)
    chunks = spread(merged)
    units = w_gate.shape[2]
    products_of = shape((tokens, units), f32)
    gate, up = call(
        own_chunk_body, (products_of, products_of), "vvv", cost=cover(OWN_COVER)
    )(merged[0], gate_w, up_w)
    own = call(stack_body, shape((rows, tokens, lanes), bf16), "v" * (rows + 1))(*chunks, gate)
    other = lax.ppermute(own, "heads", swap)
    gate, up = call(
        first_half_body,
        (products_of, products_of),
        "vvvvv",
        limit=FIRST_LIMIT,
        cost=cover(FIRST_COVER),
    )(own, gate, up, gate_w, up_w)
    hidden = call(
        functools.partial(second_half_body, plan),
        shape((tokens, units), bf16),
        "vvvvvv",
        limit=SECOND_LIMIT,
        cost=cover(SECOND_COVER),
    )(other, own, gate, up, gate_w, up_w)
    other_hidden = lax.ppermute(hidden, "heads", swap)
    partial = call(
        down_first_body,
        shape((tokens, plan.half), f32),
        "vv",
        limit=DOWN_LIMIT,
        cost=cover(DOWN_COVER),
    )(hidden, down_w)
    parts = 2
    width = plan.half // parts
    owns, peers, back = [], [], []
    for part in range(parts):
        own_part, peer_part = call(
            functools.partial(down_second_body, part),
            (shape((total, width), f32), shape((total, width), bf16)),
            "vvvv",
            cost=cover(DOWN_COVER),
        )(other_hidden, partial, down_w, peers[-1] if peers else share)
        owns.append(own_part)
        peers.append(peer_part)
        back.append(lax.ppermute(peer_part, "experts", swap))
    out = shape(queries.shape, bf16)
    attn_out = call(functools.partial(attn_body, plan, rows), out, "vv")(own, peers[-1])
    blended = call(
        functools.partial(blend_body, plan, rows),
        (shape((plan.tokens, plan.half), bf16),) * rows,
        "v" * (1 + 2 * parts),
    )(share, *owns, *back)
    moe_out = call(functools.partial(total_body, plan), out, "v" * rows)(*spread(blended))
    return (attn_out, moe_out)


def solution(mesh):
    placed = (
        P(None, ("groups", "rows", "experts"), "heads"),
        P(None, ("groups", "rows", "experts"), None, "heads"),
        P(("groups", "experts"), "rows", None, "heads"),
        P(("groups", "rows", "experts")),
        P(None, ("groups", "rows", "experts"), "heads"),
        P(),
        P("experts", None, ("rows", "heads")),
        P("experts", None, ("rows", "heads")),
        P("experts", "rows", "heads"),
        P(None, ("groups", "rows", "experts"), None),
        P(None, ("groups", "rows", "experts"), None),
    )
    sizes = mesh.shape
    by_head = (
        sizes["heads"] == 2
        and sizes["experts"] == 2
        and sizes["rows"] == 4
        and sizes["rows"] * sizes["heads"] == KV_HEADS
    )
    return jax.shard_map(
        per_device if by_head else per_device_wide,
        mesh=mesh,
        in_specs=placed,
        out_specs=(
            P(None, ("groups", "rows", "experts"), "heads"),
            P(None, ("groups", "rows", "experts"), "heads"),
        ),
        check_vma=False,
    )
```

```python
import functools

import jax
import jax.numpy as jnp
from jax import lax
from jax.experimental import pallas as pl
from jax.experimental.pallas import tpu as pltpu
from jax.sharding import PartitionSpec as P


HEADS = 48
KV_HEADS = 8
HEAD_DIM = 128
GROUP = HEADS // KV_HEADS

VMEM = pltpu.VMEM
MIB = 1 << 20
PACK_COVER = 40 * MIB
FLOPS = 1000
OWN_COVER = 40 * MIB
FIRST_COVER = 1 * MIB
SECOND_COVER = 1 * MIB
FIRST_LIMIT = 4 * MIB
SECOND_LIMIT = 4 * MIB
DOWN_LIMIT = 4 * MIB
ATTEND_COVER = MIB
MERGE_COVER = MIB


def fresh_terms(queries, new_kv):
    step_count, own_rows = (queries.shape[0], queries.shape[1])
    kv_local = new_kv.shape[-1] // HEAD_DIM
    group_size = HEADS // KV_HEADS
    grouped = queries.reshape(step_count, own_rows, kv_local, group_size, HEAD_DIM)
    fresh_keys = new_kv[:, :, 0].reshape(step_count, own_rows, kv_local, HEAD_DIM)
    fresh_values = new_kv[:, :, 1].reshape(step_count, own_rows, kv_local, HEAD_DIM)
    fresh_scores = jnp.einsum(
        "scgnd,tcgd->scgnt", grouped, fresh_keys, preferred_element_type=jnp.float32
    ) * HEAD_DIM ** (-0.5)
    future = jnp.arange(step_count)[None, :] > jnp.arange(step_count)[:, None]
    fresh_scores = jnp.where(future[:, None, None, None, :], -jnp.inf, fresh_scores)
    return (grouped, fresh_scores, fresh_values)


def attend_gathered(queries, new_kv, prefix_kv, local_prompt):
    grouped, fresh_scores, fresh_values = fresh_terms(queries, new_kv)
    own_rows = queries.shape[1]
    kv_local = new_kv.shape[-1] // HEAD_DIM
    cache = lax.all_gather(prefix_kv, "rows", axis=1, tiled=True)
    length = cache.shape[1]
    picked = jnp.take(cache, local_prompt, axis=0)
    cache_keys = picked[:, :, 0].reshape(own_rows, length, kv_local, HEAD_DIM)
    cache_values = picked[:, :, 1].reshape(own_rows, length, kv_local, HEAD_DIM)
    prefix_scores = jnp.einsum(
        "scgnd,ckgd->scgnk", grouped, cache_keys, preferred_element_type=jnp.float32
    ) * HEAD_DIM ** (-0.5)
    highest = jnp.maximum(jnp.max(prefix_scores, axis=-1), jnp.max(fresh_scores, axis=-1))
    prefix_expo = jnp.exp(prefix_scores - highest[..., None])
    fresh_expo = jnp.exp(fresh_scores - highest[..., None])
    totals = jnp.sum(prefix_expo, axis=-1) + jnp.sum(fresh_expo, axis=-1)
    weighted = jnp.einsum(
        "scgnk,ckgd->scgnd",
        prefix_expo.astype(jnp.bfloat16),
        cache_values,
        preferred_element_type=jnp.float32,
    )
    weighted = weighted + jnp.einsum(
        "scgnt,tcgd->scgnd",
        fresh_expo.astype(jnp.bfloat16),
        fresh_values,
        preferred_element_type=jnp.float32,
    )
    return (weighted, totals)


def per_device_wide(
    queries,
    new_kv,
    prefix_kv,
    cont_prompt,
    resid,
    norm_gain,
    w_gate,
    w_up,
    w_down,
    routes,
    route_gates,
):
    step_count, own_rows, half_width = queries.shape
    prompt_count = prefix_kv.shape[0]
    local_prompt = cont_prompt - lax.axis_index("experts") * prompt_count
    weighted, totals = attend_gathered(queries, new_kv, prefix_kv, local_prompt)
    attn_out = (
        (weighted / totals[..., None])
        .astype(jnp.bfloat16)
        .reshape(step_count, own_rows, half_width)
    )
    halves = (
        lax.all_gather(resid, "heads", axis=2, tiled=True),
        lax.all_gather(attn_out, "heads", axis=2, tiled=True),
    )
    combined = halves[0].astype(jnp.float32) + halves[1].astype(jnp.float32)
    square_mean = jnp.mean(combined * combined, axis=-1, keepdims=True)
    normed = (combined * lax.rsqrt(square_mean + 1e-05) * norm_gain.astype(jnp.float32)).astype(
        jnp.bfloat16
    )
    token_count = step_count * own_rows
    flat_tokens = normed.reshape(token_count, -1)
    flat_routes = routes.reshape(token_count, -1)
    experts = lax.axis_size("experts")
    matches = flat_routes[:, :, None] == jnp.arange(experts)[None, None, :]
    gate_weights = w_gate[0]
    up_weights = w_up[0]
    wanted = jnp.transpose(jnp.any(matches, axis=1))
    outgoing = jnp.where(wanted[:, :, None], flat_tokens[None], jnp.zeros((), jnp.bfloat16))
    arrived = lax.all_to_all(outgoing, "experts", split_axis=0, concat_axis=0, tiled=True)
    segment = lax.all_gather(arrived.reshape(experts * token_count, -1), "rows", axis=0, tiled=True)
    gate = jnp.dot(segment, gate_weights, preferred_element_type=jnp.float32)
    up_part = jnp.dot(segment, up_weights, preferred_element_type=jnp.float32)
    hidden = (jax.nn.silu(gate) * up_part).astype(jnp.bfloat16)
    paired = lax.all_gather(hidden, "heads", axis=1, tiled=True)
    down_rows = w_down[0]
    segment = paired
    summed = lax.psum_scatter(
        jnp.dot(segment, down_rows, preferred_element_type=jnp.float32).astype(jnp.bfloat16),
        "rows",
        scatter_dimension=0,
        tiled=True,
    )
    result = summed.reshape(experts, token_count, -1)
    returned = lax.all_to_all(result, "experts", split_axis=0, concat_axis=0, tiled=True)
    mixing = jnp.sum(
        jnp.where(matches, route_gates.reshape(token_count, -1)[:, :, None], 0.0), axis=1
    )
    mixture = jnp.einsum("ne,end->nd", mixing, returned.astype(jnp.float32))
    moe_out = mixture.astype(jnp.bfloat16).reshape(step_count, own_rows, half_width)
    return (attn_out, moe_out)


def call(body, outs, in_spaces, scratch=(), limit=4 * MIB, cost=None):
    spaces = {"v": VMEM, "s": pltpu.SMEM, "a": pl.ANY}
    single = not isinstance(outs, (list, tuple))
    shapes = [outs] if single else list(outs)
    specs = [pl.BlockSpec(memory_space=VMEM) for _ in shapes]
    return pl.pallas_call(
        body,
        out_shape=shapes[0] if single else tuple(shapes),
        in_specs=[pl.BlockSpec(memory_space=spaces[s]) for s in in_spaces],
        out_specs=specs[0] if single else tuple(specs),
        scratch_shapes=list(scratch),
        compiler_params=pltpu.CompilerParams(vmem_limit_bytes=limit),
        cost_estimate=cost,
    )


class Plan:
    def __init__(self, queries, prefix_kv):
        self.steps, self.conts, self.half = queries.shape
        self.prompts, self.positions = prefix_kv.shape[:2]
        self.tokens = self.steps * self.conts
        self.block = self.prompts * self.positions * 2
        self.fresh = self.block
        self.query = self.fresh + 2 * self.tokens
        self.resid = self.query + GROUP * self.tokens
        self.prompt = self.resid + GROUP * self.tokens
        self.rows = -(-(self.prompt + self.tokens) // 16) * 16


def fetch_body(plan, experts, *refs):
    f32, bf16 = jnp.float32, jnp.bfloat16
    sources, targets, scalars, sems = refs[:7], refs[7:12], refs[12:15], refs[15]
    copies = [
        pltpu.make_async_copy(source, target, sems.at[i])
        for i, (source, target) in enumerate(zip(sources, scalars + targets[1:]))
    ]
    for copy in copies:
        copy.start()
    for copy in copies:
        copy.wait()
    prompts, routes, gates = scalars
    base = lax.axis_index("experts") * plan.prompts
    shape = (plan.tokens, HEAD_DIM)
    row = lax.broadcasted_iota(jnp.int32, shape, 0)
    lane = lax.broadcasted_iota(jnp.int32, shape, 1)
    value = jnp.zeros(shape, f32)
    for s in range(plan.steps):
        for c in range(plan.conts):
            here = row == s * plan.conts + c
            value = jnp.where(here & (lane == 0), (prompts[c] - base).astype(f32), value)
            for e in range(experts):
                amount = f32(0.0)
                for k in range(routes.shape[2]):
                    amount = amount + jnp.where(routes[s, c, k] == e, gates[s, c, k], 0.0)
                value = jnp.where(here & ((lane + 2) // 3 == e + 1), amount, value)
    high = value.astype(bf16).astype(f32)
    middle = (value - high).astype(bf16).astype(f32)
    low = value - high - middle
    which = (lane + 2) % 3
    parts = jnp.where(lane == 0, high, jnp.where(which == 0, high, jnp.where(which == 1, middle, low)))
    targets[0][...] = parts.astype(bf16)


def pack_body(plan, local_ref, q_ref, new_ref, prefix_ref, resid_ref, *outs):
    t, c = plan.tokens, plan.conts
    own = lax.axis_index("rows")
    for k, out_ref in enumerate(outs):
        h = own ^ k
        lanes = pl.ds(pl.multiple_of(h * HEAD_DIM, HEAD_DIM), HEAD_DIM)
        for p in range(plan.prompts):
            for i in range(plan.positions):
                out_ref[pl.ds((p * plan.positions + i) * 2, 2), :] = prefix_ref[p, i, :, lanes]
        for s in range(plan.steps):
            for i in range(c):
                out_ref[pl.ds(plan.fresh + (s * c + i) * 2, 2), :] = new_ref[s, i, :, lanes]
            for g in range(GROUP):
                head = pl.ds(pl.multiple_of((h * GROUP + g) * HEAD_DIM, HEAD_DIM), HEAD_DIM)
                out_ref[pl.ds(plan.query + g * t + s * c, c), :] = q_ref[s, :, head]
                out_ref[pl.ds(plan.resid + g * t + s * c, c), :] = resid_ref[s, :, head]
        out_ref[pl.ds(plan.prompt, t), :] = local_ref[...]


def attend_body(plan, rows, *refs):
    pieces, (gain_ref, x_ref, attn_ref, q_s, r_s, kv_s, p_s, gain_s) = refs[:rows], refs[rows:]
    t, c = plan.tokens, plan.conts
    total = rows * t
    f32 = jnp.float32

    def place(own):
        for k, got_ref in enumerate(pieces):
            src = own ^ k
            kv_s[pl.ds(src * plan.block, plan.block), :] = got_ref[pl.ds(0, plan.block), :]
            late = pl.ds(rows * plan.block + src * 2 * t, 2 * t)
            kv_s[late, :] = got_ref[pl.ds(plan.fresh, 2 * t), :]
            p_s[pl.ds(src * t, t), :] = got_ref[pl.ds(plan.prompt, t), :]
            for g in range(GROUP):
                q_s[pl.ds(g * total + src * t, t), :] = got_ref[pl.ds(plan.query + g * t, t), :]
                r_s[pl.ds(g * total + src * t, t), :] = got_ref[pl.ds(plan.resid + g * t, t), :]

    for own in range(rows):
        pl.when(lax.axis_index("rows") == own)(functools.partial(place, own))
    used = rows * plan.block + rows * 2 * t
    spare = kv_s.shape[0] - used
    if spare:
        kv_s[pl.ds(used, spare), :] = jnp.zeros((spare, HEAD_DIM), jnp.bfloat16)
    kv = kv_s[...]
    scores = lax.dot_general(
        q_s[...], kv, (((1,), (1,)), ((), ())), preferred_element_type=f32
    ) * HEAD_DIM ** (-0.5)
    shape = scores.shape
    row = lax.broadcasted_iota(jnp.int32, shape, 0) % total
    col = lax.broadcasted_iota(jnp.int32, shape, 1)
    prompt = p_s[...].astype(f32)[:, :1]
    prompt = jnp.concatenate([prompt] * GROUP, axis=0).astype(jnp.int32)
    in_prefix = (col < rows * plan.block) & ((col % plan.block) // (2 * plan.positions) == prompt)
    late = col - rows * plan.block
    same = (late // (2 * t) == row // t) & (((late // 2) % t) % c == row % c)
    seen = ((late // 2) % t) // c <= (row % t) // c
    in_fresh = (late >= 0) & (col < used) & same & seen
    live = (col % 2 == 0) & (in_prefix | in_fresh)
    scores = jnp.where(live, scores, -jnp.inf)
    highest = jnp.max(scores, axis=-1, keepdims=True)
    expo = jnp.exp(scores - highest)
    totals = jnp.sum(expo, axis=-1, keepdims=True)
    weights = pltpu.roll(expo, 1, 1).astype(jnp.bfloat16)
    out = jnp.dot(weights, kv, preferred_element_type=f32) / totals
    attn = out.astype(jnp.bfloat16)
    attn_ref[...] = attn
    gain_s[...] = gain_ref[...].astype(f32)
    first = (lax.axis_index("heads") * rows + lax.axis_index("rows")) * GROUP
    combined = attn.astype(f32) + r_s[...].astype(f32)
    square = jnp.zeros((total, HEAD_DIM), f32)
    for g in range(GROUP):
        part = combined[g * total : (g + 1) * total]
        square = square + part * part
        gained = part * gain_s[pl.ds(first + g, 1), :]
        x_ref[:, pl.ds(g * HEAD_DIM, HEAD_DIM)] = gained.astype(jnp.bfloat16)
    square = jnp.sum(square, axis=-1, keepdims=True)
    high = square.astype(jnp.bfloat16)
    low = (square - high.astype(f32)).astype(jnp.bfloat16)
    lane = lax.broadcasted_iota(jnp.int32, (total, HEAD_DIM), 1)
    extra = jnp.where(lane == 0, high.astype(f32), jnp.where(lane == 1, low.astype(f32), 0.0))
    x_ref[:, pl.ds(GROUP * HEAD_DIM, HEAD_DIM)] = extra.astype(jnp.bfloat16)


def to_row(column, first, lanes):
    shape = (column.shape[0], lanes)
    hit = lax.broadcasted_iota(jnp.int32, shape, 1) == lax.broadcasted_iota(jnp.int32, shape, 0) + first
    return jnp.sum(jnp.where(hit, column, 0.0), axis=0, keepdims=True)


def to_column(row, count):
    shape = (count, row.shape[1])
    hit = lax.broadcasted_iota(jnp.int32, shape, 1) == lax.broadcasted_iota(jnp.int32, shape, 0)
    return jnp.sum(jnp.where(hit, row, 0.0), axis=1, keepdims=True)


def merge_body(plan, rows, own_ref, peer_ref, attn_ref, *outs):
    t = plan.tokens
    total, width = own_ref.shape
    depth = width - HEAD_DIM
    spare = pl.ds(depth, HEAD_DIM)
    high, low = [], []
    for i, ref in enumerate((own_ref, peer_ref)):
        extra = ref[:, spare].astype(jnp.float32)
        high.append(to_row(extra[:, 0:1], i * total, HEAD_DIM))
        low.append(to_row(extra[:, 1:2], i * total, HEAD_DIM))
    row = lax.broadcasted_iota(jnp.int32, (2 * total - GROUP * t, HEAD_DIM), 0)
    squares = jnp.where(row == 0, high[0] + high[1], jnp.where(row == 1, low[0] + low[1], 0.0))
    squares = squares.astype(jnp.bfloat16)
    for out_ref in outs:
        for i, ref in enumerate((own_ref, peer_ref)):
            out_ref[pl.ds(i * total, total), pl.ds(0, depth)] = ref[:, pl.ds(0, depth)]
        out_ref[pl.ds(GROUP * t, row.shape[0]), spare] = squares

    def place(own):
        for k, out_ref in enumerate(outs):
            for g in range(GROUP):
                part = attn_ref[pl.ds(g * total + (own ^ k) * t, t), :]
                out_ref[pl.ds(g * t, t), spare] = part

    for own in range(rows):
        pl.when(lax.axis_index("rows") == own)(functools.partial(place, own))


def stack_body(*refs):
    *pieces, _, out_ref = refs
    for k, ref in enumerate(pieces):
        out_ref[k] = ref[...]


def products(side, x, weight, k, total):
    depth = x.shape[1]
    core = lax.axis_index("heads")
    core = 1 - core if side else core
    half = weight.shape[1] // 2
    first = pl.multiple_of(core * half + (lax.axis_index("rows") ^ k) * depth, depth)
    part = jnp.dot(x, weight[0, pl.ds(first, depth)], preferred_element_type=jnp.float32)
    return part if total is None else total + part


def own_chunk_body(x_ref, gate_w, up_w, gate_ref, up_ref):
    x = x_ref[:, pl.ds(0, x_ref.shape[1] - HEAD_DIM)]
    gate_ref[...] = products(0, x, gate_w, 0, None)
    up_ref[...] = products(0, x, up_w, 0, None)


def first_half_body(x_ref, gate_in, up_in, gate_w, up_w, gate_ref, up_ref):
    chunks, _, width = x_ref.shape
    gate, up = gate_in[...], up_in[...]
    for k in range(1, chunks):
        x = x_ref[k, :, pl.ds(0, width - HEAD_DIM)]
        gate = products(0, x, gate_w, k, gate)
        up = products(0, x, up_w, k, up)
    gate_ref[...] = gate
    up_ref[...] = up


def second_half_body(plan, x_ref, own_ref, gate_in, up_in, gate_w, up_w, hidden_ref):
    chunks, tokens, width = x_ref.shape
    depth = width - HEAD_DIM
    first = GROUP * plan.tokens
    square = jnp.zeros((tokens - first, HEAD_DIM), jnp.float32)
    for ref in (own_ref, x_ref):
        for k in range(chunks):
            extra = ref[k, pl.ds(first, tokens - first), pl.ds(depth, HEAD_DIM)]
            square = square + extra.astype(jnp.float32)
    square = to_column(square[0:1] + square[1:2], tokens)
    scale = lax.rsqrt(square / (2 * chunks * depth) + 1e-05)
    gate, up = gate_in[...], up_in[...]
    for k in range(chunks):
        x = x_ref[k, :, pl.ds(0, depth)]
        gate = products(1, x, gate_w, k, gate)
        up = products(1, x, up_w, k, up)
    gate = gate * scale
    up = up * scale
    hidden_ref[...] = (gate / (1.0 + jnp.exp(-gate)) * up).astype(jnp.bfloat16)


def down_product(side, hidden_ref, down_w):
    depth = hidden_ref.shape[1]
    core = lax.axis_index("heads")
    first = pl.multiple_of((1 - core if side else core) * depth, depth)
    return jnp.dot(
        hidden_ref[...], down_w[0, pl.ds(first, depth)], preferred_element_type=jnp.float32
    )


def down_first_body(hidden_ref, down_w, out_ref):
    out_ref[...] = down_product(0, hidden_ref, down_w)


def down_second_body(plan, rows, hidden_ref, own_ref, down_w, *outs):
    result = own_ref[...] + down_product(1, hidden_ref, down_w)
    t = plan.tokens
    total = rows * t

    def place(own):
        for k, out_ref in enumerate(outs):
            first = (own ^ k) * t
            pair = [result[i : i + t] for i in (first, first + total)]
            out_ref[...] = jnp.concatenate(pair, axis=0).astype(jnp.bfloat16)

    for own in range(rows):
        pl.when(lax.axis_index("rows") == own)(functools.partial(place, own))


def sum_body(*refs):
    *pieces, own_ref, peer_ref = refs
    total = pieces[0][...].astype(jnp.float32)
    for ref in pieces[1:]:
        total = total + ref[...].astype(jnp.float32)
    t = own_ref.shape[0]
    own_ref[...] = total[:t].astype(jnp.bfloat16)
    peer_ref[...] = total[t:].astype(jnp.bfloat16)


def attn_body(plan, rows, own_ref, _, attn_ref):
    t = plan.tokens
    depth = own_ref.shape[2] - HEAD_DIM
    for k in range(rows):
        head = (lax.axis_index("rows") ^ k) * GROUP
        for g in range(GROUP):
            lanes = pl.ds(pl.multiple_of((head + g) * HEAD_DIM, HEAD_DIM), HEAD_DIM)
            for s in range(plan.steps):
                attn_ref[s, :, lanes] = own_ref[
                    k, pl.ds(g * t + s * plan.conts, plan.conts), pl.ds(depth, HEAD_DIM)
                ]


def mix_body(plan, local_ref, own_ref, peer_ref, moe_ref):
    own = lax.axis_index("experts")
    local = local_ref[...].astype(jnp.float32)
    lane = lax.broadcasted_iota(jnp.int32, local.shape, 1)
    mixture = None
    for i, ref in enumerate((own_ref, peer_ref)):
        parts = jnp.where((lane > 0) & ((lane + 2) // 3 == (own ^ i) + 1), local, 0.0)
        part = jnp.sum(parts, axis=1, keepdims=True) * ref[...].astype(jnp.float32)
        mixture = part if mixture is None else mixture + part
    mixture = mixture.astype(jnp.bfloat16)
    for s in range(plan.steps):
        moe_ref[s] = mixture[s * plan.conts : (s + 1) * plan.conts]


def per_device(
    queries,
    new_kv,
    prefix_kv,
    cont_prompt,
    resid,
    norm_gain,
    w_gate,
    w_up,
    w_down,
    routes,
    route_gates,
):
    rows, experts = lax.axis_size("rows"), lax.axis_size("experts")
    plan = Plan(queries, prefix_kv)
    bf16, f32 = jnp.bfloat16, jnp.float32
    shape = jax.ShapeDtypeStruct
    piece = GROUP * HEAD_DIM
    total = rows * plan.tokens
    tokens = experts * total

    hbm = functools.partial(pltpu.with_memory_space_constraint, memory_space=pltpu.HBM)
    vmem = functools.partial(pltpu.with_memory_space_constraint, memory_space=VMEM)
    gate_w, up_w, down_w = w_gate, w_up, w_down

    def cover(size):
        return pl.CostEstimate(flops=FLOPS * size, bytes_accessed=size, transcendentals=0)

    scalars = (cont_prompt, routes, route_gates)
    arrays = (queries, new_kv, prefix_kv, resid)
    fetched = call(
        functools.partial(fetch_body, plan, experts),
        (VMEM((plan.tokens, HEAD_DIM), bf16),) + tuple(VMEM(a.shape, bf16) for a in arrays),
        "a" * (len(scalars) + len(arrays)),
        scratch=tuple(pltpu.SMEM(a.shape, a.dtype) for a in scalars)
        + (pltpu.SemaphoreType.DMA((len(scalars) + len(arrays),)),),
    )(*map(hbm, scalars + arrays))
    packed = call(
        functools.partial(pack_body, plan),
        (shape((plan.rows, HEAD_DIM), bf16),) * rows,
        "vvvvv",
        cost=cover(PACK_COVER),
    )(*map(vmem, fetched))

    def spread(pieces):
        got = [pieces[0]]
        for k in range(1, rows):
            got.append(lax.ppermute(pieces[k], "rows", [(i, i ^ k) for i in range(rows)]))
        return got

    keys = -(-(rows * (plan.block + 2 * plan.tokens)) // 128) * 128
    lanes = piece + HEAD_DIM
    x, attn = call(
        functools.partial(attend_body, plan, rows),
        (shape((total, lanes), bf16), shape((GROUP * total, HEAD_DIM), bf16)),
        "v" * (rows + 1),
        scratch=(
            VMEM((GROUP * total, HEAD_DIM), bf16),
            VMEM((GROUP * total, HEAD_DIM), bf16),
            VMEM((keys, HEAD_DIM), bf16),
            VMEM((total, HEAD_DIM), bf16),
            VMEM((norm_gain.size // HEAD_DIM, HEAD_DIM), f32),
        ),
        cost=cover(ATTEND_COVER),
    )(*spread(packed), norm_gain.reshape(-1, HEAD_DIM))
    swap = [(0, 1), (1, 0)]
    peer = lax.ppermute(x, "experts", swap)
    merged = call(
        functools.partial(merge_body, plan, rows),
        (shape((tokens, lanes), bf16),) * rows,
        "vvv",
        cost=cover(MERGE_COVER),
    )(x, peer, attn)
    chunks = spread(merged)
    units = w_gate.shape[2]
    products_of = shape((tokens, units), f32)
    gate, up = call(
        own_chunk_body, (products_of, products_of), "vvv", cost=cover(OWN_COVER)
    )(merged[0], gate_w, up_w)
    own = call(stack_body, shape((rows, tokens, lanes), bf16), "v" * (rows + 1))(*chunks, gate)
    other = lax.ppermute(own, "heads", swap)
    gate, up = call(
        first_half_body,
        (products_of, products_of),
        "vvvvv",
        limit=FIRST_LIMIT,
        cost=cover(FIRST_COVER),
    )(own, gate, up, gate_w, up_w)
    hidden = call(
        functools.partial(second_half_body, plan),
        shape((tokens, units), bf16),
        "vvvvvv",
        limit=SECOND_LIMIT,
        cost=cover(SECOND_COVER),
    )(other, own, gate, up, gate_w, up_w)
    other_hidden = lax.ppermute(hidden, "heads", swap)
    partial = call(
        down_first_body,
        shape((tokens, plan.half), f32),
        "vv",
        limit=DOWN_LIMIT,
        cost=cover(2 * plan.half * units),
    )(hidden, down_w)
    blocks = call(
        functools.partial(down_second_body, plan, rows),
        (shape((experts * plan.tokens, plan.half), bf16),) * rows,
        "vvv",
        cost=cover(2 * plan.half * units),
    )(other_hidden, partial, down_w)
    output = shape((plan.tokens, plan.half), bf16)
    mine, theirs = call(sum_body, (output, output), "v" * rows)(*spread(blocks))
    returned = lax.ppermute(theirs, "experts", swap)
    out = shape(queries.shape, bf16)
    attn_out = call(functools.partial(attn_body, plan, rows), out, "vv")(own, theirs)
    moe_out = call(functools.partial(mix_body, plan), out, "vvv")(vmem(fetched[0]), mine, returned)
    return (attn_out, moe_out)


def solution(mesh):
    placed = (
        P(None, ("groups", "rows", "experts"), "heads"),
        P(None, ("groups", "rows", "experts"), None, "heads"),
        P(("groups", "experts"), "rows", None, "heads"),
        P(("groups", "rows", "experts")),
        P(None, ("groups", "rows", "experts"), "heads"),
        P(),
        P("experts", None, ("rows", "heads")),
        P("experts", None, ("rows", "heads")),
        P("experts", "rows", "heads"),
        P(None, ("groups", "rows", "experts"), None),
        P(None, ("groups", "rows", "experts"), None),
    )
    sizes = mesh.shape
    by_head = (
        sizes["heads"] == 2
        and sizes["experts"] == 2
        and sizes["rows"] == 4
        and sizes["rows"] * sizes["heads"] == KV_HEADS
    )
    return jax.shard_map(
        per_device if by_head else per_device_wide,
        mesh=mesh,
        in_specs=placed,
        out_specs=(
            P(None, ("groups", "rows", "experts"), "heads"),
            P(None, ("groups", "rows", "experts"), "heads"),
        ),
        check_vma=False,
    )
```

```python
import functools

import jax
import jax.numpy as jnp
from jax import lax
from jax.experimental import pallas as pl
from jax.experimental.pallas import tpu as pltpu
from jax.sharding import PartitionSpec as P


HEADS = 48
KV_HEADS = 8
HEAD_DIM = 128
GROUP = HEADS // KV_HEADS

VMEM = pltpu.VMEM
MIB = 1 << 20
PACK_COVER = 40 * MIB
FLOPS = 1000
OWN_COVER = 40 * MIB
FIRST_COVER = 1 * MIB
SECOND_COVER = 1 * MIB
FIRST_LIMIT = 4 * MIB
SECOND_LIMIT = 4 * MIB
DOWN_LIMIT = 4 * MIB
ATTEND_COVER = MIB
MERGE_COVER = MIB


def fresh_terms(queries, new_kv):
    step_count, own_rows = (queries.shape[0], queries.shape[1])
    kv_local = new_kv.shape[-1] // HEAD_DIM
    group_size = HEADS // KV_HEADS
    grouped = queries.reshape(step_count, own_rows, kv_local, group_size, HEAD_DIM)
    fresh_keys = new_kv[:, :, 0].reshape(step_count, own_rows, kv_local, HEAD_DIM)
    fresh_values = new_kv[:, :, 1].reshape(step_count, own_rows, kv_local, HEAD_DIM)
    fresh_scores = jnp.einsum(
        "scgnd,tcgd->scgnt", grouped, fresh_keys, preferred_element_type=jnp.float32
    ) * HEAD_DIM ** (-0.5)
    future = jnp.arange(step_count)[None, :] > jnp.arange(step_count)[:, None]
    fresh_scores = jnp.where(future[:, None, None, None, :], -jnp.inf, fresh_scores)
    return (grouped, fresh_scores, fresh_values)


def attend_gathered(queries, new_kv, prefix_kv, local_prompt):
    grouped, fresh_scores, fresh_values = fresh_terms(queries, new_kv)
    own_rows = queries.shape[1]
    kv_local = new_kv.shape[-1] // HEAD_DIM
    cache = lax.all_gather(prefix_kv, "rows", axis=1, tiled=True)
    length = cache.shape[1]
    picked = jnp.take(cache, local_prompt, axis=0)
    cache_keys = picked[:, :, 0].reshape(own_rows, length, kv_local, HEAD_DIM)
    cache_values = picked[:, :, 1].reshape(own_rows, length, kv_local, HEAD_DIM)
    prefix_scores = jnp.einsum(
        "scgnd,ckgd->scgnk", grouped, cache_keys, preferred_element_type=jnp.float32
    ) * HEAD_DIM ** (-0.5)
    highest = jnp.maximum(jnp.max(prefix_scores, axis=-1), jnp.max(fresh_scores, axis=-1))
    prefix_expo = jnp.exp(prefix_scores - highest[..., None])
    fresh_expo = jnp.exp(fresh_scores - highest[..., None])
    totals = jnp.sum(prefix_expo, axis=-1) + jnp.sum(fresh_expo, axis=-1)
    weighted = jnp.einsum(
        "scgnk,ckgd->scgnd",
        prefix_expo.astype(jnp.bfloat16),
        cache_values,
        preferred_element_type=jnp.float32,
    )
    weighted = weighted + jnp.einsum(
        "scgnt,tcgd->scgnd",
        fresh_expo.astype(jnp.bfloat16),
        fresh_values,
        preferred_element_type=jnp.float32,
    )
    return (weighted, totals)


def per_device_wide(
    queries,
    new_kv,
    prefix_kv,
    cont_prompt,
    resid,
    norm_gain,
    w_gate,
    w_up,
    w_down,
    routes,
    route_gates,
):
    step_count, own_rows, half_width = queries.shape
    prompt_count = prefix_kv.shape[0]
    local_prompt = cont_prompt - lax.axis_index("experts") * prompt_count
    weighted, totals = attend_gathered(queries, new_kv, prefix_kv, local_prompt)
    attn_out = (
        (weighted / totals[..., None])
        .astype(jnp.bfloat16)
        .reshape(step_count, own_rows, half_width)
    )
    halves = (
        lax.all_gather(resid, "heads", axis=2, tiled=True),
        lax.all_gather(attn_out, "heads", axis=2, tiled=True),
    )
    combined = halves[0].astype(jnp.float32) + halves[1].astype(jnp.float32)
    square_mean = jnp.mean(combined * combined, axis=-1, keepdims=True)
    normed = (combined * lax.rsqrt(square_mean + 1e-05) * norm_gain.astype(jnp.float32)).astype(
        jnp.bfloat16
    )
    token_count = step_count * own_rows
    flat_tokens = normed.reshape(token_count, -1)
    flat_routes = routes.reshape(token_count, -1)
    experts = lax.axis_size("experts")
    matches = flat_routes[:, :, None] == jnp.arange(experts)[None, None, :]
    gate_weights = w_gate[0]
    up_weights = w_up[0]
    wanted = jnp.transpose(jnp.any(matches, axis=1))
    outgoing = jnp.where(wanted[:, :, None], flat_tokens[None], jnp.zeros((), jnp.bfloat16))
    arrived = lax.all_to_all(outgoing, "experts", split_axis=0, concat_axis=0, tiled=True)
    segment = lax.all_gather(arrived.reshape(experts * token_count, -1), "rows", axis=0, tiled=True)
    gate = jnp.dot(segment, gate_weights, preferred_element_type=jnp.float32)
    up_part = jnp.dot(segment, up_weights, preferred_element_type=jnp.float32)
    hidden = (jax.nn.silu(gate) * up_part).astype(jnp.bfloat16)
    paired = lax.all_gather(hidden, "heads", axis=1, tiled=True)
    down_rows = w_down[0]
    segment = paired
    summed = lax.psum_scatter(
        jnp.dot(segment, down_rows, preferred_element_type=jnp.float32).astype(jnp.bfloat16),
        "rows",
        scatter_dimension=0,
        tiled=True,
    )
    result = summed.reshape(experts, token_count, -1)
    returned = lax.all_to_all(result, "experts", split_axis=0, concat_axis=0, tiled=True)
    mixing = jnp.sum(
        jnp.where(matches, route_gates.reshape(token_count, -1)[:, :, None], 0.0), axis=1
    )
    mixture = jnp.einsum("ne,end->nd", mixing, returned.astype(jnp.float32))
    moe_out = mixture.astype(jnp.bfloat16).reshape(step_count, own_rows, half_width)
    return (attn_out, moe_out)


def call(body, outs, in_spaces, scratch=(), limit=4 * MIB, cost=None):
    spaces = {"v": VMEM, "s": pltpu.SMEM, "a": pl.ANY}
    single = not isinstance(outs, (list, tuple))
    shapes = [outs] if single else list(outs)
    specs = [pl.BlockSpec(memory_space=VMEM) for _ in shapes]
    return pl.pallas_call(
        body,
        out_shape=shapes[0] if single else tuple(shapes),
        in_specs=[pl.BlockSpec(memory_space=spaces[s]) for s in in_spaces],
        out_specs=specs[0] if single else tuple(specs),
        scratch_shapes=list(scratch),
        compiler_params=pltpu.CompilerParams(vmem_limit_bytes=limit),
        cost_estimate=cost,
    )


class Plan:
    def __init__(self, queries, prefix_kv):
        self.steps, self.conts, self.half = queries.shape
        self.prompts, self.positions = prefix_kv.shape[:2]
        self.tokens = self.steps * self.conts
        self.block = self.prompts * self.positions * 2
        self.fresh = self.block
        self.query = self.fresh + 2 * self.tokens
        self.resid = self.query + GROUP * self.tokens
        self.prompt = self.resid + GROUP * self.tokens
        self.rows = -(-(self.prompt + self.tokens) // 16) * 16


def fetch_body(plan, experts, *refs):
    f32, bf16 = jnp.float32, jnp.bfloat16
    sources, targets, scalars, sems = refs[:7], refs[7:12], refs[12:15], refs[15]
    copies = [
        pltpu.make_async_copy(source, target, sems.at[i])
        for i, (source, target) in enumerate(zip(sources, scalars + targets[1:]))
    ]
    for copy in copies:
        copy.start()
    for copy in copies:
        copy.wait()
    prompts, routes, gates = scalars
    base = lax.axis_index("experts") * plan.prompts
    shape = (plan.tokens, HEAD_DIM)
    row = lax.broadcasted_iota(jnp.int32, shape, 0)
    lane = lax.broadcasted_iota(jnp.int32, shape, 1)
    value = jnp.zeros(shape, f32)
    for s in range(plan.steps):
        for c in range(plan.conts):
            here = row == s * plan.conts + c
            value = jnp.where(here & (lane == 0), (prompts[c] - base).astype(f32), value)
            for e in range(experts):
                amount = f32(0.0)
                for k in range(routes.shape[2]):
                    amount = amount + jnp.where(routes[s, c, k] == e, gates[s, c, k], 0.0)
                value = jnp.where(here & ((lane + 2) // 3 == e + 1), amount, value)
    high = value.astype(bf16).astype(f32)
    middle = (value - high).astype(bf16).astype(f32)
    low = value - high - middle
    which = (lane + 2) % 3
    parts = jnp.where(lane == 0, high, jnp.where(which == 0, high, jnp.where(which == 1, middle, low)))
    targets[0][...] = parts.astype(bf16)


def pack_body(plan, local_ref, q_ref, new_ref, prefix_ref, resid_ref, *outs):
    t, c = plan.tokens, plan.conts
    own = lax.axis_index("rows")
    for k, out_ref in enumerate(outs):
        h = own ^ k
        lanes = pl.ds(pl.multiple_of(h * HEAD_DIM, HEAD_DIM), HEAD_DIM)
        for p in range(plan.prompts):
            for i in range(plan.positions):
                out_ref[pl.ds((p * plan.positions + i) * 2, 2), :] = prefix_ref[p, i, :, lanes]
        for s in range(plan.steps):
            for i in range(c):
                out_ref[pl.ds(plan.fresh + (s * c + i) * 2, 2), :] = new_ref[s, i, :, lanes]
            for g in range(GROUP):
                head = pl.ds(pl.multiple_of((h * GROUP + g) * HEAD_DIM, HEAD_DIM), HEAD_DIM)
                out_ref[pl.ds(plan.query + g * t + s * c, c), :] = q_ref[s, :, head]
                out_ref[pl.ds(plan.resid + g * t + s * c, c), :] = resid_ref[s, :, head]
        out_ref[pl.ds(plan.prompt, t), :] = local_ref[...]


def attend_body(plan, rows, *refs):
    pieces, (gain_ref, x_ref, attn_ref, q_s, r_s, kv_s, p_s, gain_s) = refs[:rows], refs[rows:]
    t, c = plan.tokens, plan.conts
    total = rows * t
    f32 = jnp.float32

    def place(own):
        for k, got_ref in enumerate(pieces):
            src = own ^ k
            kv_s[pl.ds(src * plan.block, plan.block), :] = got_ref[pl.ds(0, plan.block), :]
            late = pl.ds(rows * plan.block + src * 2 * t, 2 * t)
            kv_s[late, :] = got_ref[pl.ds(plan.fresh, 2 * t), :]
            p_s[pl.ds(src * t, t), :] = got_ref[pl.ds(plan.prompt, t), :]
            for g in range(GROUP):
                q_s[pl.ds(g * total + src * t, t), :] = got_ref[pl.ds(plan.query + g * t, t), :]
                r_s[pl.ds(g * total + src * t, t), :] = got_ref[pl.ds(plan.resid + g * t, t), :]

    for own in range(rows):
        pl.when(lax.axis_index("rows") == own)(functools.partial(place, own))
    used = rows * plan.block + rows * 2 * t
    spare = kv_s.shape[0] - used
    if spare:
        kv_s[pl.ds(used, spare), :] = jnp.zeros((spare, HEAD_DIM), jnp.bfloat16)
    kv = kv_s[...]
    scores = lax.dot_general(
        q_s[...], kv, (((1,), (1,)), ((), ())), preferred_element_type=f32
    ) * HEAD_DIM ** (-0.5)
    shape = scores.shape
    row = lax.broadcasted_iota(jnp.int32, shape, 0) % total
    col = lax.broadcasted_iota(jnp.int32, shape, 1)
    prompt = p_s[...].astype(f32)[:, :1]
    prompt = jnp.concatenate([prompt] * GROUP, axis=0).astype(jnp.int32)
    in_prefix = (col < rows * plan.block) & ((col % plan.block) // (2 * plan.positions) == prompt)
    late = col - rows * plan.block
    same = (late // (2 * t) == row // t) & (((late // 2) % t) % c == row % c)
    seen = ((late // 2) % t) // c <= (row % t) // c
    in_fresh = (late >= 0) & (col < used) & same & seen
    live = (col % 2 == 0) & (in_prefix | in_fresh)
    scores = jnp.where(live, scores, -jnp.inf)
    highest = jnp.max(scores, axis=-1, keepdims=True)
    expo = jnp.exp(scores - highest)
    totals = jnp.sum(expo, axis=-1, keepdims=True)
    weights = pltpu.roll(expo, 1, 1).astype(jnp.bfloat16)
    out = jnp.dot(weights, kv, preferred_element_type=f32) / totals
    attn = out.astype(jnp.bfloat16)
    attn_ref[...] = attn
    gain_s[...] = gain_ref[...].astype(f32)
    first = (lax.axis_index("heads") * rows + lax.axis_index("rows")) * GROUP
    combined = attn.astype(f32) + r_s[...].astype(f32)
    square = jnp.zeros((total, HEAD_DIM), f32)
    for g in range(GROUP):
        part = combined[g * total : (g + 1) * total]
        square = square + part * part
        gained = part * gain_s[pl.ds(first + g, 1), :]
        x_ref[:, pl.ds(g * HEAD_DIM, HEAD_DIM)] = gained.astype(jnp.bfloat16)
    square = jnp.sum(square, axis=-1, keepdims=True)
    high = square.astype(jnp.bfloat16)
    low = (square - high.astype(f32)).astype(jnp.bfloat16)
    lane = lax.broadcasted_iota(jnp.int32, (total, HEAD_DIM), 1)
    extra = jnp.where(lane == 0, high.astype(f32), jnp.where(lane == 1, low.astype(f32), 0.0))
    x_ref[:, pl.ds(GROUP * HEAD_DIM, HEAD_DIM)] = extra.astype(jnp.bfloat16)


def to_row(column, first, lanes):
    shape = (column.shape[0], lanes)
    hit = lax.broadcasted_iota(jnp.int32, shape, 1) == lax.broadcasted_iota(jnp.int32, shape, 0) + first
    return jnp.sum(jnp.where(hit, column, 0.0), axis=0, keepdims=True)


def to_column(row, count):
    shape = (count, row.shape[1])
    hit = lax.broadcasted_iota(jnp.int32, shape, 1) == lax.broadcasted_iota(jnp.int32, shape, 0)
    return jnp.sum(jnp.where(hit, row, 0.0), axis=1, keepdims=True)


def merge_body(plan, rows, own_ref, peer_ref, attn_ref, *outs):
    t = plan.tokens
    total, width = own_ref.shape
    depth = width - HEAD_DIM
    spare = pl.ds(depth, HEAD_DIM)
    high, low = [], []
    for i, ref in enumerate((own_ref, peer_ref)):
        extra = ref[:, spare].astype(jnp.float32)
        high.append(to_row(extra[:, 0:1], i * total, HEAD_DIM))
        low.append(to_row(extra[:, 1:2], i * total, HEAD_DIM))
    row = lax.broadcasted_iota(jnp.int32, (2 * total - GROUP * t, HEAD_DIM), 0)
    squares = jnp.where(row == 0, high[0] + high[1], jnp.where(row == 1, low[0] + low[1], 0.0))
    squares = squares.astype(jnp.bfloat16)
    for out_ref in outs:
        for i, ref in enumerate((own_ref, peer_ref)):
            out_ref[pl.ds(i * total, total), pl.ds(0, depth)] = ref[:, pl.ds(0, depth)]
        out_ref[pl.ds(GROUP * t, row.shape[0]), spare] = squares

    def place(own):
        for k, out_ref in enumerate(outs):
            for g in range(GROUP):
                part = attn_ref[pl.ds(g * total + (own ^ k) * t, t), :]
                out_ref[pl.ds(g * t, t), spare] = part

    for own in range(rows):
        pl.when(lax.axis_index("rows") == own)(functools.partial(place, own))


def stack_body(*refs):
    *pieces, _, out_ref = refs
    for k, ref in enumerate(pieces):
        out_ref[k] = ref[...]


def products(side, x, weight, k, total):
    depth = x.shape[1]
    core = lax.axis_index("heads")
    core = 1 - core if side else core
    half = weight.shape[1] // 2
    first = pl.multiple_of(core * half + (lax.axis_index("rows") ^ k) * depth, depth)
    part = jnp.dot(x, weight[0, pl.ds(first, depth)], preferred_element_type=jnp.float32)
    return part if total is None else total + part


def own_chunk_body(x_ref, gate_w, up_w, gate_ref, up_ref):
    x = x_ref[:, pl.ds(0, x_ref.shape[1] - HEAD_DIM)]
    gate_ref[...] = products(0, x, gate_w, 0, None)
    up_ref[...] = products(0, x, up_w, 0, None)


def pair_chunk_body(x_ref, gate_in, up_in, gate_w, up_w, gate_ref, up_ref):
    x = x_ref[:, pl.ds(0, x_ref.shape[1] - HEAD_DIM)]
    gate_ref[...] = products(1, x, gate_w, 0, gate_in[...])
    up_ref[...] = products(1, x, up_w, 0, up_in[...])


def first_half_body(x_ref, gate_in, up_in, gate_w, up_w, gate_ref, up_ref):
    chunks, _, width = x_ref.shape
    gate, up = gate_in[...], up_in[...]
    for k in range(chunks):
        x = x_ref[k, :, pl.ds(0, width - HEAD_DIM)]
        gate = products(0, x, gate_w, k + 1, gate)
        up = products(0, x, up_w, k + 1, up)
    gate_ref[...] = gate
    up_ref[...] = up


def second_half_body(
    plan, x_ref, own_ref, mine_ref, pair_ref, gate_in, up_in, gate_w, up_w, hidden_ref
):
    chunks, tokens, width = x_ref.shape
    depth = width - HEAD_DIM
    first = GROUP * plan.tokens
    square = jnp.zeros((tokens - first, HEAD_DIM), jnp.float32)
    rows, spare = pl.ds(first, tokens - first), pl.ds(depth, HEAD_DIM)
    for ref in (own_ref, x_ref):
        for k in range(chunks):
            square = square + ref[k, rows, spare].astype(jnp.float32)
    for ref in (mine_ref, pair_ref):
        square = square + ref[rows, spare].astype(jnp.float32)
    square = to_column(square[0:1] + square[1:2], tokens)
    scale = lax.rsqrt(square / (2 * (chunks + 1) * depth) + 1e-05)
    gate, up = gate_in[...], up_in[...]
    for k in range(chunks):
        x = x_ref[k, :, pl.ds(0, depth)]
        gate = products(1, x, gate_w, k + 1, gate)
        up = products(1, x, up_w, k + 1, up)
    gate = gate * scale
    up = up * scale
    hidden_ref[...] = (gate / (1.0 + jnp.exp(-gate)) * up).astype(jnp.bfloat16)


def down_product(side, hidden_ref, down_w):
    depth = hidden_ref.shape[1]
    core = lax.axis_index("heads")
    first = pl.multiple_of((1 - core if side else core) * depth, depth)
    return jnp.dot(
        hidden_ref[...], down_w[0, pl.ds(first, depth)], preferred_element_type=jnp.float32
    )


def down_first_body(hidden_ref, down_w, out_ref):
    out_ref[...] = down_product(0, hidden_ref, down_w)


def down_second_body(plan, rows, hidden_ref, own_ref, down_w, *outs):
    result = own_ref[...] + down_product(1, hidden_ref, down_w)
    t = plan.tokens
    total = rows * t

    def place(own):
        for k, out_ref in enumerate(outs):
            first = (own ^ k) * t
            pair = [result[i : i + t] for i in (first, first + total)]
            out_ref[...] = jnp.concatenate(pair, axis=0).astype(jnp.bfloat16)

    for own in range(rows):
        pl.when(lax.axis_index("rows") == own)(functools.partial(place, own))


def sum_body(*refs):
    *pieces, own_ref, peer_ref = refs
    total = pieces[0][...].astype(jnp.float32)
    for ref in pieces[1:]:
        total = total + ref[...].astype(jnp.float32)
    t = own_ref.shape[0]
    own_ref[...] = total[:t].astype(jnp.bfloat16)
    peer_ref[...] = total[t:].astype(jnp.bfloat16)


def attn_body(plan, rows, mine_ref, own_ref, _, attn_ref):
    t = plan.tokens
    depth = own_ref.shape[2] - HEAD_DIM
    for k in range(rows):
        head = (lax.axis_index("rows") ^ k) * GROUP
        for g in range(GROUP):
            lanes = pl.ds(pl.multiple_of((head + g) * HEAD_DIM, HEAD_DIM), HEAD_DIM)
            for s in range(plan.steps):
                ref = own_ref.at[k - 1] if k else mine_ref
                attn_ref[s, :, lanes] = ref[
                    pl.ds(g * t + s * plan.conts, plan.conts), pl.ds(depth, HEAD_DIM)
                ]


def mix_body(plan, local_ref, own_ref, peer_ref, moe_ref):
    own = lax.axis_index("experts")
    local = local_ref[...].astype(jnp.float32)
    lane = lax.broadcasted_iota(jnp.int32, local.shape, 1)
    mixture = None
    for i, ref in enumerate((own_ref, peer_ref)):
        parts = jnp.where((lane > 0) & ((lane + 2) // 3 == (own ^ i) + 1), local, 0.0)
        part = jnp.sum(parts, axis=1, keepdims=True) * ref[...].astype(jnp.float32)
        mixture = part if mixture is None else mixture + part
    mixture = mixture.astype(jnp.bfloat16)
    for s in range(plan.steps):
        moe_ref[s] = mixture[s * plan.conts : (s + 1) * plan.conts]


def per_device(
    queries,
    new_kv,
    prefix_kv,
    cont_prompt,
    resid,
    norm_gain,
    w_gate,
    w_up,
    w_down,
    routes,
    route_gates,
):
    rows, experts = lax.axis_size("rows"), lax.axis_size("experts")
    plan = Plan(queries, prefix_kv)
    bf16, f32 = jnp.bfloat16, jnp.float32
    shape = jax.ShapeDtypeStruct
    piece = GROUP * HEAD_DIM
    total = rows * plan.tokens
    tokens = experts * total

    hbm = functools.partial(pltpu.with_memory_space_constraint, memory_space=pltpu.HBM)
    vmem = functools.partial(pltpu.with_memory_space_constraint, memory_space=VMEM)
    gate_w, up_w, down_w = w_gate, w_up, w_down

    def cover(size):
        return pl.CostEstimate(flops=FLOPS * size, bytes_accessed=size, transcendentals=0)

    scalars = (cont_prompt, routes, route_gates)
    arrays = (queries, new_kv, prefix_kv, resid)
    fetched = call(
        functools.partial(fetch_body, plan, experts),
        (VMEM((plan.tokens, HEAD_DIM), bf16),) + tuple(VMEM(a.shape, bf16) for a in arrays),
        "a" * (len(scalars) + len(arrays)),
        scratch=tuple(pltpu.SMEM(a.shape, a.dtype) for a in scalars)
        + (pltpu.SemaphoreType.DMA((len(scalars) + len(arrays),)),),
    )(*map(hbm, scalars + arrays))
    packed = call(
        functools.partial(pack_body, plan),
        (shape((plan.rows, HEAD_DIM), bf16),) * rows,
        "vvvvv",
        cost=cover(PACK_COVER),
    )(*map(vmem, fetched))

    def spread(pieces):
        got = [pieces[0]]
        for k in range(1, rows):
            got.append(lax.ppermute(pieces[k], "rows", [(i, i ^ k) for i in range(rows)]))
        return got

    keys = -(-(rows * (plan.block + 2 * plan.tokens)) // 128) * 128
    lanes = piece + HEAD_DIM
    x, attn = call(
        functools.partial(attend_body, plan, rows),
        (shape((total, lanes), bf16), shape((GROUP * total, HEAD_DIM), bf16)),
        "v" * (rows + 1),
        scratch=(
            VMEM((GROUP * total, HEAD_DIM), bf16),
            VMEM((GROUP * total, HEAD_DIM), bf16),
            VMEM((keys, HEAD_DIM), bf16),
            VMEM((total, HEAD_DIM), bf16),
            VMEM((norm_gain.size // HEAD_DIM, HEAD_DIM), f32),
        ),
        cost=cover(ATTEND_COVER),
    )(*spread(packed), norm_gain.reshape(-1, HEAD_DIM))
    swap = [(0, 1), (1, 0)]
    peer = lax.ppermute(x, "experts", swap)
    merged = call(
        functools.partial(merge_body, plan, rows),
        (shape((tokens, lanes), bf16),) * rows,
        "vvv",
        cost=cover(MERGE_COVER),
    )(x, peer, attn)
    chunks = spread(merged)
    units = w_gate.shape[2]
    products_of = shape((tokens, units), f32)
    pair = lax.ppermute(merged[0], "heads", swap)
    gate, up = call(
        own_chunk_body, (products_of, products_of), "vvv", cost=cover(OWN_COVER)
    )(merged[0], gate_w, up_w)
    gate, up = call(
        pair_chunk_body, (products_of, products_of), "vvvvv", cost=cover(FIRST_COVER)
    )(pair, gate, up, gate_w, up_w)
    own = call(stack_body, shape((rows - 1, tokens, lanes), bf16), "v" * rows)(*chunks[1:], gate)
    other = lax.ppermute(own, "heads", swap)
    gate, up = call(
        first_half_body,
        (products_of, products_of),
        "vvvvv",
        limit=FIRST_LIMIT,
        cost=cover(FIRST_COVER),
    )(own, gate, up, gate_w, up_w)
    hidden = call(
        functools.partial(second_half_body, plan),
        shape((tokens, units), bf16),
        "vvvvvvvv",
        limit=SECOND_LIMIT,
        cost=cover(SECOND_COVER),
    )(other, own, merged[0], pair, gate, up, gate_w, up_w)
    other_hidden = lax.ppermute(hidden, "heads", swap)
    partial = call(
        down_first_body,
        shape((tokens, plan.half), f32),
        "vv",
        limit=DOWN_LIMIT,
        cost=cover(2 * plan.half * units),
    )(hidden, down_w)
    blocks = call(
        functools.partial(down_second_body, plan, rows),
        (shape((experts * plan.tokens, plan.half), bf16),) * rows,
        "vvv",
        cost=cover(2 * plan.half * units),
    )(other_hidden, partial, down_w)
    output = shape((plan.tokens, plan.half), bf16)
    mine, theirs = call(sum_body, (output, output), "v" * rows)(*spread(blocks))
    returned = lax.ppermute(theirs, "experts", swap)
    out = shape(queries.shape, bf16)
    attn_out = call(functools.partial(attn_body, plan, rows), out, "vvv")(merged[0], own, theirs)
    moe_out = call(functools.partial(mix_body, plan), out, "vvv")(vmem(fetched[0]), mine, returned)
    return (attn_out, moe_out)


def solution(mesh):
    placed = (
        P(None, ("groups", "rows", "experts"), "heads"),
        P(None, ("groups", "rows", "experts"), None, "heads"),
        P(("groups", "experts"), "rows", None, "heads"),
        P(("groups", "rows", "experts")),
        P(None, ("groups", "rows", "experts"), "heads"),
        P(),
        P("experts", None, ("rows", "heads")),
        P("experts", None, ("rows", "heads")),
        P("experts", "rows", "heads"),
        P(None, ("groups", "rows", "experts"), None),
        P(None, ("groups", "rows", "experts"), None),
    )
    sizes = mesh.shape
    by_head = (
        sizes["heads"] == 2
        and sizes["experts"] == 2
        and sizes["rows"] == 4
        and sizes["rows"] * sizes["heads"] == KV_HEADS
    )
    return jax.shard_map(
        per_device if by_head else per_device_wide,
        mesh=mesh,
        in_specs=placed,
        out_specs=(
            P(None, ("groups", "rows", "experts"), "heads"),
            P(None, ("groups", "rows", "experts"), "heads"),
        ),
        check_vma=False,
    )
```

```python
import functools

import jax
import jax.numpy as jnp
from jax import lax
from jax.experimental import pallas as pl
from jax.experimental.pallas import tpu as pltpu
from jax.sharding import PartitionSpec as P


HEADS = 48
KV_HEADS = 8
HEAD_DIM = 128
GROUP = HEADS // KV_HEADS

VMEM = pltpu.VMEM
MIB = 1 << 20
PACK_COVER = 40 * MIB
FLOPS = 1000
OWN_COVER = 40 * MIB
FIRST_COVER = 1 * MIB
SECOND_COVER = 1 * MIB
FIRST_LIMIT = 4 * MIB
SECOND_LIMIT = 4 * MIB
DOWN_LIMIT = 4 * MIB
ATTEND_COVER = MIB
MERGE_COVER = MIB


def fresh_terms(queries, new_kv):
    step_count, own_rows = (queries.shape[0], queries.shape[1])
    kv_local = new_kv.shape[-1] // HEAD_DIM
    group_size = HEADS // KV_HEADS
    grouped = queries.reshape(step_count, own_rows, kv_local, group_size, HEAD_DIM)
    fresh_keys = new_kv[:, :, 0].reshape(step_count, own_rows, kv_local, HEAD_DIM)
    fresh_values = new_kv[:, :, 1].reshape(step_count, own_rows, kv_local, HEAD_DIM)
    fresh_scores = jnp.einsum(
        "scgnd,tcgd->scgnt", grouped, fresh_keys, preferred_element_type=jnp.float32
    ) * HEAD_DIM ** (-0.5)
    future = jnp.arange(step_count)[None, :] > jnp.arange(step_count)[:, None]
    fresh_scores = jnp.where(future[:, None, None, None, :], -jnp.inf, fresh_scores)
    return (grouped, fresh_scores, fresh_values)


def attend_gathered(queries, new_kv, prefix_kv, local_prompt):
    grouped, fresh_scores, fresh_values = fresh_terms(queries, new_kv)
    own_rows = queries.shape[1]
    kv_local = new_kv.shape[-1] // HEAD_DIM
    cache = lax.all_gather(prefix_kv, "rows", axis=1, tiled=True)
    length = cache.shape[1]
    picked = jnp.take(cache, local_prompt, axis=0)
    cache_keys = picked[:, :, 0].reshape(own_rows, length, kv_local, HEAD_DIM)
    cache_values = picked[:, :, 1].reshape(own_rows, length, kv_local, HEAD_DIM)
    prefix_scores = jnp.einsum(
        "scgnd,ckgd->scgnk", grouped, cache_keys, preferred_element_type=jnp.float32
    ) * HEAD_DIM ** (-0.5)
    highest = jnp.maximum(jnp.max(prefix_scores, axis=-1), jnp.max(fresh_scores, axis=-1))
    prefix_expo = jnp.exp(prefix_scores - highest[..., None])
    fresh_expo = jnp.exp(fresh_scores - highest[..., None])
    totals = jnp.sum(prefix_expo, axis=-1) + jnp.sum(fresh_expo, axis=-1)
    weighted = jnp.einsum(
        "scgnk,ckgd->scgnd",
        prefix_expo.astype(jnp.bfloat16),
        cache_values,
        preferred_element_type=jnp.float32,
    )
    weighted = weighted + jnp.einsum(
        "scgnt,tcgd->scgnd",
        fresh_expo.astype(jnp.bfloat16),
        fresh_values,
        preferred_element_type=jnp.float32,
    )
    return (weighted, totals)


def per_device_wide(
    queries,
    new_kv,
    prefix_kv,
    cont_prompt,
    resid,
    norm_gain,
    w_gate,
    w_up,
    w_down,
    routes,
    route_gates,
):
    step_count, own_rows, half_width = queries.shape
    prompt_count = prefix_kv.shape[0]
    local_prompt = cont_prompt - lax.axis_index("experts") * prompt_count
    weighted, totals = attend_gathered(queries, new_kv, prefix_kv, local_prompt)
    attn_out = (
        (weighted / totals[..., None])
        .astype(jnp.bfloat16)
        .reshape(step_count, own_rows, half_width)
    )
    halves = (
        lax.all_gather(resid, "heads", axis=2, tiled=True),
        lax.all_gather(attn_out, "heads", axis=2, tiled=True),
    )
    combined = halves[0].astype(jnp.float32) + halves[1].astype(jnp.float32)
    square_mean = jnp.mean(combined * combined, axis=-1, keepdims=True)
    normed = (combined * lax.rsqrt(square_mean + 1e-05) * norm_gain.astype(jnp.float32)).astype(
        jnp.bfloat16
    )
    token_count = step_count * own_rows
    flat_tokens = normed.reshape(token_count, -1)
    flat_routes = routes.reshape(token_count, -1)
    experts = lax.axis_size("experts")
    matches = flat_routes[:, :, None] == jnp.arange(experts)[None, None, :]
    gate_weights = w_gate[0]
    up_weights = w_up[0]
    wanted = jnp.transpose(jnp.any(matches, axis=1))
    outgoing = jnp.where(wanted[:, :, None], flat_tokens[None], jnp.zeros((), jnp.bfloat16))
    arrived = lax.all_to_all(outgoing, "experts", split_axis=0, concat_axis=0, tiled=True)
    segment = lax.all_gather(arrived.reshape(experts * token_count, -1), "rows", axis=0, tiled=True)
    gate = jnp.dot(segment, gate_weights, preferred_element_type=jnp.float32)
    up_part = jnp.dot(segment, up_weights, preferred_element_type=jnp.float32)
    hidden = (jax.nn.silu(gate) * up_part).astype(jnp.bfloat16)
    paired = lax.all_gather(hidden, "heads", axis=1, tiled=True)
    down_rows = w_down[0]
    segment = paired
    summed = lax.psum_scatter(
        jnp.dot(segment, down_rows, preferred_element_type=jnp.float32).astype(jnp.bfloat16),
        "rows",
        scatter_dimension=0,
        tiled=True,
    )
    result = summed.reshape(experts, token_count, -1)
    returned = lax.all_to_all(result, "experts", split_axis=0, concat_axis=0, tiled=True)
    mixing = jnp.sum(
        jnp.where(matches, route_gates.reshape(token_count, -1)[:, :, None], 0.0), axis=1
    )
    mixture = jnp.einsum("ne,end->nd", mixing, returned.astype(jnp.float32))
    moe_out = mixture.astype(jnp.bfloat16).reshape(step_count, own_rows, half_width)
    return (attn_out, moe_out)


def call(body, outs, in_spaces, scratch=(), limit=4 * MIB, cost=None):
    spaces = {"v": VMEM, "s": pltpu.SMEM, "a": pl.ANY}
    single = not isinstance(outs, (list, tuple))
    shapes = [outs] if single else list(outs)
    specs = [pl.BlockSpec(memory_space=VMEM) for _ in shapes]
    return pl.pallas_call(
        body,
        out_shape=shapes[0] if single else tuple(shapes),
        in_specs=[pl.BlockSpec(memory_space=spaces[s]) for s in in_spaces],
        out_specs=specs[0] if single else tuple(specs),
        scratch_shapes=list(scratch),
        compiler_params=pltpu.CompilerParams(vmem_limit_bytes=limit),
        cost_estimate=cost,
    )


class Plan:
    def __init__(self, queries, prefix_kv):
        self.steps, self.conts, self.half = queries.shape
        self.prompts, self.positions = prefix_kv.shape[:2]
        self.tokens = self.steps * self.conts
        self.block = self.prompts * self.positions * 2
        self.fresh = self.block
        self.query = self.fresh + 2 * self.tokens
        self.resid = self.query + GROUP * self.tokens
        self.prompt = self.resid + GROUP * self.tokens
        self.rows = -(-(self.prompt + self.tokens) // 16) * 16


def fetch_body(plan, experts, *refs):
    f32, bf16 = jnp.float32, jnp.bfloat16
    sources, targets, scalars, sems = refs[:7], refs[7:12], refs[12:15], refs[15]
    copies = [
        pltpu.make_async_copy(source, target, sems.at[i])
        for i, (source, target) in enumerate(zip(sources, scalars + targets[1:]))
    ]
    for copy in copies:
        copy.start()
    for copy in copies:
        copy.wait()
    prompts, routes, gates = scalars
    base = lax.axis_index("experts") * plan.prompts
    shape = (plan.tokens, HEAD_DIM)
    row = lax.broadcasted_iota(jnp.int32, shape, 0)
    lane = lax.broadcasted_iota(jnp.int32, shape, 1)
    value = jnp.zeros(shape, f32)
    for s in range(plan.steps):
        for c in range(plan.conts):
            here = row == s * plan.conts + c
            value = jnp.where(here & (lane == 0), (prompts[c] - base).astype(f32), value)
            for e in range(experts):
                amount = f32(0.0)
                for k in range(routes.shape[2]):
                    amount = amount + jnp.where(routes[s, c, k] == e, gates[s, c, k], 0.0)
                value = jnp.where(here & ((lane + 2) // 3 == e + 1), amount, value)
    high = value.astype(bf16).astype(f32)
    middle = (value - high).astype(bf16).astype(f32)
    low = value - high - middle
    which = (lane + 2) % 3
    parts = jnp.where(lane == 0, high, jnp.where(which == 0, high, jnp.where(which == 1, middle, low)))
    targets[0][...] = parts.astype(bf16)


def pack_body(plan, local_ref, q_ref, new_ref, prefix_ref, resid_ref, *outs):
    t, c = plan.tokens, plan.conts
    own = lax.axis_index("rows")
    for k, out_ref in enumerate(outs):
        h = own ^ k
        lanes = pl.ds(pl.multiple_of(h * HEAD_DIM, HEAD_DIM), HEAD_DIM)
        for p in range(plan.prompts):
            for i in range(plan.positions):
                out_ref[pl.ds((p * plan.positions + i) * 2, 2), :] = prefix_ref[p, i, :, lanes]
        for s in range(plan.steps):
            for i in range(c):
                out_ref[pl.ds(plan.fresh + (s * c + i) * 2, 2), :] = new_ref[s, i, :, lanes]
            for g in range(GROUP):
                head = pl.ds(pl.multiple_of((h * GROUP + g) * HEAD_DIM, HEAD_DIM), HEAD_DIM)
                out_ref[pl.ds(plan.query + g * t + s * c, c), :] = q_ref[s, :, head]
                out_ref[pl.ds(plan.resid + g * t + s * c, c), :] = resid_ref[s, :, head]
        out_ref[pl.ds(plan.prompt, t), :] = local_ref[...]


def attend_body(plan, rows, *refs):
    pieces, (gain_ref, x_ref, attn_ref, q_s, r_s, kv_s, p_s, gain_s) = refs[:rows], refs[rows:]
    t, c = plan.tokens, plan.conts
    total = rows * t
    f32 = jnp.float32

    def place(own):
        for k, got_ref in enumerate(pieces):
            src = own ^ k
            kv_s[pl.ds(src * plan.block, plan.block), :] = got_ref[pl.ds(0, plan.block), :]
            late = pl.ds(rows * plan.block + src * 2 * t, 2 * t)
            kv_s[late, :] = got_ref[pl.ds(plan.fresh, 2 * t), :]
            p_s[pl.ds(src * t, t), :] = got_ref[pl.ds(plan.prompt, t), :]
            for g in range(GROUP):
                q_s[pl.ds(g * total + src * t, t), :] = got_ref[pl.ds(plan.query + g * t, t), :]
                r_s[pl.ds(g * total + src * t, t), :] = got_ref[pl.ds(plan.resid + g * t, t), :]

    for own in range(rows):
        pl.when(lax.axis_index("rows") == own)(functools.partial(place, own))
    used = rows * plan.block + rows * 2 * t
    spare = kv_s.shape[0] - used
    if spare:
        kv_s[pl.ds(used, spare), :] = jnp.zeros((spare, HEAD_DIM), jnp.bfloat16)
    kv = kv_s[...]
    scores = lax.dot_general(
        q_s[...], kv, (((1,), (1,)), ((), ())), preferred_element_type=f32
    ) * HEAD_DIM ** (-0.5)
    shape = scores.shape
    row = lax.broadcasted_iota(jnp.int32, shape, 0) % total
    col = lax.broadcasted_iota(jnp.int32, shape, 1)
    prompt = p_s[...].astype(f32)[:, :1]
    prompt = jnp.concatenate([prompt] * GROUP, axis=0).astype(jnp.int32)
    in_prefix = (col < rows * plan.block) & ((col % plan.block) // (2 * plan.positions) == prompt)
    late = col - rows * plan.block
    same = (late // (2 * t) == row // t) & (((late // 2) % t) % c == row % c)
    seen = ((late // 2) % t) // c <= (row % t) // c
    in_fresh = (late >= 0) & (col < used) & same & seen
    live = (col % 2 == 0) & (in_prefix | in_fresh)
    scores = jnp.where(live, scores, -jnp.inf)
    highest = jnp.max(scores, axis=-1, keepdims=True)
    expo = jnp.exp(scores - highest)
    totals = jnp.sum(expo, axis=-1, keepdims=True)
    weights = pltpu.roll(expo, 1, 1).astype(jnp.bfloat16)
    out = jnp.dot(weights, kv, preferred_element_type=f32) / totals
    attn = out.astype(jnp.bfloat16)
    attn_ref[...] = attn
    gain_s[...] = gain_ref[...].astype(f32)
    first = (lax.axis_index("heads") * rows + lax.axis_index("rows")) * GROUP
    combined = attn.astype(f32) + r_s[...].astype(f32)
    square = jnp.zeros((total, HEAD_DIM), f32)
    for g in range(GROUP):
        part = combined[g * total : (g + 1) * total]
        square = square + part * part
        gained = part * gain_s[pl.ds(first + g, 1), :]
        x_ref[:, pl.ds(g * HEAD_DIM, HEAD_DIM)] = gained.astype(jnp.bfloat16)
    square = jnp.sum(square, axis=-1, keepdims=True)
    high = square.astype(jnp.bfloat16)
    low = (square - high.astype(f32)).astype(jnp.bfloat16)
    lane = lax.broadcasted_iota(jnp.int32, (total, HEAD_DIM), 1)
    extra = jnp.where(lane == 0, high.astype(f32), jnp.where(lane == 1, low.astype(f32), 0.0))
    x_ref[:, pl.ds(GROUP * HEAD_DIM, HEAD_DIM)] = extra.astype(jnp.bfloat16)


def to_row(column, first, lanes):
    shape = (column.shape[0], lanes)
    hit = lax.broadcasted_iota(jnp.int32, shape, 1) == lax.broadcasted_iota(jnp.int32, shape, 0) + first
    return jnp.sum(jnp.where(hit, column, 0.0), axis=0, keepdims=True)


def to_column(row, count):
    shape = (count, row.shape[1])
    hit = lax.broadcasted_iota(jnp.int32, shape, 1) == lax.broadcasted_iota(jnp.int32, shape, 0)
    return jnp.sum(jnp.where(hit, row, 0.0), axis=1, keepdims=True)


def merge_body(plan, rows, own_ref, peer_ref, attn_ref, *outs):
    t = plan.tokens
    total, width = own_ref.shape
    depth = width - HEAD_DIM
    spare = pl.ds(depth, HEAD_DIM)
    high, low = [], []
    for i, ref in enumerate((own_ref, peer_ref)):
        extra = ref[:, spare].astype(jnp.float32)
        high.append(to_row(extra[:, 0:1], i * total, HEAD_DIM))
        low.append(to_row(extra[:, 1:2], i * total, HEAD_DIM))
    row = lax.broadcasted_iota(jnp.int32, (2 * total - GROUP * t, HEAD_DIM), 0)
    squares = jnp.where(row == 0, high[0] + high[1], jnp.where(row == 1, low[0] + low[1], 0.0))
    squares = squares.astype(jnp.bfloat16)
    for out_ref in outs:
        for i, ref in enumerate((own_ref, peer_ref)):
            out_ref[pl.ds(i * total, total), pl.ds(0, depth)] = ref[:, pl.ds(0, depth)]
        out_ref[pl.ds(GROUP * t, row.shape[0]), spare] = squares

    def place(own):
        for k, out_ref in enumerate(outs):
            for g in range(GROUP):
                part = attn_ref[pl.ds(g * total + (own ^ k) * t, t), :]
                out_ref[pl.ds(g * t, t), spare] = part

    for own in range(rows):
        pl.when(lax.axis_index("rows") == own)(functools.partial(place, own))


def stack_body(*refs):
    *pieces, _, out_ref = refs
    for k, ref in enumerate(pieces):
        out_ref[k] = ref[...]


def products(side, x, weight, k, total):
    depth = x.shape[1]
    core = lax.axis_index("heads")
    core = 1 - core if side else core
    half = weight.shape[1] // 2
    first = pl.multiple_of(core * half + (lax.axis_index("rows") ^ k) * depth, depth)
    part = jnp.dot(x, weight[0, pl.ds(first, depth)], preferred_element_type=jnp.float32)
    return part if total is None else total + part


def pull(source, first, target, sems):
    parts = sems.shape[0]
    step = target.shape[0] // parts

    def copy(i):
        rows = pl.ds(pl.multiple_of(first + i * step, step), step)
        into = pl.ds(pl.multiple_of(i * step, step), step)
        return pltpu.make_async_copy(source.at[0, rows], target.at[into], sems.at[i])

    def start():
        pl.loop(0, parts)(lambda i: copy(i).start())

    def finish():
        pl.loop(0, parts)(lambda i: copy(i).wait())

    return start, finish


def own_chunk_body(x_ref, gate_w, up_w, down_hbm, gate_ref, up_ref, down_ref, sems):
    half = down_ref.shape[0]
    start, finish = pull(down_hbm, lax.axis_index("heads") * half, down_ref, sems)
    start()
    x = x_ref[:, pl.ds(0, x_ref.shape[1] - HEAD_DIM)]
    gate_ref[...] = products(0, x, gate_w, 0, None)
    up_ref[...] = products(0, x, up_w, 0, None)
    finish()


def pair_chunk_body(x_ref, gate_in, up_in, gate_w, up_w, gate_ref, up_ref):
    x = x_ref[:, pl.ds(0, x_ref.shape[1] - HEAD_DIM)]
    gate_ref[...] = products(1, x, gate_w, 0, gate_in[...])
    up_ref[...] = products(1, x, up_w, 0, up_in[...])


def first_half_body(
    x_ref, gate_in, up_in, gate_w, up_w, down_hbm, gate_ref, up_ref, down_ref, sems
):
    quarter = down_ref.shape[0]
    other = (1 - lax.axis_index("heads")) * (2 * quarter)
    start, finish = pull(down_hbm, other, down_ref, sems)
    start()
    chunks, _, width = x_ref.shape
    gate, up = gate_in[...], up_in[...]
    for k in range(chunks):
        x = x_ref[k, :, pl.ds(0, width - HEAD_DIM)]
        gate = products(0, x, gate_w, k + 1, gate)
        up = products(0, x, up_w, k + 1, up)
    gate_ref[...] = gate
    up_ref[...] = up
    finish()


def second_half_body(
    plan,
    x_ref,
    own_ref,
    mine_ref,
    pair_ref,
    gate_in,
    up_in,
    gate_w,
    up_w,
    down_hbm,
    hidden_ref,
    down_ref,
    sems,
):
    quarter = down_ref.shape[0]
    other = (1 - lax.axis_index("heads")) * (2 * quarter) + quarter
    start, finish = pull(down_hbm, other, down_ref, sems)
    start()
    chunks, tokens, width = x_ref.shape
    depth = width - HEAD_DIM
    first = GROUP * plan.tokens
    square = jnp.zeros((tokens - first, HEAD_DIM), jnp.float32)
    rows, spare = pl.ds(first, tokens - first), pl.ds(depth, HEAD_DIM)
    for ref in (own_ref, x_ref):
        for k in range(chunks):
            square = square + ref[k, rows, spare].astype(jnp.float32)
    for ref in (mine_ref, pair_ref):
        square = square + ref[rows, spare].astype(jnp.float32)
    square = to_column(square[0:1] + square[1:2], tokens)
    scale = lax.rsqrt(square / (2 * (chunks + 1) * depth) + 1e-05)
    gate, up = gate_in[...], up_in[...]
    for k in range(chunks):
        x = x_ref[k, :, pl.ds(0, depth)]
        gate = products(1, x, gate_w, k + 1, gate)
        up = products(1, x, up_w, k + 1, up)
    gate = gate * scale
    up = up * scale
    hidden_ref[...] = (gate / (1.0 + jnp.exp(-gate)) * up).astype(jnp.bfloat16)
    finish()


def down_first_body(hidden_ref, down_w, out_ref):
    out_ref[...] = jnp.dot(hidden_ref[...], down_w[...], preferred_element_type=jnp.float32)


def down_second_body(plan, rows, hidden_ref, own_ref, *refs):
    weights, outs = refs[:-rows], refs[-rows:]
    result = own_ref[...]
    for i, weight in enumerate(weights):
        depth = weight.shape[0]
        result = result + jnp.dot(
            hidden_ref[:, pl.ds(i * depth, depth)], weight[...], preferred_element_type=jnp.float32
        )
    t = plan.tokens
    total = rows * t

    def place(own):
        for k, out_ref in enumerate(outs):
            first = (own ^ k) * t
            pair = [result[i : i + t] for i in (first, first + total)]
            out_ref[...] = jnp.concatenate(pair, axis=0).astype(jnp.bfloat16)

    for own in range(rows):
        pl.when(lax.axis_index("rows") == own)(functools.partial(place, own))


def sum_body(*refs):
    *pieces, own_ref, peer_ref = refs
    total = pieces[0][...].astype(jnp.float32)
    for ref in pieces[1:]:
        total = total + ref[...].astype(jnp.float32)
    t = own_ref.shape[0]
    own_ref[...] = total[:t].astype(jnp.bfloat16)
    peer_ref[...] = total[t:].astype(jnp.bfloat16)


def attn_body(plan, rows, mine_ref, own_ref, _, attn_ref):
    t = plan.tokens
    depth = own_ref.shape[2] - HEAD_DIM
    for k in range(rows):
        head = (lax.axis_index("rows") ^ k) * GROUP
        for g in range(GROUP):
            lanes = pl.ds(pl.multiple_of((head + g) * HEAD_DIM, HEAD_DIM), HEAD_DIM)
            for s in range(plan.steps):
                ref = own_ref.at[k - 1] if k else mine_ref
                attn_ref[s, :, lanes] = ref[
                    pl.ds(g * t + s * plan.conts, plan.conts), pl.ds(depth, HEAD_DIM)
                ]


def mix_body(plan, local_ref, own_ref, peer_ref, moe_ref):
    own = lax.axis_index("experts")
    local = local_ref[...].astype(jnp.float32)
    lane = lax.broadcasted_iota(jnp.int32, local.shape, 1)
    mixture = None
    for i, ref in enumerate((own_ref, peer_ref)):
        parts = jnp.where((lane > 0) & ((lane + 2) // 3 == (own ^ i) + 1), local, 0.0)
        part = jnp.sum(parts, axis=1, keepdims=True) * ref[...].astype(jnp.float32)
        mixture = part if mixture is None else mixture + part
    mixture = mixture.astype(jnp.bfloat16)
    for s in range(plan.steps):
        moe_ref[s] = mixture[s * plan.conts : (s + 1) * plan.conts]


def per_device(
    queries,
    new_kv,
    prefix_kv,
    cont_prompt,
    resid,
    norm_gain,
    w_gate,
    w_up,
    w_down,
    routes,
    route_gates,
):
    rows, experts = lax.axis_size("rows"), lax.axis_size("experts")
    plan = Plan(queries, prefix_kv)
    bf16, f32 = jnp.bfloat16, jnp.float32
    shape = jax.ShapeDtypeStruct
    piece = GROUP * HEAD_DIM
    total = rows * plan.tokens
    tokens = experts * total

    hbm = functools.partial(pltpu.with_memory_space_constraint, memory_space=pltpu.HBM)
    vmem = functools.partial(pltpu.with_memory_space_constraint, memory_space=VMEM)
    gate_w, up_w, down_w = w_gate, w_up, hbm(w_down)

    def cover(size):
        return pl.CostEstimate(flops=FLOPS * size, bytes_accessed=size, transcendentals=0)

    scalars = (cont_prompt, routes, route_gates)
    arrays = (queries, new_kv, prefix_kv, resid)
    fetched = call(
        functools.partial(fetch_body, plan, experts),
        (VMEM((plan.tokens, HEAD_DIM), bf16),) + tuple(VMEM(a.shape, bf16) for a in arrays),
        "a" * (len(scalars) + len(arrays)),
        scratch=tuple(pltpu.SMEM(a.shape, a.dtype) for a in scalars)
        + (pltpu.SemaphoreType.DMA((len(scalars) + len(arrays),)),),
    )(*map(hbm, scalars + arrays))
    packed = call(
        functools.partial(pack_body, plan),
        (shape((plan.rows, HEAD_DIM), bf16),) * rows,
        "vvvvv",
        cost=cover(PACK_COVER),
    )(*map(vmem, fetched))

    def spread(pieces):
        got = [pieces[0]]
        for k in range(1, rows):
            got.append(lax.ppermute(pieces[k], "rows", [(i, i ^ k) for i in range(rows)]))
        return got

    keys = -(-(rows * (plan.block + 2 * plan.tokens)) // 128) * 128
    lanes = piece + HEAD_DIM
    x, attn = call(
        functools.partial(attend_body, plan, rows),
        (shape((total, lanes), bf16), shape((GROUP * total, HEAD_DIM), bf16)),
        "v" * (rows + 1),
        scratch=(
            VMEM((GROUP * total, HEAD_DIM), bf16),
            VMEM((GROUP * total, HEAD_DIM), bf16),
            VMEM((keys, HEAD_DIM), bf16),
            VMEM((total, HEAD_DIM), bf16),
            VMEM((norm_gain.size // HEAD_DIM, HEAD_DIM), f32),
        ),
        cost=cover(ATTEND_COVER),
    )(*spread(packed), norm_gain.reshape(-1, HEAD_DIM))
    swap = [(0, 1), (1, 0)]
    peer = lax.ppermute(x, "experts", swap)
    merged = call(
        functools.partial(merge_body, plan, rows),
        (shape((tokens, lanes), bf16),) * rows,
        "vvv",
        cost=cover(MERGE_COVER),
    )(x, peer, attn)
    chunks = spread(merged)
    units = w_gate.shape[2]
    products_of = shape((tokens, units), f32)
    pair = lax.ppermute(merged[0], "heads", swap)
    half, wide = w_down.shape[1] // 2, w_down.shape[2]
    sems = (pltpu.SemaphoreType.DMA((4,)),)
    gate, up, down_own = call(
        own_chunk_body,
        (products_of, products_of, VMEM((half, wide), bf16)),
        "vvva",
        sems,
        cost=cover(OWN_COVER),
    )(merged[0], gate_w, up_w, down_w)
    gate, up = call(
        pair_chunk_body, (products_of, products_of), "vvvvv", cost=cover(FIRST_COVER)
    )(pair, gate, up, gate_w, up_w)
    own = call(stack_body, shape((rows - 1, tokens, lanes), bf16), "v" * rows)(*chunks[1:], gate)
    other = lax.ppermute(own, "heads", swap)
    gate, up, down_near = call(
        first_half_body,
        (products_of, products_of, VMEM((half // 2, wide), bf16)),
        "vvvvva",
        sems,
        limit=FIRST_LIMIT,
        cost=cover(FIRST_COVER),
    )(own, gate, up, gate_w, up_w, down_w)
    hidden, down_far = call(
        functools.partial(second_half_body, plan),
        (shape((tokens, units), bf16), VMEM((half // 2, wide), bf16)),
        "vvvvvvvva",
        sems,
        limit=SECOND_LIMIT,
        cost=cover(SECOND_COVER),
    )(other, own, merged[0], pair, gate, up, gate_w, up_w, down_w)
    other_hidden = lax.ppermute(hidden, "heads", swap)
    partial = call(
        down_first_body,
        shape((tokens, plan.half), f32),
        "vv",
        limit=DOWN_LIMIT,
        cost=cover(2 * plan.half * units),
    )(hidden, vmem(down_own))
    blocks = call(
        functools.partial(down_second_body, plan, rows),
        (shape((experts * plan.tokens, plan.half), bf16),) * rows,
        "vvvv",
        cost=cover(2 * plan.half * units),
    )(other_hidden, partial, vmem(down_near), vmem(down_far))
    output = shape((plan.tokens, plan.half), bf16)
    mine, theirs = call(sum_body, (output, output), "v" * rows)(*spread(blocks))
    returned = lax.ppermute(theirs, "experts", swap)
    out = shape(queries.shape, bf16)
    attn_out = call(functools.partial(attn_body, plan, rows), out, "vvv")(merged[0], own, theirs)
    moe_out = call(functools.partial(mix_body, plan), out, "vvv")(vmem(fetched[0]), mine, returned)
    return (attn_out, moe_out)


def solution(mesh):
    placed = (
        P(None, ("groups", "rows", "experts"), "heads"),
        P(None, ("groups", "rows", "experts"), None, "heads"),
        P(("groups", "experts"), "rows", None, "heads"),
        P(("groups", "rows", "experts")),
        P(None, ("groups", "rows", "experts"), "heads"),
        P(),
        P("experts", None, ("rows", "heads")),
        P("experts", None, ("rows", "heads")),
        P("experts", "rows", "heads"),
        P(None, ("groups", "rows", "experts"), None),
        P(None, ("groups", "rows", "experts"), None),
    )
    sizes = mesh.shape
    by_head = (
        sizes["heads"] == 2
        and sizes["experts"] == 2
        and sizes["rows"] == 4
        and sizes["rows"] * sizes["heads"] == KV_HEADS
    )
    return jax.shard_map(
        per_device if by_head else per_device_wide,
        mesh=mesh,
        in_specs=placed,
        out_specs=(
            P(None, ("groups", "rows", "experts"), "heads"),
            P(None, ("groups", "rows", "experts"), "heads"),
        ),
        check_vma=False,
    )
```
